32 devices in a mesh: px: 2 (over y), py: 4 (over z), case: 4 (over x, core).
Axes of the slice: x: 2, y: 2, z: 4, core: 2. Of those that a mesh axis runs over, the one named last changes fastest.
Arguments:
- comp_type: int32 [1024], P(('px', 'py')), may hold values from 0 to 7
- stiffness: float32 [1024], P(('px', 'py')), may hold values from 0.3 to 3
- near_port: int32 [1024], P(('px', 'py')), may hold values from 0 to 127
- far_owner: int32 [1024, 1], P(('px', 'py')), may hold values from 0 to 7; in each aligned block of 128 rows (0 to 127, 128 to 255, ...) at most 24 rows name the same one
- far_port: int32 [1024], P(('px', 'py')), may hold values from 0 to 127
- bubble_load: float32 [64, 32, 1024], P(None, 'case', ('px', 'py')), may hold values from -6 to 6
- port_load: float32 [48, 32, 1024], P(None, 'case', ('px', 'py')), may hold values from -3 to 3
- bubble_inverse: float32 [8, 64, 64], replicated, may hold values from -1.5 to 2, as said below
- coupling: float32 [8, 96, 64], replicated, may hold values from -0.1 to 0.1
- port_block: float32 [8, 96, 96], replicated, may hold values from -3 to 8, as said below
Outputs:
- port_solution: float32 [48, 32, 1024], P(None, 'case', ('px', 'py'))
- port_residual: float32 [48, 32, 1024], P(None, 'case', ('px', 'py'))
- bubble_solution: float32 [64, 32, 1024], P(None, 'case', ('px', 'py'))
The draws below stay inside these ranges and needn't reach their ends.
Inputs may be any that keep to these rules, and one draw needn't show every extreme that they name: `far_owner`: among the 128 components of one partition, at most 24 name the same owner, a bound that some block reaches. `bubble_inverse`: each matrix is symmetric positive definite. `port_block`: each matrix is symmetric positive definite.
All inputs are finite; a program needn't handle non-finite values.
Results may differ from the reference program's by a relative error of at most 0.00016.
Values sent between devices are 32-bit elements; how exact they have to be, the bound alone decides.
A program may use at most 64 MiB of HBM per device.

```python
import math
import jax
import jax.numpy as jnp
import numpy as np
from jax import lax

MODES = 64
PD = 48
TYPES = 8
ITERS = 2
COMP_DEV = 128
NPART = 8
PORT_DEV = 128
CAP = 24
COMPONENTS = 1024
PORTS = 1024
CASES = 32
N_PX = 2
N_PY = 4


def draw_bubble_inverse(key, part):
    base = jax.random.uniform(key, (TYPES, MODES, MODES), jnp.float32, -1.7, 1.7)
    square = jnp.einsum('tij,tkj->tik', base, base) / MODES
    return 0.5 * jnp.eye(MODES, dtype=jnp.float32)[None, :, :] + 0.5 * square


def draw_port_block(key, part):
    size_ports = 2 * PD
    base = jax.random.uniform(key, (TYPES, size_ports, size_ports), jnp.float32, -1.7, 1.7)
    square = jnp.einsum('tij,tkj->tik', base, base) / size_ports
    return 5.0 * jnp.eye(size_ports, dtype=jnp.float32)[None, :, :] + square


def place_ends(array, stream_key, low, largest):
    spot = [jax.random.randint(jax.random.fold_in(stream_key, axis), (), 0, length) for axis, length in enumerate(array.shape)]
    widest = array.shape.index(max(array.shape))
    neighbour = spot[:widest] + [(spot[widest] + 1) % array.shape[widest]] + spot[widest + 1:]
    return array.at[tuple(spot)].set(low).at[tuple(neighbour)].set(largest)


def shard_levels(rng, extent, pieces, least, largest):
    loudness, own = 1.0, jax.random.fold_in(rng, 6)
    for position, parts in pieces:
        draws = jnp.exp(jax.random.uniform(jax.random.fold_in(own, position), (parts,), jnp.float32, least / len(pieces), largest / len(pieces)))
        loudness = loudness * jnp.repeat(draws, extent[position] // parts).reshape([-1 if axis == position else 1 for axis in range(len(extent))])
    return loudness


def assign_block(rng, own, number, rows, count, top, most, lean):
    sequence = jax.random.permutation(rng, count)
    crowded, common = shares(count, rows * top, most, lean, True), shares(count, rows * top, most, lean, False)
    places = jnp.arange(count)

    def named(sizes, rotation):
        used = int((sizes > 0).sum())
        fixed = max(1, used // 4)
        moved = fixed + (places - fixed + rotation * (used - fixed)) % max(1, count - fixed)
        return jnp.zeros((count,), jnp.int32).at[sequence[jnp.where(places < fixed, places, moved)]].set(jnp.asarray(sizes, jnp.int32))

    sizes = jnp.where(number % 4 == 0, named(crowded, number // 4), named(common, number - number // 4 - 1))
    mixed = jax.random.permutation(jax.random.fold_in(own, 3), count)
    source_of, taker = mixed[0:count // 2 * 2:2], mixed[1:count // 2 * 2:2]
    slack = jnp.minimum(sizes[source_of] - 1, most - sizes[taker]) // 2
    slack = jnp.where((source_of == sequence[0]) | (taker == sequence[0]) | (sizes[taker] == 0), 0, jnp.maximum(slack, 0))
    moved = jax.random.randint(jax.random.fold_in(own, 4), (count // 2,), 0, 1 << 20) % (slack + 1)
    sizes = sizes.at[source_of].add(-moved).at[taker].add(moved)
    labels = jnp.searchsorted(jnp.cumsum(sizes), jnp.arange(rows * top), side="right").astype(jnp.int32)
    table = labels.reshape(top, rows).T
    table = table[jax.random.permutation(jax.random.fold_in(own, 1), rows)]
    rotation = jax.random.randint(jax.random.fold_in(own, 2), (rows, 1), 0, top)
    return jnp.take_along_axis(table, (jnp.arange(top)[None, :] + rotation) % top, axis=1)


def shares(number_of, total, reach, skew, full):
    weights = [(1 << 20) // math.isqrt(standing ** skew) + 1 for standing in range(1, number_of + 1)]
    largest = reach if full else min(reach, max(-(-total // number_of), total * weights[0] // sum(weights)))
    least = 1 if total - largest >= number_of - 1 else 0
    counts, surplus = [largest] + [least] * (number_of - 1), total - largest - least * (number_of - 1)
    while surplus > 0:
        free = [i for i in range(1, number_of) if counts[i] < largest] or [i for i in range(1, number_of) if counts[i] < reach]
        pool, remaining = sum([weights[i] for i in free]), surplus
        for i in free:
            extra = min(reach - counts[i], max(1, remaining * weights[i] // pool), surplus)
            counts[i] = counts[i] + extra
            surplus = surplus - extra
    return np.array(counts)


def normal_values(key, dims, spread, most, pieces=(), kind=jnp.bfloat16):
    values = spread * jax.random.normal(key, dims, jnp.float32)
    if pieces:
        values = values * shard_levels(key, dims, pieces, -0.22, 0.18)
    return jnp.clip(values, -most, most).astype(kind)


def setup_inputs(seed: int = 0) -> dict:
    key_of = jax.random.split(jax.random.key(seed), 11)
    comp_type = place_ends(jax.random.randint(key_of[0], (COMPONENTS,), 0, TYPES), jax.random.fold_in(key_of[0], 1), 0, TYPES - 1).astype(jnp.int32)
    stiffness = jnp.clip(jnp.exp(math.log(3.0) - 2.3025851 * jax.random.uniform(key_of[1], (COMPONENTS,), jnp.float32) ** shard_levels(key_of[1], (COMPONENTS,), ((0, 8),), -0.2, 0.2)), 0.3, 3.0)
    near_port = place_ends(jax.random.randint(key_of[2], (COMPONENTS,), 0, PORT_DEV), jax.random.fold_in(key_of[2], 1), 0, PORT_DEV - 1).astype(jnp.int32)
    far_owner_keys = jax.random.split(jax.random.fold_in(key_of[3], 1), COMPONENTS // COMP_DEV)
    far_owner_turns = jax.random.permutation(jax.random.fold_in(key_of[3], 3), COMPONENTS // COMP_DEV)
    far_owner = jax.vmap(lambda own, number: assign_block(jax.random.fold_in(key_of[3], 2), own, number, COMP_DEV, NPART, 1, CAP, 2))(far_owner_keys, far_owner_turns).reshape((COMPONENTS, 1))
    far_port = place_ends(jax.random.randint(key_of[4], (COMPONENTS,), 0, PORT_DEV), jax.random.fold_in(key_of[4], 1), 0, PORT_DEV - 1).astype(jnp.int32)
    bubble_load = normal_values(key_of[5], (MODES, CASES, COMPONENTS), 1.0, 6.0, ((1, 4), (2, 8)), jnp.float32)
    port_load = normal_values(key_of[6], (PD, CASES, PORTS), 0.5, 3.0, ((1, 4), (2, 8)), jnp.float32)
    bubble_inverse = draw_bubble_inverse(jax.random.fold_in(key_of[10], 71), 0)
    coupling = jnp.clip(jax.random.uniform(key_of[8], (TYPES, 2 * PD, MODES), jnp.float32, -0.1, 0.1), -0.1, 0.1)
    port_block = draw_port_block(jax.random.fold_in(key_of[10], 71), 0)
    return {"comp_type": comp_type, "stiffness": stiffness, "near_port": near_port, "far_owner": far_owner, "far_port": far_port, "bubble_load": bubble_load, "port_load": port_load, "bubble_inverse": bubble_inverse, "coupling": coupling, "port_block": port_block}


HIGH = lax.Precision.HIGHEST

def type_tables(bubble_inverse, coupling, port_block):
    reduced = jnp.einsum('tpm,tmn->tpn', coupling, bubble_inverse, precision=HIGH)
    schur_table = port_block - jnp.einsum('tpm,tqm->tpq', reduced, coupling, precision=HIGH)
    return (reduced, schur_table)

def apply_tables(table, comp_type, factor, vectors):
    in_rows = vectors.shape[0]
    case_count = vectors.shape[1]
    part_count = N_PX * N_PY
    vector_blocks = vectors.reshape(in_rows, case_count, part_count, COMP_DEV).transpose(2, 0, 1, 3)
    kind_blocks = comp_type.reshape(part_count, COMP_DEV)
    factor_blocks = factor.reshape(part_count, COMP_DEV)

    def one_block(packed):
        vector_part, kind_part, factor_part = packed
        matrices = jnp.take(table, kind_part, axis=0)
        result = jnp.einsum('cyx,xkc->ykc', matrices, vector_part, precision=HIGH)
        return result * factor_part[None, None, :]
    results = lax.map(one_block, (vector_blocks, kind_blocks, factor_blocks))
    return results.transpose(1, 2, 0, 3).reshape(results.shape[1], case_count, part_count * COMP_DEV)

def port_indices(near_port, far_owner, far_port):
    owners = jnp.arange(COMPONENTS, dtype=jnp.int32) // COMP_DEV
    return (owners * PORT_DEV + near_port, far_owner[:, 0] * PORT_DEV + far_port)

def spread_ports(port_field, near_global, far_global):
    return jnp.concatenate([jnp.take(port_field, near_global, axis=2), jnp.take(port_field, far_global, axis=2)], axis=0)

def assemble(values, near_global, far_global):
    near_sum = jax.ops.segment_sum(jnp.moveaxis(values[:PD], 2, 0), near_global, num_segments=PORTS)
    far_sum = jax.ops.segment_sum(jnp.moveaxis(values[PD:], 2, 0), far_global, num_segments=PORTS)
    return jnp.moveaxis(near_sum + far_sum, 0, 2)

def port_gram(lhs_field, rhs_field):
    product = jnp.einsum('dkp,djp->kj', lhs_field, rhs_field, precision=HIGH)
    return 0.5 * (product + product.T)

def combine_columns(port_field, weights):
    return jnp.einsum('djp,jk->dkp', port_field, weights, precision=HIGH)

def spd_solve(matrix, target):
    factor = jnp.linalg.cholesky(matrix)
    middle = lax.linalg.triangular_solve(factor, target, left_side=True, lower=True)
    return lax.linalg.triangular_solve(factor, middle, left_side=True, lower=True, transpose_a=True)

def reference(comp_type, stiffness, near_port, far_owner, far_port, bubble_load, port_load, bubble_inverse, coupling, port_block):
    reduced, schur_table = type_tables(bubble_inverse, coupling, port_block)
    near_global, far_global = port_indices(near_port, far_owner, far_port)
    unit_scale = jnp.ones_like(stiffness)
    condensed = -apply_tables(reduced, comp_type, unit_scale, bubble_load)
    rhs_field = port_load + assemble(condensed, near_global, far_global)

    def operate(port_field):
        local_field = spread_ports(port_field, near_global, far_global)
        return assemble(apply_tables(schur_table, comp_type, stiffness, local_field), near_global, far_global)
    solution = jnp.zeros_like(rhs_field)
    residual = rhs_field
    direction = rhs_field
    residual_gram = port_gram(residual, residual)
    for iteration in range(ITERS):
        image_field = operate(direction)
        curvature = port_gram(direction, image_field)
        step_coef = spd_solve(curvature, residual_gram)
        solution = solution + combine_columns(direction, step_coef)
        residual = residual - combine_columns(image_field, step_coef)
        if iteration + 1 < ITERS:
            next_gram = port_gram(residual, residual)
            update_coef = spd_solve(residual_gram, next_gram)
            direction = residual + combine_columns(direction, update_coef)
            residual_gram = next_gram
    port_values = spread_ports(solution, near_global, far_global)
    transposed = jnp.transpose(reduced, (0, 2, 1))
    bubble_solution = apply_tables(bubble_inverse, comp_type, 1.0 / stiffness, bubble_load) - apply_tables(transposed, comp_type, unit_scale, port_values)
    return (solution, residual, bubble_solution)
```

```python
import jax
import jax.numpy as jnp
from jax import lax
from jax.experimental import pallas as pl
from jax.experimental.pallas import tpu as pltpu
from jax.sharding import PartitionSpec as P

HIGH = lax.Precision.HIGHEST
F32 = jnp.float32
BF16 = jnp.bfloat16
MESH = pl.DeviceIdType.MESH
NT = (((1,), (1,)), ((), ()))
TN = (((0,), (0,)), ((), ()))


def split(x):
    top = x.astype(BF16)
    return top, (x - top.astype(F32)).astype(BF16)


def mm(a, b):
    return jnp.dot(a, b, preferred_element_type=F32)


def exact(a, b, dims=(((1,), (0,)), ((), ()))):
    return lax.dot_general(a, b, dims, precision=HIGH, preferred_element_type=F32)


def gauss_solve(matrix, target):
    n = matrix.shape[0]
    aug = jnp.concatenate([matrix, target], axis=1)
    rows = lax.broadcasted_iota(jnp.int32, aug.shape, 0)
    for j in range(0, n, 2):
        row0, row1 = aug[j:j + 1, :], aug[j + 1:j + 2, :]
        col0 = jnp.broadcast_to(aug[:, j:j + 1], aug.shape)
        col1 = jnp.broadcast_to(aug[:, j + 1:j + 2], aug.shape)
        a, c = col0[j:j + 1, :], col0[j + 1:j + 2, :]
        b, d = col1[j:j + 1, :], col1[j + 1:j + 2, :]
        scale = 1.0 / (a * d - b * c)
        new0 = (d * row0 - b * row1) * scale
        new1 = (a * row1 - c * row0) * scale
        rest = aug - col0 * new0 - col1 * new1
        aug = jnp.where(rows == j, new0, jnp.where(rows == j + 1, new1, rest))
    return aug[:, n:]


def kernel(
    sizes,
    kind_hbm,
    near_hbm,
    owner_hbm,
    far_hbm,
    stiff_hbm,
    bload_hbm,
    pload_hbm,
    binv_hbm,
    coup_hbm,
    pblock_hbm,
    sol_ref,
    res_ref,
    bub_ref,
    kind_ref,
    near_ref,
    owner_ref,
    far_ref,
    stiff_ref,
    bload_ref,
    pload_ref,
    binv_ref,
    coup_ref,
    pblock_ref,
    ask_send,
    ask_recv,
    far_send,
    far_recv,
    gath,
    image,
    rows_all,
    pair_send,
    pair_recv,
    curve_send,
    curve_recv,
    curve_mine,
    curve_all,
    inv_keep,
    nat_far,
    in_sem,
    part_ssem,
    part_rsem,
    case_ssem,
    case_rsem,
):
    parts, npy, nq, depth, width, chunks = sizes
    my_x, my_y, my_c = lax.axis_index("px"), lax.axis_index("py"), lax.axis_index("case")
    me = my_x * npy + my_y

    def part_id(step):
        other = lax.rem(me + step + parts, parts)
        return (other // npy, lax.rem(other, npy), my_c)

    def case_to(step):
        if nq == 4:
            other = my_c + (step % 2) * (1 - 2 * lax.rem(my_c, 2))
            return other + (step // 2) * (2 - 4 * (my_c // 2))
        return lax.rem(my_c + step, nq)

    def case_from(step):
        return case_to(step) if nq == 4 else lax.rem(my_c + nq - step, nq)

    def case_id(step):
        return (my_x, my_y, case_to(step))

    direct = (1, 2) if nq == 4 else tuple(range(1, nq))

    barrier = pltpu.get_barrier_semaphore()

    def greet_part(i, _):
        pl.semaphore_signal(barrier, inc=1, device_id=part_id(i), device_id_type=MESH)
        return 0

    lax.fori_loop(1, parts, greet_part, 0)
    for i in range(1, nq):
        pl.semaphore_signal(barrier, inc=1, device_id=case_id(i), device_id_type=MESH)

    inputs = (
        (near_hbm, near_ref),
        (owner_hbm, owner_ref),
        (far_hbm, far_ref),
        (kind_hbm, kind_ref),
        (binv_hbm, binv_ref),
        (bload_hbm, bload_ref),
        (coup_hbm, coup_ref),
        (stiff_hbm, stiff_ref),
        (pload_hbm, pload_ref),
        (pblock_hbm, pblock_ref),
    )
    fetches = [
        pltpu.make_async_copy(src, dst, in_sem.at[i]) for i, (src, dst) in enumerate(inputs)
    ]
    for fetch in fetches:
        fetch.start()

    kinds = binv_ref.shape[0]
    modes, ncase, ncomp = bload_ref.shape
    pd = pload_ref.shape[0]
    nport = pload_ref.shape[2]
    slots = parts * depth
    allcase = nq * ncase

    for fetch in fetches[0:4]:
        fetch.wait()
    kind_row = kind_ref[...]
    near_row = near_ref[...]
    owner_row = owner_ref[...]
    far_row = far_ref[...]

    def as_column(row):
        return jnp.broadcast_to(row.astype(F32), (ncomp, ncomp)).T

    sub = lax.broadcasted_iota(jnp.int32, (ncomp, ncomp), 0)
    lane = lax.broadcasted_iota(jnp.int32, (ncomp, ncomp), 1)
    same = (as_column(owner_row) == owner_row.astype(F32)) & (sub < lane)
    rank = jnp.sum(jnp.where(same, 1.0, 0.0), axis=0, keepdims=True).astype(jnp.int32)
    step_row = lax.rem(owner_row - me + parts, parts)
    slot_row = step_row * depth + rank
    slot_sub = lax.broadcasted_iota(jnp.int32, (slots, ncomp), 0)
    slot_pick = jnp.where(slot_sub == slot_row, 1.0, 0.0).astype(BF16)
    step_sub = lax.broadcasted_iota(jnp.int32, (parts, ncomp), 0)
    naming = jnp.where(step_sub == step_row, (far_row + 1).astype(F32), 0.0)
    ranked = jnp.where(sub == rank, 1.0, 0.0)
    wanted = exact(naming, ranked, NT) - 1.0
    wanted = wanted.reshape(parts, 1, ncomp)
    ask_send[...] = wanted
    ask_recv[0] = wanted[0]
    near_in = jnp.where(sub == near_row, 1.0, 0.0).astype(BF16)
    near_out = jnp.where(lane.astype(F32) == as_column(near_row), 1.0, 0.0).astype(BF16)

    order = sorted(range(1, parts), key=lambda i: -min(i % npy, npy - i % npy))

    def send_parts(src, dst, e, sign):
        def body(i, _):
            pltpu.make_async_remote_copy(
                src_ref=src(i),
                dst_ref=dst(i),
                send_sem=part_ssem.at[e],
                recv_sem=part_rsem.at[e],
                device_id=part_id(i if sign > 0 else -i),
                device_id_type=MESH,
            ).start()
            return 0

        if parts <= 8:
            for i in order:
                body(i, 0)
        else:
            lax.fori_loop(1, parts, body, 0)

    def wait_on(ref, sem):
        pltpu.make_async_copy(ref, ref, sem).wait()

    rest = pl.ds(1, parts - 1)

    def tile_cases(row):
        return jnp.concatenate([row] * ncase, axis=1)

    kind_all = tile_cases(kind_row)
    masks = [jnp.where(kind_all == t, 1.0, 0.0).astype(BF16) for t in range(kinds)]

    def apply_tables(tab, x):
        top, low = split(x)
        lanes = x.shape[1]
        xt = jnp.concatenate([top * m[:, :lanes] for m in masks], axis=0)
        xl = jnp.concatenate([low * m[:, :lanes] for m in masks], axis=0)
        return mm(tab[0], xt) + mm(tab[0], xl) + mm(tab[1], xt)

    def wide(field, rows):
        return jnp.concatenate(
            [field[k * rows:(k + 1) * rows] for k in range(field.shape[0] // rows)], axis=1
        )

    def tall(x):
        return jnp.concatenate(
            [x[:, k * ncomp:(k + 1) * ncomp] for k in range(x.shape[1] // ncomp)], axis=0
        )

    def pick(x, onehot):
        top, low = split(x)
        return mm(jnp.concatenate([top, low], axis=1), jnp.concatenate([onehot, onehot], axis=0))

    def start_far(e, j, onehot, x, sign):
        top, low = split(x)
        out = lax.dot_general(
            jnp.concatenate([onehot, onehot], axis=1),
            jnp.concatenate([top, low], axis=1),
            NT,
            preferred_element_type=F32,
        ).reshape(parts, depth, width)
        far_send[e, j] = out
        far_recv[e, j, 0] = out[0]
        send_parts(
            lambda i: far_send.at[e, j, i], lambda i: far_recv.at[e, j, i], 3 + e * chunks + j, sign
        )

    def finish_far(e, j, onehot):
        wait_on(far_recv.at[e, j, rest], part_rsem.at[3 + e * chunks + j])
        got = far_recv[e, j].reshape(slots, width).T
        top, low = split(got)
        return mm(top, onehot) + mm(low, onehot)

    def send_case(f, src, dst, sem, step):
        pltpu.make_async_remote_copy(
            src_ref=src,
            dst_ref=dst,
            send_sem=case_ssem.at[f, sem],
            recv_sem=case_rsem.at[f, sem],
            device_id=case_id(step),
            device_id_type=MESH,
        ).start()

    def publish(f, field):
        for k in range(ncase):
            gath[f, my_c, :, k, :] = field[k * pd:(k + 1) * pd]
        for i in reversed(direct):
            send_case(f, gath.at[f, my_c], gath.at[f, my_c], i, i)

    def forward(f):
        if nq == 4:
            block = gath.at[f, case_from(2)]
            wait_on(block, case_rsem.at[f, 2])
            send_case(f, block, block, 3, 1)

    def collect(f):
        for i in range(1, nq):
            if nq != 4 or i != 2:
                wait_on(gath.at[f, case_from(i)], case_rsem.at[f, i])

        def body(d, _):
            cols = pl.ds(pl.multiple_of(d * nport, nport), nport)
            for q in range(nq):
                rows_all[pl.ds(f * allcase + q * ncase, ncase), cols] = gath[f, q, d]
            return 0

        lax.fori_loop(0, pd, body, 0, unroll=4)

    def field_rows(f, count=1):
        return rows_all[f * allcase:(f + count) * allcase, :]

    def image_rows(s, field):
        for k in range(ncase):
            image[s, :, k, :] = field[k * pd:(k + 1) * pd]
        return jnp.concatenate([image[s, d] for d in range(pd)], axis=1)

    def start_gram(value):
        folded = jnp.concatenate(
            [value[8 * r:8 * r + 8] for r in range(value.shape[0] // 8)], axis=1
        )
        pair_send[...] = folded
        pair_recv[0] = folded
        send_parts(lambda i: pair_send, lambda i: pair_recv.at[i], 1, 1)

    def finish_gram():
        wait_on(pair_recv.at[rest], part_rsem.at[1])
        total = jnp.sum(pair_recv[...], axis=0)
        return jnp.concatenate(
            [total[:, allcase * r:allcase * (r + 1)] for r in range(total.shape[1] // allcase)],
            axis=0,
        )

    def sym(g):
        return 0.5 * (g + g.T)

    def part(x, j):
        return x[j * width:(j + 1) * width]

    for fetch in fetches[4:7]:
        fetch.wait()
    inv_tab = split(jnp.concatenate([binv_ref[t] for t in range(kinds)], axis=1))
    coup_tab = split(jnp.concatenate([coup_ref[t].T for t in range(kinds)], axis=1))
    loads = jnp.concatenate([bload_ref[:, k, :] for k in range(ncase)], axis=1)
    lifted = apply_tables(inv_tab, loads)
    inv_keep[...] = lifted
    condensed = -apply_tables(coup_tab, lifted)
    leaving = tall(condensed[pd:])
    pl.semaphore_wait(barrier, parts - 1 + nq - 1)
    send_parts(lambda i: ask_send.at[i], lambda i: ask_recv.at[i], 0, 1)
    for j in range(chunks):
        start_far(0, j, slot_pick, part(leaving, j), 1)
    for fetch in fetches[7:]:
        fetch.wait()
    stiff = tile_cases(stiff_ref[...])
    red_t = [exact(binv_ref[t], coup_ref[t], TN) for t in range(kinds)]
    schur = [pblock_ref[t] - exact(red_t[t], coup_ref[t], TN) for t in range(kinds)]
    schur_tab = split(jnp.concatenate(schur, axis=1))
    red_tab = split(jnp.concatenate(red_t, axis=1))
    own = jnp.concatenate([pload_ref[:, k, :] for k in range(ncase)], axis=0)
    own = own + pick(tall(condensed[:pd]), near_out)
    wait_on(ask_recv.at[rest], part_rsem.at[0])
    asked = ask_recv[...].reshape(parts, ncomp)
    asked = jnp.concatenate([asked] * (ncomp // parts), axis=0).T
    port_lane = lax.broadcasted_iota(jnp.int32, (depth, nport), 1).astype(F32)
    asked_pick = jnp.concatenate(
        [jnp.where(asked[0:depth, i:i + 1] == port_lane, 1.0, 0.0) for i in range(parts)], axis=0
    ).astype(BF16)

    def arrive(e, own, onward):
        pieces = []
        for j in range(chunks):
            piece = part(own, j) + finish_far(e, j, asked_pick)
            if onward:
                start_far(e + 1, j, asked_pick, piece, -1)
            pieces.append(piece)
        return jnp.concatenate(pieces, axis=0)

    def operate(e, near, between):
        cuts = [0, ((chunks - 1) * width) // pd, ncase] if chunks > 1 else [0, ncase]
        far, near_y, far_y, sent, have = None, None, None, 0, 0
        for a, b in zip(cuts[:-1], cuts[1:]):
            if b == ncase:
                between()
            while have * width < b * pd:
                piece = finish_far(e, have, slot_pick)
                far = piece if far is None else jnp.concatenate([far, piece], axis=0)
                have += 1
            rows = slice(a * pd, b * pd)
            ends = jnp.concatenate([wide(near[rows], pd), wide(far[rows], pd)], axis=0)
            y = apply_tables(schur_tab, ends) * stiff[:, a * ncomp:b * ncomp]
            out = tall(y[pd:])
            far_y = out if far_y is None else jnp.concatenate([far_y, out], axis=0)
            out = tall(y[:pd])
            near_y = out if near_y is None else jnp.concatenate([near_y, out], axis=0)
            while (sent + 1) * width <= b * pd:
                start_far(e + 1, sent, slot_pick, part(far_y, sent), 1)
                sent += 1
        return far, far_y, pick(near_y, near_out)

    base = arrive(0, own, True)
    publish(0, base)
    far_base, _, own = operate(1, pick(base, near_in), lambda: forward(0))
    publish(3, far_base)
    first = arrive(2, own, True)
    publish(1, first)
    near = pick(first, near_in)
    forward(3)
    collect(0)
    far_first, far_image, own = operate(3, near, lambda: forward(1))
    publish(4, far_first)
    collect(1)
    pair = field_rows(0, 2)
    square = exact(pair, pair, NT)
    start_gram(
        jnp.concatenate(
            [
                square[0:allcase, 0:allcase],
                square[0:allcase, allcase:],
                square[allcase:, allcase:],
            ],
            axis=0,
        )
    )
    near_curve = exact(image_rows(0, own), field_rows(1), NT)
    far_lines = image_rows(1, far_image)
    second = arrive(4, own, False)
    publish(2, second)
    forward(4)
    collect(4)

    n = allcase
    curve = near_curve + exact(far_lines, field_rows(4), NT)
    curve = jnp.concatenate([curve, jnp.zeros((ncase, 128 - n), F32)], axis=1)
    curve_send[...] = curve
    curve_recv[0] = curve
    send_parts(lambda i: curve_send, lambda i: curve_recv.at[i], 2, 1)

    grams = finish_gram()
    g00 = sym(grams[0:n])
    g01 = sym(grams[n:2 * n])
    g11 = sym(grams[2 * n:3 * n])
    both = gauss_solve(g01, jnp.concatenate([g00, g11], axis=1))
    forward(2)
    image_both = exact(g11, both)
    mine = jnp.where(
        lax.broadcasted_iota(jnp.int32, (n, ncase), 0)
        == lax.broadcasted_iota(jnp.int32, (n, ncase), 1) + my_c * ncase,
        1.0,
        0.0,
    )
    chosen = exact(jnp.concatenate([image_both[:, 0:n] - g01, both[:, 0:n]], axis=0), mine)

    wait_on(curve_recv.at[rest], part_rsem.at[2])
    total = jnp.sum(curve_recv[...], axis=0)
    curve_mine[...] = total
    curve_all[my_c] = total
    for i in range(1, nq):
        send_case(5, curve_mine, curve_all.at[my_c], i, i)
    collect(3)
    for i in range(1, nq):
        wait_on(curve_all.at[case_from(i)], case_rsem.at[5, i])
    g12 = curve_all[...].reshape(n, 128)[:, 0:n]
    beta = gauss_solve(sym(g12) - sym(image_both[:, n:2 * n]), chosen[0:n])
    alpha = chosen[n:2 * n] + exact(both[:, n:2 * n], beta)
    coefs = jnp.concatenate([alpha, -beta], axis=0).T
    ctop, clow = split(coefs)
    stack = jnp.concatenate([ctop, clow], axis=0)

    def mix(f):
        vtop, vlow = split(field_rows(f, 2))
        lead = mm(stack, vtop)
        return lead[0:ncase] + lead[ncase:] + mm(ctop, vlow)

    answer_rows = mix(0)
    for d in range(pd):
        sol_ref[d] = answer_rows[:, d * nport:(d + 1) * nport]
    far_rows = mix(3)
    for d in range(pd):
        nat_far[d] = far_rows[:, d * nport:(d + 1) * nport]
    answer = jnp.concatenate([sol_ref[:, k, :] for k in range(ncase)], axis=0)
    near = wide(pick(answer, near_in), pd)
    ends = jnp.concatenate(
        [near, jnp.concatenate([nat_far[:, k, :] for k in range(ncase)], axis=1)], axis=0
    )
    scaled = inv_keep[...] / stiff
    back = scaled - apply_tables(red_tab, ends)
    for k in range(ncase):
        bub_ref[:, k, :] = back[:, k * ncomp:(k + 1) * ncomp]
    collect(2)
    drop_rows = mix(1)
    for d in range(pd):
        res_ref[d] = gath[0, my_c, d] - drop_rows[:, d * nport:(d + 1) * nport]

    wait_on(ask_send.at[rest], part_ssem.at[0])
    for e in range(5):
        for j in range(chunks):
            wait_on(far_send.at[e, j, rest], part_ssem.at[3 + e * chunks + j])
    wait_on(pair_recv.at[rest], part_ssem.at[1])
    wait_on(curve_recv.at[rest], part_ssem.at[2])
    for f in range(5):
        for i in range(1, nq):
            wait_on(gath.at[f, my_c], case_ssem.at[f, i])
    for i in range(1, nq):
        wait_on(curve_mine, case_ssem.at[5, i])


def emit(*refs):
    count = len(refs) // 2
    sems = refs[-1]
    copies = [
        pltpu.make_async_copy(refs[i], refs[count + i], sems.at[i]) for i in range(count)
    ]
    for copy in copies:
        copy.start()
    for copy in copies:
        copy.wait()


def local(
    comp_type,
    stiffness,
    near_port,
    far_owner,
    far_port,
    bubble_load,
    port_load,
    bubble_inverse,
    coupling,
    port_block,
):
    npy = lax.axis_size("py")
    parts = lax.axis_size("px") * npy
    nq = lax.axis_size("case")
    ncomp = comp_type.shape[0]
    modes, ncase, _ = bubble_load.shape
    pd, _, nport = port_load.shape
    kinds = bubble_inverse.shape[0]
    cap = 3 * ncomp // (2 * parts)
    depth = -(-cap // 8) * 8
    allcase = nq * ncase
    width = 128 if (ncase * pd) % 128 == 0 else ncase * pd
    chunks = ncase * pd // width
    vmem = pl.BlockSpec(memory_space=pltpu.VMEM)
    hbm = pl.BlockSpec(memory_space=pltpu.HBM)

    def body(*refs):
        kernel((parts, npy, nq, depth, width, chunks), *refs)

    shapes = (
        jax.ShapeDtypeStruct(port_load.shape, F32),
        jax.ShapeDtypeStruct(port_load.shape, F32),
        jax.ShapeDtypeStruct(bubble_load.shape, F32),
    )
    results = pl.pallas_call(
        body,
        out_shape=shapes,
        in_specs=[hbm] * 10,
        out_specs=(vmem, vmem, vmem),
        scratch_shapes=[
            pltpu.VMEM((1, ncomp), jnp.int32),
            pltpu.VMEM((1, ncomp), jnp.int32),
            pltpu.VMEM((1, ncomp), jnp.int32),
            pltpu.VMEM((1, ncomp), jnp.int32),
            pltpu.VMEM((1, ncomp), F32),
            pltpu.VMEM(bubble_load.shape, F32),
            pltpu.VMEM(port_load.shape, F32),
            pltpu.VMEM(bubble_inverse.shape, F32),
            pltpu.VMEM((kinds, modes, 2 * pd), F32),
            pltpu.VMEM(port_block.shape, F32),
            pltpu.VMEM((parts, 1, ncomp), F32),
            pltpu.VMEM((parts, 1, ncomp), F32),
            pltpu.VMEM((5, chunks, parts, depth, width), F32),
            pltpu.VMEM((5, chunks, parts, depth, width), F32),
            pltpu.VMEM((5, nq, pd, ncase, nport), F32),
            pltpu.VMEM((2, pd, ncase, nport), F32),
            pltpu.VMEM((5 * allcase, pd * nport), F32),
            pltpu.VMEM((8, 3 * allcase * allcase // 8), F32),
            pltpu.VMEM((parts, 8, 3 * allcase * allcase // 8), F32),
            pltpu.VMEM((ncase, 128), F32),
            pltpu.VMEM((parts, ncase, 128), F32),
            pltpu.VMEM((ncase, 128), F32),
            pltpu.VMEM((nq, ncase, 128), F32),
            pltpu.VMEM((modes, ncase * ncomp), F32),
            pltpu.VMEM((pd, ncase, nport), F32),
            pltpu.SemaphoreType.DMA((10,)),
            pltpu.SemaphoreType.DMA((3 + 5 * chunks,)),
            pltpu.SemaphoreType.DMA((3 + 5 * chunks,)),
            pltpu.SemaphoreType.DMA((6, nq)),
            pltpu.SemaphoreType.DMA((6, nq)),
        ],
        compiler_params=pltpu.CompilerParams(
            collective_id=0, has_side_effects=True, vmem_limit_bytes=32 * 1024 * 1024
        ),
        name="condensed_solve",
    )(
        comp_type.reshape(1, ncomp),
        near_port.reshape(1, ncomp),
        far_owner.reshape(1, ncomp),
        far_port.reshape(1, ncomp),
        stiffness.reshape(1, ncomp),
        bubble_load,
        port_load,
        bubble_inverse,
        jnp.swapaxes(coupling, 1, 2),
        port_block,
    )
    return pl.pallas_call(
        emit,
        out_shape=shapes,
        in_specs=[vmem] * 3,
        out_specs=(hbm, hbm, hbm),
        scratch_shapes=[pltpu.SemaphoreType.DMA((3,))],
        compiler_params=pltpu.CompilerParams(vmem_limit_bytes=4 * 1024 * 1024),
        name="emit",
    )(*results)


def solution(mesh):
    placed = (
        P(("px", "py")),
        P(("px", "py")),
        P(("px", "py")),
        P(("px", "py"), None),
        P(("px", "py")),
        P(None, "case", ("px", "py")),
        P(None, "case", ("px", "py")),
        P(),
        P(),
        P(),
    )
    return jax.shard_map(
        local,
        mesh=mesh,
        in_specs=placed,
        out_specs=(
            P(None, "case", ("px", "py")),
            P(None, "case", ("px", "py")),
            P(None, "case", ("px", "py")),
        ),
        check_vma=False,
    )
```

```python
import jax
import jax.numpy as jnp
from jax import lax
from jax.experimental import pallas as pl
from jax.experimental.pallas import tpu as pltpu
from jax.sharding import PartitionSpec as P

HIGH = lax.Precision.HIGHEST
F32 = jnp.float32
BF16 = jnp.bfloat16
MESH = pl.DeviceIdType.MESH
NT = (((1,), (1,)), ((), ()))
TN = (((0,), (0,)), ((), ()))


def split(x):
    top = x.astype(BF16)
    return top, (x - top.astype(F32)).astype(BF16)


def mm(a, b):
    return jnp.dot(a, b, preferred_element_type=F32)


def exact(a, b, dims=(((1,), (0,)), ((), ()))):
    return lax.dot_general(a, b, dims, precision=HIGH, preferred_element_type=F32)


def gauss_solve(matrix, target):
    n = matrix.shape[0]
    aug = jnp.concatenate([matrix, target], axis=1)
    rows = lax.broadcasted_iota(jnp.int32, aug.shape, 0)
    for j in range(0, n, 2):
        row0, row1 = aug[j:j + 1, :], aug[j + 1:j + 2, :]
        col0 = jnp.broadcast_to(aug[:, j:j + 1], aug.shape)
        col1 = jnp.broadcast_to(aug[:, j + 1:j + 2], aug.shape)
        a, c = col0[j:j + 1, :], col0[j + 1:j + 2, :]
        b, d = col1[j:j + 1, :], col1[j + 1:j + 2, :]
        scale = 1.0 / (a * d - b * c)
        new0 = (d * row0 - b * row1) * scale
        new1 = (a * row1 - c * row0) * scale
        rest = aug - col0 * new0 - col1 * new1
        aug = jnp.where(rows == j, new0, jnp.where(rows == j + 1, new1, rest))
    return aug[:, n:]


def kernel(
    sizes,
    kind_hbm,
    near_hbm,
    owner_hbm,
    far_hbm,
    stiff_hbm,
    bload_hbm,
    pload_hbm,
    binv_hbm,
    coup_hbm,
    pblock_hbm,
    sol_ref,
    res_ref,
    bub_ref,
    kind_ref,
    near_ref,
    owner_ref,
    far_ref,
    stiff_ref,
    bload_ref,
    pload_ref,
    binv_ref,
    coup_ref,
    pblock_ref,
    ask_send,
    ask_recv,
    far_send,
    far_recv,
    gath,
    image,
    rows_all,
    pair_send,
    pair_recv,
    curve_send,
    curve_recv,
    curve_mine,
    curve_all,
    inv_keep,
    nat_far,
    in_sem,
    part_ssem,
    part_rsem,
    case_ssem,
    case_rsem,
):
    parts, npy, nq, depth, width, chunks = sizes
    my_x, my_y, my_c = lax.axis_index("px"), lax.axis_index("py"), lax.axis_index("case")
    me = my_x * npy + my_y

    def part_id(step):
        other = lax.rem(me + step + parts, parts)
        return (other // npy, lax.rem(other, npy), my_c)

    def case_to(step):
        if nq == 4:
            other = my_c + (step % 2) * (1 - 2 * lax.rem(my_c, 2))
            return other + (step // 2) * (2 - 4 * (my_c // 2))
        return lax.rem(my_c + step, nq)

    def case_from(step):
        return case_to(step) if nq == 4 else lax.rem(my_c + nq - step, nq)

    def case_id(step):
        return (my_x, my_y, case_to(step))

    direct = (1, 2) if nq == 4 else tuple(range(1, nq))

    barrier = pltpu.get_barrier_semaphore()

    def greet_part(i, _):
        pl.semaphore_signal(barrier, inc=1, device_id=part_id(i), device_id_type=MESH)
        return 0

    lax.fori_loop(1, parts, greet_part, 0)
    for i in range(1, nq):
        pl.semaphore_signal(barrier, inc=1, device_id=case_id(i), device_id_type=MESH)

    inputs = (
        (near_hbm, near_ref),
        (owner_hbm, owner_ref),
        (far_hbm, far_ref),
        (kind_hbm, kind_ref),
        (binv_hbm, binv_ref),
        (bload_hbm, bload_ref),
        (coup_hbm, coup_ref),
        (stiff_hbm, stiff_ref),
        (pload_hbm, pload_ref),
        (pblock_hbm, pblock_ref),
    )
    fetches = [
        pltpu.make_async_copy(src, dst, in_sem.at[i]) for i, (src, dst) in enumerate(inputs)
    ]
    for fetch in fetches:
        fetch.start()

    kinds = binv_ref.shape[0]
    modes, ncase, ncomp = bload_ref.shape
    pd = pload_ref.shape[0]
    nport = pload_ref.shape[2]
    slots = parts * depth
    allcase = nq * ncase

    for fetch in fetches[0:4]:
        fetch.wait()
    kind_row = kind_ref[...]
    near_row = near_ref[...]
    owner_row = owner_ref[...]
    far_row = far_ref[...]

    def as_column(row):
        return jnp.broadcast_to(row.astype(F32), (ncomp, ncomp)).T

    sub = lax.broadcasted_iota(jnp.int32, (ncomp, ncomp), 0)
    lane = lax.broadcasted_iota(jnp.int32, (ncomp, ncomp), 1)
    same = (as_column(owner_row) == owner_row.astype(F32)) & (sub < lane)
    rank = jnp.sum(jnp.where(same, 1.0, 0.0), axis=0, keepdims=True).astype(jnp.int32)
    step_row = lax.rem(owner_row - me + parts, parts)
    slot_row = step_row * depth + rank
    slot_sub = lax.broadcasted_iota(jnp.int32, (slots, ncomp), 0)
    slot_pick = jnp.where(slot_sub == slot_row, 1.0, 0.0).astype(BF16)
    step_sub = lax.broadcasted_iota(jnp.int32, (parts, ncomp), 0)
    naming = jnp.where(step_sub == step_row, (far_row + 1).astype(F32), 0.0)
    ranked = jnp.where(sub == rank, 1.0, 0.0)
    wanted = exact(naming, ranked, NT) - 1.0
    wanted = wanted.reshape(parts, 1, ncomp)
    ask_send[...] = wanted
    ask_recv[0] = wanted[0]
    near_in = jnp.where(sub == near_row, 1.0, 0.0).astype(BF16)
    near_out = jnp.where(lane.astype(F32) == as_column(near_row), 1.0, 0.0).astype(BF16)

    order = sorted(range(1, parts), key=lambda i: -min(i % npy, npy - i % npy))

    def send_parts(src, dst, e, sign):
        def body(i, _):
            pltpu.make_async_remote_copy(
                src_ref=src(i),
                dst_ref=dst(i),
                send_sem=part_ssem.at[e],
                recv_sem=part_rsem.at[e],
                device_id=part_id(i if sign > 0 else -i),
                device_id_type=MESH,
            ).start()
            return 0

        if parts <= 8:
            for i in order:
                body(i, 0)
        else:
            lax.fori_loop(1, parts, body, 0)

    def wait_on(ref, sem):
        pltpu.make_async_copy(ref, ref, sem).wait()

    rest = pl.ds(1, parts - 1)

    def tile_cases(row):
        return jnp.concatenate([row] * ncase, axis=1)

    kind_all = tile_cases(kind_row)
    masks = [jnp.where(kind_all == t, 1.0, 0.0).astype(BF16) for t in range(kinds)]

    def apply_tables(tab, x):
        top, low = split(x)
        lanes = x.shape[1]
        xt = jnp.concatenate([top * m[:, :lanes] for m in masks], axis=0)
        xl = jnp.concatenate([low * m[:, :lanes] for m in masks], axis=0)
        return mm(tab[0], xt) + mm(tab[0], xl) + mm(tab[1], xt)

    def wide(field, rows):
        return jnp.concatenate(
            [field[k * rows:(k + 1) * rows] for k in range(field.shape[0] // rows)], axis=1
        )

    def tall(x):
        return jnp.concatenate(
            [x[:, k * ncomp:(k + 1) * ncomp] for k in range(x.shape[1] // ncomp)], axis=0
        )

    def pick(x, onehot):
        top, low = split(x)
        return mm(jnp.concatenate([top, low], axis=1), jnp.concatenate([onehot, onehot], axis=0))

    def start_far(e, j, onehot, x, sign):
        top, low = split(x)
        out = lax.dot_general(
            jnp.concatenate([onehot, onehot], axis=1),
            jnp.concatenate([top, low], axis=1),
            NT,
            preferred_element_type=F32,
        ).reshape(parts, depth, width)
        far_send[e, j] = out
        far_recv[e, j, 0] = out[0]
        send_parts(
            lambda i: far_send.at[e, j, i], lambda i: far_recv.at[e, j, i], 3 + e * chunks + j, sign
        )

    def finish_far(e, j, onehot):
        wait_on(far_recv.at[e, j, rest], part_rsem.at[3 + e * chunks + j])
        got = far_recv[e, j].reshape(slots, width).T
        top, low = split(got)
        return mm(top, onehot) + mm(low, onehot)

    def send_case(f, src, dst, sem, step):
        pltpu.make_async_remote_copy(
            src_ref=src,
            dst_ref=dst,
            send_sem=case_ssem.at[f, sem],
            recv_sem=case_rsem.at[f, sem],
            device_id=case_id(step),
            device_id_type=MESH,
        ).start()

    def publish(f, field):
        for k in range(ncase):
            gath[f, my_c, :, k, :] = field[k * pd:(k + 1) * pd]
        for i in reversed(direct):
            send_case(f, gath.at[f, my_c], gath.at[f, my_c], i, i)

    def forward(f):
        if nq == 4:
            block = gath.at[f, case_from(2)]
            wait_on(block, case_rsem.at[f, 2])
            send_case(f, block, block, 3, 1)

    def collect(f):
        for i in range(1, nq):
            if nq != 4 or i != 2:
                wait_on(gath.at[f, case_from(i)], case_rsem.at[f, i])

        def body(d, _):
            cols = pl.ds(pl.multiple_of(d * nport, nport), nport)
            for q in range(nq):
                rows_all[pl.ds(f * allcase + q * ncase, ncase), cols] = gath[f, q, d]
            return 0

        lax.fori_loop(0, pd, body, 0, unroll=4)

    def field_rows(f, count=1):
        return rows_all[f * allcase:(f + count) * allcase, :]

    def image_rows(s, field):
        for k in range(ncase):
            image[s, :, k, :] = field[k * pd:(k + 1) * pd]
        return jnp.concatenate([image[s, d] for d in range(pd)], axis=1)

    def start_gram(value):
        folded = jnp.concatenate(
            [value[8 * r:8 * r + 8] for r in range(value.shape[0] // 8)], axis=1
        )
        pair_send[...] = folded
        pair_recv[0] = folded
        send_parts(lambda i: pair_send, lambda i: pair_recv.at[i], 1, 1)

    def finish_gram():
        wait_on(pair_recv.at[rest], part_rsem.at[1])
        total = jnp.sum(pair_recv[...], axis=0)
        return jnp.concatenate(
            [total[:, allcase * r:allcase * (r + 1)] for r in range(total.shape[1] // allcase)],
            axis=0,
        )

    def sym(g):
        return 0.5 * (g + g.T)

    def part(x, j):
        return x[j * width:(j + 1) * width]

    for fetch in fetches[4:7]:
        fetch.wait()
    inv_tab = split(jnp.concatenate([binv_ref[t] for t in range(kinds)], axis=1))
    coup_tab = split(jnp.concatenate([coup_ref[t].T for t in range(kinds)], axis=1))
    loads = jnp.concatenate([bload_ref[:, k, :] for k in range(ncase)], axis=1)
    lifted = apply_tables(inv_tab, loads)
    inv_keep[...] = lifted
    condensed = -apply_tables(coup_tab, lifted)
    leaving = tall(condensed[pd:])
    pl.semaphore_wait(barrier, parts - 1 + nq - 1)
    send_parts(lambda i: ask_send.at[i], lambda i: ask_recv.at[i], 0, 1)
    for j in range(chunks):
        start_far(0, j, slot_pick, part(leaving, j), 1)
    for fetch in fetches[7:]:
        fetch.wait()
    stiff = tile_cases(stiff_ref[...])
    red_t = [exact(binv_ref[t], coup_ref[t], TN) for t in range(kinds)]
    schur = [pblock_ref[t] - exact(red_t[t], coup_ref[t], TN) for t in range(kinds)]
    schur_tab = split(jnp.concatenate(schur, axis=1))
    red_tab = split(jnp.concatenate(red_t, axis=1))
    own = jnp.concatenate([pload_ref[:, k, :] for k in range(ncase)], axis=0)
    own = own + pick(tall(condensed[:pd]), near_out)
    wait_on(ask_recv.at[rest], part_rsem.at[0])
    asked = ask_recv[...].reshape(parts, ncomp)
    asked = jnp.concatenate([asked] * (ncomp // parts), axis=0).T
    port_lane = lax.broadcasted_iota(jnp.int32, (depth, nport), 1).astype(F32)
    asked_pick = jnp.concatenate(
        [jnp.where(asked[0:depth, i:i + 1] == port_lane, 1.0, 0.0) for i in range(parts)], axis=0
    ).astype(BF16)

    def arrive(e, own, onward):
        pieces = []
        for j in range(chunks):
            piece = part(own, j) + finish_far(e, j, asked_pick)
            if onward:
                start_far(e + 1, j, asked_pick, piece, -1)
            pieces.append(piece)
        return jnp.concatenate(pieces, axis=0)

    def operate(e, near, between):
        cuts = [0, ((chunks - 1) * width) // pd, ncase] if chunks > 1 else [0, ncase]
        far, near_y, far_y, sent, have = None, None, None, 0, 0
        for a, b in zip(cuts[:-1], cuts[1:]):
            if b == ncase:
                between()
            while have * width < b * pd:
                piece = finish_far(e, have, slot_pick)
                far = piece if far is None else jnp.concatenate([far, piece], axis=0)
                have += 1
            rows = slice(a * pd, b * pd)
            ends = jnp.concatenate([wide(near[rows], pd), wide(far[rows], pd)], axis=0)
            y = apply_tables(schur_tab, ends) * stiff[:, a * ncomp:b * ncomp]
            out = tall(y[pd:])
            far_y = out if far_y is None else jnp.concatenate([far_y, out], axis=0)
            out = tall(y[:pd])
            near_y = out if near_y is None else jnp.concatenate([near_y, out], axis=0)
            while (sent + 1) * width <= b * pd:
                start_far(e + 1, sent, slot_pick, part(far_y, sent), 1)
                sent += 1
        return far, far_y, pick(near_y, near_out)

    base = arrive(0, own, True)
    publish(0, base)
    far_base, _, own = operate(1, pick(base, near_in), lambda: forward(0))
    publish(3, far_base)
    first = arrive(2, own, True)
    publish(1, first)
    near = pick(first, near_in)
    forward(3)
    collect(0)
    far_first, far_image, own = operate(3, near, lambda: forward(1))
    publish(4, far_first)
    collect(1)
    pair = field_rows(0, 2)
    square = exact(pair, pair, NT)
    start_gram(
        jnp.concatenate(
            [
                square[0:allcase, 0:allcase],
                square[0:allcase, allcase:],
                square[allcase:, allcase:],
            ],
            axis=0,
        )
    )
    near_curve = exact(image_rows(0, own), field_rows(1), NT)
    far_lines = image_rows(1, far_image)
    second = arrive(4, own, False)
    publish(2, second)
    forward(4)
    collect(4)

    n = allcase
    curve = near_curve + exact(far_lines, field_rows(4), NT)
    curve = jnp.concatenate([curve, jnp.zeros((ncase, 128 - n), F32)], axis=1)
    curve_send[...] = curve
    curve_recv[0] = curve
    send_parts(lambda i: curve_send, lambda i: curve_recv.at[i], 2, 1)

    grams = finish_gram()
    g00 = sym(grams[0:n])
    g01 = sym(grams[n:2 * n])
    g11 = sym(grams[2 * n:3 * n])
    both = gauss_solve(g01, jnp.concatenate([g00, g11], axis=1))
    forward(2)
    image_both = exact(g11, both)
    mine = jnp.where(
        lax.broadcasted_iota(jnp.int32, (n, ncase), 0)
        == lax.broadcasted_iota(jnp.int32, (n, ncase), 1) + my_c * ncase,
        1.0,
        0.0,
    )
    chosen = exact(jnp.concatenate([image_both[:, 0:n] - g01, both[:, 0:n]], axis=0), mine)

    wait_on(curve_recv.at[rest], part_rsem.at[2])
    total = jnp.sum(curve_recv[...], axis=0)
    curve_mine[...] = total
    curve_all[my_c] = total
    for i in range(1, nq):
        send_case(5, curve_mine, curve_all.at[my_c], i, i)
    collect(3)
    for i in range(1, nq):
        wait_on(curve_all.at[case_from(i)], case_rsem.at[5, i])
    g12 = curve_all[...].reshape(n, 128)[:, 0:n]
    beta = gauss_solve(sym(g12) - sym(image_both[:, n:2 * n]), chosen[0:n])
    alpha = chosen[n:2 * n] + exact(both[:, n:2 * n], beta)
    coefs = jnp.concatenate([alpha, -beta], axis=0).T
    ctop, clow = split(coefs)
    stack = jnp.concatenate([ctop, clow], axis=0)

    def mix(f):
        vtop, vlow = split(field_rows(f, 2))
        lead = mm(stack, vtop)
        return lead[0:ncase] + lead[ncase:] + mm(ctop, vlow)

    answer_rows = mix(0)
    for d in range(pd):
        sol_ref[d] = answer_rows[:, d * nport:(d + 1) * nport]
    far_rows = mix(3)
    for d in range(pd):
        nat_far[d] = far_rows[:, d * nport:(d + 1) * nport]
    answer = jnp.concatenate([sol_ref[:, k, :] for k in range(ncase)], axis=0)
    near = wide(pick(answer, near_in), pd)
    ends = jnp.concatenate(
        [near, jnp.concatenate([nat_far[:, k, :] for k in range(ncase)], axis=1)], axis=0
    )
    scaled = inv_keep[...] / stiff
    back = scaled - apply_tables(red_tab, ends)
    for k in range(ncase):
        bub_ref[:, k, :] = back[:, k * ncomp:(k + 1) * ncomp]
    collect(2)
    drop_rows = mix(1)
    for d in range(pd):
        res_ref[d] = gath[0, my_c, d] - drop_rows[:, d * nport:(d + 1) * nport]

    wait_on(ask_send.at[rest], part_ssem.at[0])
    for e in range(5):
        for j in range(chunks):
            wait_on(far_send.at[e, j, rest], part_ssem.at[3 + e * chunks + j])
    wait_on(pair_recv.at[rest], part_ssem.at[1])
    wait_on(curve_recv.at[rest], part_ssem.at[2])
    for f in range(5):
        for i in range(1, nq):
            wait_on(gath.at[f, my_c], case_ssem.at[f, i])
    for i in range(1, nq):
        wait_on(curve_mine, case_ssem.at[5, i])


def emit(*refs):
    count = len(refs) // 2
    sems = refs[-1]
    copies = [
        pltpu.make_async_copy(refs[i], refs[count + i], sems.at[i]) for i in range(count)
    ]
    for copy in copies:
        copy.start()
    for copy in copies:
        copy.wait()


def local(
    comp_type,
    stiffness,
    near_port,
    far_owner,
    far_port,
    bubble_load,
    port_load,
    bubble_inverse,
    coupling,
    port_block,
):
    npy = lax.axis_size("py")
    parts = lax.axis_size("px") * npy
    nq = lax.axis_size("case")
    ncomp = comp_type.shape[0]
    modes, ncase, _ = bubble_load.shape
    pd, _, nport = port_load.shape
    kinds = bubble_inverse.shape[0]
    cap = 3 * ncomp // (2 * parts)
    depth = -(-cap // 8) * 8
    allcase = nq * ncase
    width = 128 if (ncase * pd) % 128 == 0 else ncase * pd
    chunks = ncase * pd // width
    vmem = pl.BlockSpec(memory_space=pltpu.VMEM)
    hbm = pl.BlockSpec(memory_space=pltpu.HBM)

    def body(*refs):
        kernel((parts, npy, nq, depth, width, chunks), *refs)

    shapes = (
        jax.ShapeDtypeStruct(port_load.shape, F32),
        jax.ShapeDtypeStruct(port_load.shape, F32),
        jax.ShapeDtypeStruct(bubble_load.shape, F32),
    )
    results = pl.pallas_call(
        body,
        out_shape=shapes,
        in_specs=[hbm] * 10,
        out_specs=(vmem, vmem, vmem),
        scratch_shapes=[
            pltpu.VMEM((1, ncomp), jnp.int32),
            pltpu.VMEM((1, ncomp), jnp.int32),
            pltpu.VMEM((1, ncomp), jnp.int32),
            pltpu.VMEM((1, ncomp), jnp.int32),
            pltpu.VMEM((1, ncomp), F32),
            pltpu.VMEM(bubble_load.shape, F32),
            pltpu.VMEM(port_load.shape, F32),
            pltpu.VMEM(bubble_inverse.shape, F32),
            pltpu.VMEM((kinds, modes, 2 * pd), F32),
            pltpu.VMEM(port_block.shape, F32),
            pltpu.VMEM((parts, 1, ncomp), F32),
            pltpu.VMEM((parts, 1, ncomp), F32),
            pltpu.VMEM((5, chunks, parts, depth, width), F32),
            pltpu.VMEM((5, chunks, parts, depth, width), F32),
            pltpu.VMEM((5, nq, pd, ncase, nport), F32),
            pltpu.VMEM((2, pd, ncase, nport), F32),
            pltpu.VMEM((5 * allcase, pd * nport), F32),
            pltpu.VMEM((8, 3 * allcase * allcase // 8), F32),
            pltpu.VMEM((parts, 8, 3 * allcase * allcase // 8), F32),
            pltpu.VMEM((ncase, 128), F32),
            pltpu.VMEM((parts, ncase, 128), F32),
            pltpu.VMEM((ncase, 128), F32),
            pltpu.VMEM((nq, ncase, 128), F32),
            pltpu.VMEM((modes, ncase * ncomp), F32),
            pltpu.VMEM((pd, ncase, nport), F32),
            pltpu.SemaphoreType.DMA((10,)),
            pltpu.SemaphoreType.DMA((3 + 5 * chunks,)),
            pltpu.SemaphoreType.DMA((3 + 5 * chunks,)),
            pltpu.SemaphoreType.DMA((6, nq)),
            pltpu.SemaphoreType.DMA((6, nq)),
        ],
        compiler_params=pltpu.CompilerParams(
            collective_id=0, has_side_effects=True, vmem_limit_bytes=32 * 1024 * 1024
        ),
        name="condensed_solve",
    )(
        *(
            pltpu.with_memory_space_constraint(x, pltpu.HBM)
            for x in (
                comp_type.reshape(1, ncomp),
                near_port.reshape(1, ncomp),
                far_owner.reshape(1, ncomp),
                far_port.reshape(1, ncomp),
                stiffness.reshape(1, ncomp),
                bubble_load,
                port_load,
                bubble_inverse,
                jnp.swapaxes(coupling, 1, 2),
                port_block,
            )
        )
    )
    return pl.pallas_call(
        emit,
        out_shape=shapes,
        in_specs=[vmem] * 3,
        out_specs=(hbm, hbm, hbm),
        scratch_shapes=[pltpu.SemaphoreType.DMA((3,))],
        compiler_params=pltpu.CompilerParams(vmem_limit_bytes=4 * 1024 * 1024),
        name="emit",
    )(*results)


def solution(mesh):
    placed = (
        P(("px", "py")),
        P(("px", "py")),
        P(("px", "py")),
        P(("px", "py"), None),
        P(("px", "py")),
        P(None, "case", ("px", "py")),
        P(None, "case", ("px", "py")),
        P(),
        P(),
        P(),
    )
    return jax.shard_map(
        local,
        mesh=mesh,
        in_specs=placed,
        out_specs=(
            P(None, "case", ("px", "py")),
            P(None, "case", ("px", "py")),
            P(None, "case", ("px", "py")),
        ),
        check_vma=False,
    )
```

```python
import jax
import jax.numpy as jnp
from jax import lax
from jax.experimental import pallas as pl
from jax.experimental.pallas import tpu as pltpu
from jax.sharding import PartitionSpec as P

HIGH = lax.Precision.HIGHEST
F32 = jnp.float32
BF16 = jnp.bfloat16
MESH = pl.DeviceIdType.MESH
NT = (((1,), (1,)), ((), ()))
TN = (((0,), (0,)), ((), ()))


def split(x):
    top = x.astype(BF16)
    return top, (x - top.astype(F32)).astype(BF16)


def mm(a, b):
    return jnp.dot(a, b, preferred_element_type=F32)


def exact(a, b, dims=(((1,), (0,)), ((), ()))):
    return lax.dot_general(a, b, dims, precision=HIGH, preferred_element_type=F32)


def gauss_solve(matrix, target):
    n = matrix.shape[0]
    aug = jnp.concatenate([matrix, target], axis=1)
    rows = lax.broadcasted_iota(jnp.int32, aug.shape, 0)
    for j in range(0, n, 2):
        row0, row1 = aug[j:j + 1, :], aug[j + 1:j + 2, :]
        col0 = jnp.broadcast_to(aug[:, j:j + 1], aug.shape)
        col1 = jnp.broadcast_to(aug[:, j + 1:j + 2], aug.shape)
        a, c = col0[j:j + 1, :], col0[j + 1:j + 2, :]
        b, d = col1[j:j + 1, :], col1[j + 1:j + 2, :]
        scale = 1.0 / (a * d - b * c)
        new0 = (d * row0 - b * row1) * scale
        new1 = (a * row1 - c * row0) * scale
        rest = aug - col0 * new0 - col1 * new1
        aug = jnp.where(rows == j, new0, jnp.where(rows == j + 1, new1, rest))
    return aug[:, n:]


def kernel(
    sizes,
    kind_hbm,
    near_hbm,
    owner_hbm,
    far_hbm,
    stiff_hbm,
    bload_hbm,
    pload_hbm,
    binv_hbm,
    coup_hbm,
    pblock_hbm,
    sol_ref,
    res_ref,
    bub_ref,
    kind_ref,
    near_ref,
    owner_ref,
    far_ref,
    stiff_ref,
    bload_ref,
    pload_ref,
    binv_ref,
    coup_ref,
    pblock_ref,
    ask_send,
    ask_recv,
    far_send,
    far_recv,
    gath,
    rows_all,
    pair_send,
    pair_recv,
    curve_send,
    curve_recv,
    curve_mine,
    curve_all,
    inv_keep,
    nat_far,
    in_sem,
    part_ssem,
    part_rsem,
    case_ssem,
    case_rsem,
):
    parts, npy, nq, depth, width, chunks = sizes
    my_x, my_y, my_c = lax.axis_index("px"), lax.axis_index("py"), lax.axis_index("case")
    me = my_x * npy + my_y

    def part_id(step):
        other = lax.rem(me + step + parts, parts)
        return (other // npy, lax.rem(other, npy), my_c)

    def case_to(step):
        if nq == 4:
            other = my_c + (step % 2) * (1 - 2 * lax.rem(my_c, 2))
            return other + (step // 2) * (2 - 4 * (my_c // 2))
        return lax.rem(my_c + step, nq)

    def case_from(step):
        return case_to(step) if nq == 4 else lax.rem(my_c + nq - step, nq)

    def case_id(step):
        return (my_x, my_y, case_to(step))

    direct = (1, 2) if nq == 4 else tuple(range(1, nq))

    barrier = pltpu.get_barrier_semaphore()

    def greet_part(i, _):
        pl.semaphore_signal(barrier, inc=1, device_id=part_id(i), device_id_type=MESH)
        return 0

    lax.fori_loop(1, parts, greet_part, 0)
    for i in range(1, nq):
        pl.semaphore_signal(barrier, inc=1, device_id=case_id(i), device_id_type=MESH)

    inputs = (
        (near_hbm, near_ref),
        (owner_hbm, owner_ref),
        (far_hbm, far_ref),
        (kind_hbm, kind_ref),
        (stiff_hbm, stiff_ref),
        (binv_hbm, binv_ref),
        (bload_hbm, bload_ref),
        (coup_hbm, coup_ref),
        (pload_hbm, pload_ref),
        (pblock_hbm, pblock_ref),
    )
    fetches = [
        pltpu.make_async_copy(src, dst, in_sem.at[i]) for i, (src, dst) in enumerate(inputs)
    ]
    for fetch in fetches:
        fetch.start()

    kinds = binv_ref.shape[0]
    modes, ncase, ncomp = bload_ref.shape
    pd = pload_ref.shape[0]
    nport = pload_ref.shape[2]
    slots = parts * depth
    allcase = nq * ncase

    for fetch in fetches[0:5]:
        fetch.wait()
    kind_row = kind_ref[...]
    near_row = near_ref[...]
    owner_row = owner_ref[...]
    far_row = far_ref[...]

    def as_column(row):
        return jnp.broadcast_to(row.astype(F32), (ncomp, ncomp)).T

    sub = lax.broadcasted_iota(jnp.int32, (ncomp, ncomp), 0)
    lane = lax.broadcasted_iota(jnp.int32, (ncomp, ncomp), 1)
    same = (as_column(owner_row) == owner_row.astype(F32)) & (sub < lane)
    rank = jnp.sum(jnp.where(same, 1.0, 0.0), axis=0, keepdims=True).astype(jnp.int32)
    step_row = lax.rem(owner_row - me + parts, parts)
    slot_row = step_row * depth + rank
    slot_sub = lax.broadcasted_iota(jnp.int32, (slots, ncomp), 0)
    slot_pick = jnp.where(slot_sub == slot_row, 1.0, 0.0).astype(BF16)
    step_sub = lax.broadcasted_iota(jnp.int32, (parts, ncomp), 0)
    naming = jnp.concatenate(
        [
            jnp.where(step_sub == step_row, row, 0.0)
            for row in ((far_row + 1).astype(F32), kind_row.astype(F32), stiff_ref[...])
        ],
        axis=0,
    )
    ranked = jnp.where(sub == rank, 1.0, 0.0)
    wanted = exact(naming, ranked, NT)
    wanted = jnp.concatenate([wanted[r * parts:(r + 1) * parts] for r in range(3)], axis=1)
    wanted = wanted.reshape(parts, 1, 3 * ncomp)
    ask_send[...] = wanted
    ask_recv[0] = wanted[0]
    near_in = jnp.where(sub == near_row, 1.0, 0.0).astype(BF16)
    near_out = jnp.where(lane.astype(F32) == as_column(near_row), 1.0, 0.0).astype(BF16)
    near_slots = lax.dot_general(slot_pick, near_in, NT, preferred_element_type=F32).astype(BF16)

    order = sorted(range(1, parts), key=lambda i: -min(i % npy, npy - i % npy))

    def send_parts(src, dst, e, sign):
        def body(i, _):
            pltpu.make_async_remote_copy(
                src_ref=src(i),
                dst_ref=dst(i),
                send_sem=part_ssem.at[e],
                recv_sem=part_rsem.at[e],
                device_id=part_id(i if sign > 0 else -i),
                device_id_type=MESH,
            ).start()
            return 0

        if parts <= 8:
            for i in order:
                body(i, 0)
        else:
            lax.fori_loop(1, parts, body, 0)

    def wait_on(ref, sem):
        pltpu.make_async_copy(ref, ref, sem).wait()

    rest = pl.ds(1, parts - 1)

    def tile_cases(row):
        return jnp.concatenate([row] * ncase, axis=1)

    def kind_masks(row):
        row = tile_cases(row)
        return [jnp.where(row == t, 1.0, 0.0).astype(BF16) for t in range(kinds)]

    masks = kind_masks(kind_row)

    def table(parts_of):
        top, low = split(parts_of)
        return top, jnp.concatenate([top, low], axis=0)

    def apply_tables(tab, x, masks):
        top, low = split(x)
        lanes = x.shape[1]
        xt = jnp.concatenate([top * m[:, :lanes] for m in masks], axis=0)
        xl = jnp.concatenate([low * m[:, :lanes] for m in masks], axis=0)
        lead = mm(tab[1], xt)
        rows = tab[0].shape[0]
        return lead[:rows] + lead[rows:] + mm(tab[0], xl)

    def wide(field, rows):
        return jnp.concatenate(
            [field[k * rows:(k + 1) * rows] for k in range(field.shape[0] // rows)], axis=1
        )

    def tall(x, count):
        return jnp.concatenate(
            [x[:, k * count:(k + 1) * count] for k in range(x.shape[1] // count)], axis=0
        )

    def pick(x, onehot):
        top, low = split(x)
        return mm(jnp.concatenate([top, low], axis=1), jnp.concatenate([onehot, onehot], axis=0))

    def at_slots(onehot, x):
        top, low = split(x)
        return lax.dot_general(
            jnp.concatenate([onehot, onehot], axis=1),
            jnp.concatenate([top, low], axis=1),
            NT,
            preferred_element_type=F32,
        )

    def place(x, onehot):
        top, low = split(x)
        return mm(top, onehot) + mm(low, onehot)

    def take_far(e, j):
        wait_on(far_recv.at[e, j, rest], part_rsem.at[3 + e * chunks + j])
        return far_recv[e, j].reshape(slots, width).T

    def post(e, j, out, sign):
        far_send[e, j] = out
        far_recv[e, j, 0] = out[0]
        send_parts(
            lambda i: far_send.at[e, j, i], lambda i: far_recv.at[e, j, i], 3 + e * chunks + j, sign
        )

    def send_case(f, src, dst, sem, step):
        pltpu.make_async_remote_copy(
            src_ref=src,
            dst_ref=dst,
            send_sem=case_ssem.at[f, sem],
            recv_sem=case_rsem.at[f, sem],
            device_id=case_id(step),
            device_id_type=MESH,
        ).start()

    def publish(f, field):
        for k in range(ncase):
            gath[f, my_c, :, k, :] = field[k * pd:(k + 1) * pd]
        for i in reversed(direct):
            send_case(f, gath.at[f, my_c], gath.at[f, my_c], i, i)

    def forward(f):
        if nq == 4:
            block = gath.at[f, case_from(2)]
            wait_on(block, case_rsem.at[f, 2])
            send_case(f, block, block, 3, 1)

    def collect(f):
        for i in range(1, nq):
            if nq != 4 or i != 2:
                wait_on(gath.at[f, case_from(i)], case_rsem.at[f, i])

        def body(d, _):
            cols = pl.ds(pl.multiple_of(d * nport, nport), nport)
            for q in range(nq):
                rows_all[pl.ds(f * allcase + q * ncase, ncase), cols] = gath[f, q, d]
            return 0

        lax.fori_loop(0, pd, body, 0, unroll=4)

    def field_rows(f, count=1):
        return rows_all[f * allcase:(f + count) * allcase, :]

    def start_gram(value):
        folded = jnp.concatenate(
            [value[8 * r:8 * r + 8] for r in range(value.shape[0] // 8)], axis=1
        )
        pair_send[...] = folded
        pair_recv[0] = folded
        send_parts(lambda i: pair_send, lambda i: pair_recv.at[i], 1, 1)

    def finish_gram():
        wait_on(pair_recv.at[rest], part_rsem.at[1])
        total = jnp.sum(pair_recv[...], axis=0)
        return jnp.concatenate(
            [total[:, allcase * r:allcase * (r + 1)] for r in range(total.shape[1] // allcase)],
            axis=0,
        )

    def sym(g):
        return 0.5 * (g + g.T)

    def part(x, j):
        return x[j * width:(j + 1) * width]

    for fetch in fetches[5:8]:
        fetch.wait()
    inv_tab = table(jnp.concatenate([binv_ref[t] for t in range(kinds)], axis=1))
    coup_tab = table(jnp.concatenate([coup_ref[t].T for t in range(kinds)], axis=1))
    loads = jnp.concatenate([bload_ref[:, k, :] for k in range(ncase)], axis=1)
    lifted = apply_tables(inv_tab, loads, masks)
    inv_keep[...] = lifted
    condensed = -apply_tables(coup_tab, lifted, masks)
    leaving = tall(condensed[pd:], ncomp)
    pl.semaphore_wait(barrier, parts - 1 + nq - 1)
    send_parts(lambda i: ask_send.at[i], lambda i: ask_recv.at[i], 0, 1)
    for j in range(chunks):
        post(0, j, at_slots(slot_pick, part(leaving, j)).reshape(parts, depth, width), 1)
    for fetch in fetches[8:]:
        fetch.wait()
    stiff = tile_cases(stiff_ref[...])
    red_t = [exact(binv_ref[t], coup_ref[t], TN) for t in range(kinds)]
    schur = [pblock_ref[t] - exact(red_t[t], coup_ref[t], TN) for t in range(kinds)]
    schur = jnp.concatenate(schur, axis=1)
    near_tab, far_tab = table(schur[:pd]), table(schur[pd:])
    red_tab = table(jnp.concatenate(red_t, axis=1))
    own = jnp.concatenate([pload_ref[:, k, :] for k in range(ncase)], axis=0)
    own = own + pick(tall(condensed[:pd], ncomp), near_out)
    wait_on(ask_recv.at[rest], part_rsem.at[0])
    asked = ask_recv[...].reshape(parts, 3 * ncomp)
    ports = jnp.concatenate([asked[:, 0:ncomp]] * (ncomp // parts), axis=0).T
    port_lane = lax.broadcasted_iota(jnp.int32, (depth, nport), 1).astype(F32)
    asked_pick = jnp.concatenate(
        [jnp.where(ports[0:depth, i:i + 1] - 1.0 == port_lane, 1.0, 0.0) for i in range(parts)],
        axis=0,
    ).astype(BF16)

    def slot_line(r):
        return jnp.concatenate(
            [asked[i:i + 1, r * ncomp:r * ncomp + depth] for i in range(parts)], axis=1
        )

    slot_masks = kind_masks(slot_line(1))
    slot_stiff = tile_cases(slot_line(2))
    both_picks = jnp.concatenate([asked_pick, near_slots], axis=0)

    def scatter(e, j, piece):
        out = at_slots(both_picks, piece)
        post(e, j, out[:slots].reshape(parts, depth, width), -1)
        post(e + 1, j, out[slots:].reshape(parts, depth, width), 1)

    def join(a, b):
        return b if a is None else jnp.concatenate([a, b], axis=0)

    def operate(e, field, onward, between):
        near = pick(field, near_in)
        cuts = [0] + [((j + 1) * width) // pd for j in range(chunks)]
        far, far_at, near_at, image, have, sent = None, None, None, None, 0, 0
        for a, b in zip(cuts[:-1], cuts[1:]):
            if b == ncase:
                between()
            while have * width < b * pd:
                far = join(far, place(take_far(e, have), slot_pick))
                far_at = join(far_at, far_send[e, have].reshape(slots, width).T)
                near_at = join(near_at, take_far(e + 1, have))
                have += 1
            rows = slice(a * pd, b * pd)
            ends = jnp.concatenate([wide(near[rows], pd), wide(far[rows], pd)], axis=0)
            y = apply_tables(near_tab, ends, masks) * stiff[:, a * ncomp:b * ncomp]
            done = pick(tall(y, ncomp), near_out)
            ends = jnp.concatenate([wide(near_at[rows], pd), wide(far_at[rows], pd)], axis=0)
            y = apply_tables(far_tab, ends, slot_masks) * slot_stiff[:, a * slots:b * slots]
            image = join(image, done + place(tall(y, slots), asked_pick))
            while onward and (sent + 1) * width <= b * pd:
                scatter(e + 2, sent, part(image, sent))
                sent += 1
        return far, image

    base = None
    for j in range(chunks):
        piece = part(own, j) + place(take_far(0, j), asked_pick)
        scatter(1, j, piece)
        base = join(base, piece)
    publish(0, base)
    far_base, first = operate(1, base, True, lambda: forward(0))
    publish(1, first)
    publish(3, far_base)

    def grams_of_two():
        forward(1)
        collect(0)
        collect(1)
        pair = field_rows(0, 2)
        square = exact(pair, pair, NT)
        start_gram(
            jnp.concatenate(
                [
                    square[0:allcase, 0:allcase],
                    square[0:allcase, allcase:],
                    square[allcase:, allcase:],
                ],
                axis=0,
            )
        )
        forward(3)

    far_first, second = operate(3, first, False, grams_of_two)
    publish(4, far_first)
    publish(2, second)
    second_rows = jnp.concatenate([gath[2, my_c, d] for d in range(pd)], axis=1)

    n = allcase
    curve = exact(second_rows, field_rows(1), NT)
    curve = jnp.concatenate([curve, jnp.zeros((ncase, 128 - n), F32)], axis=1)
    curve_send[...] = curve
    curve_recv[0] = curve
    send_parts(lambda i: curve_send, lambda i: curve_recv.at[i], 2, 1)

    grams = finish_gram()
    g00 = sym(grams[0:n])
    g01 = sym(grams[n:2 * n])
    g11 = sym(grams[2 * n:3 * n])
    both = gauss_solve(g01, jnp.concatenate([g00, g11], axis=1))
    image_both = exact(g11, both)
    mine = jnp.where(
        lax.broadcasted_iota(jnp.int32, (n, ncase), 0)
        == lax.broadcasted_iota(jnp.int32, (n, ncase), 1) + my_c * ncase,
        1.0,
        0.0,
    )
    chosen = exact(jnp.concatenate([image_both[:, 0:n] - g01, both[:, 0:n]], axis=0), mine)

    forward(4)
    wait_on(curve_recv.at[rest], part_rsem.at[2])
    total = jnp.sum(curve_recv[...], axis=0)
    curve_mine[...] = total
    curve_all[my_c] = total
    for i in range(1, nq):
        send_case(5, curve_mine, curve_all.at[my_c], i, i)
    collect(3)
    forward(2)
    for i in range(1, nq):
        wait_on(curve_all.at[case_from(i)], case_rsem.at[5, i])
    g12 = curve_all[...].reshape(n, 128)[:, 0:n]
    beta = gauss_solve(sym(g12) - sym(image_both[:, n:2 * n]), chosen[0:n])
    alpha = chosen[n:2 * n] + exact(both[:, n:2 * n], beta)
    coefs = jnp.concatenate([alpha, -beta], axis=0).T
    ctop, clow = split(coefs)
    stack = jnp.concatenate([ctop, clow], axis=0)

    def mix(f):
        vtop, vlow = split(field_rows(f, 2))
        lead = mm(stack, vtop)
        return lead[0:ncase] + lead[ncase:] + mm(ctop, vlow)

    answer_rows = mix(0)
    for d in range(pd):
        sol_ref[d] = answer_rows[:, d * nport:(d + 1) * nport]
    collect(4)
    far_rows = mix(3)
    for d in range(pd):
        nat_far[d] = far_rows[:, d * nport:(d + 1) * nport]
    answer = jnp.concatenate([sol_ref[:, k, :] for k in range(ncase)], axis=0)
    near = wide(pick(answer, near_in), pd)
    ends = jnp.concatenate(
        [near, jnp.concatenate([nat_far[:, k, :] for k in range(ncase)], axis=1)], axis=0
    )
    scaled = inv_keep[...] / stiff
    back = scaled - apply_tables(red_tab, ends, masks)
    for k in range(ncase):
        bub_ref[:, k, :] = back[:, k * ncomp:(k + 1) * ncomp]
    collect(2)
    drop_rows = mix(1)
    for d in range(pd):
        res_ref[d] = gath[0, my_c, d] - drop_rows[:, d * nport:(d + 1) * nport]

    wait_on(ask_send.at[rest], part_ssem.at[0])
    for e in range(5):
        for j in range(chunks):
            wait_on(far_send.at[e, j, rest], part_ssem.at[3 + e * chunks + j])
    wait_on(pair_recv.at[rest], part_ssem.at[1])
    wait_on(curve_recv.at[rest], part_ssem.at[2])
    for f in range(5):
        for i in range(1, nq):
            wait_on(gath.at[f, my_c], case_ssem.at[f, i])
    for i in range(1, nq):
        wait_on(curve_mine, case_ssem.at[5, i])


def emit(*refs):
    count = len(refs) // 2
    sems = refs[-1]
    copies = [
        pltpu.make_async_copy(refs[i], refs[count + i], sems.at[i]) for i in range(count)
    ]
    for copy in copies:
        copy.start()
    for copy in copies:
        copy.wait()


def local(
    comp_type,
    stiffness,
    near_port,
    far_owner,
    far_port,
    bubble_load,
    port_load,
    bubble_inverse,
    coupling,
    port_block,
):
    npy = lax.axis_size("py")
    parts = lax.axis_size("px") * npy
    nq = lax.axis_size("case")
    ncomp = comp_type.shape[0]
    modes, ncase, _ = bubble_load.shape
    pd, _, nport = port_load.shape
    kinds = bubble_inverse.shape[0]
    cap = 3 * ncomp // (2 * parts)
    depth = -(-cap // 8) * 8
    allcase = nq * ncase
    width = 128 if (ncase * pd) % 128 == 0 else ncase * pd
    chunks = ncase * pd // width
    vmem = pl.BlockSpec(memory_space=pltpu.VMEM)
    hbm = pl.BlockSpec(memory_space=pltpu.HBM)

    def body(*refs):
        kernel((parts, npy, nq, depth, width, chunks), *refs)

    shapes = (
        jax.ShapeDtypeStruct(port_load.shape, F32),
        jax.ShapeDtypeStruct(port_load.shape, F32),
        jax.ShapeDtypeStruct(bubble_load.shape, F32),
    )
    results = pl.pallas_call(
        body,
        out_shape=shapes,
        in_specs=[hbm] * 10,
        out_specs=(vmem, vmem, vmem),
        scratch_shapes=[
            pltpu.VMEM((1, ncomp), jnp.int32),
            pltpu.VMEM((1, ncomp), jnp.int32),
            pltpu.VMEM((1, ncomp), jnp.int32),
            pltpu.VMEM((1, ncomp), jnp.int32),
            pltpu.VMEM((1, ncomp), F32),
            pltpu.VMEM(bubble_load.shape, F32),
            pltpu.VMEM(port_load.shape, F32),
            pltpu.VMEM(bubble_inverse.shape, F32),
            pltpu.VMEM((kinds, modes, 2 * pd), F32),
            pltpu.VMEM(port_block.shape, F32),
            pltpu.VMEM((parts, 1, 3 * ncomp), F32),
            pltpu.VMEM((parts, 1, 3 * ncomp), F32),
            pltpu.VMEM((5, chunks, parts, depth, width), F32),
            pltpu.VMEM((5, chunks, parts, depth, width), F32),
            pltpu.VMEM((5, nq, pd, ncase, nport), F32),
            pltpu.VMEM((5 * allcase, pd * nport), F32),
            pltpu.VMEM((8, 3 * allcase * allcase // 8), F32),
            pltpu.VMEM((parts, 8, 3 * allcase * allcase // 8), F32),
            pltpu.VMEM((ncase, 128), F32),
            pltpu.VMEM((parts, ncase, 128), F32),
            pltpu.VMEM((ncase, 128), F32),
            pltpu.VMEM((nq, ncase, 128), F32),
            pltpu.VMEM((modes, ncase * ncomp), F32),
            pltpu.VMEM((pd, ncase, nport), F32),
            pltpu.SemaphoreType.DMA((10,)),
            pltpu.SemaphoreType.DMA((3 + 5 * chunks,)),
            pltpu.SemaphoreType.DMA((3 + 5 * chunks,)),
            pltpu.SemaphoreType.DMA((6, nq)),
            pltpu.SemaphoreType.DMA((6, nq)),
        ],
        compiler_params=pltpu.CompilerParams(
            collective_id=0, has_side_effects=True, vmem_limit_bytes=32 * 1024 * 1024
        ),
        name="condensed_solve",
    )(
        *(
            pltpu.with_memory_space_constraint(x, pltpu.HBM)
            for x in (
                comp_type.reshape(1, ncomp),
                near_port.reshape(1, ncomp),
                far_owner.reshape(1, ncomp),
                far_port.reshape(1, ncomp),
                stiffness.reshape(1, ncomp),
                bubble_load,
                port_load,
                bubble_inverse,
                jnp.swapaxes(coupling, 1, 2),
                port_block,
            )
        )
    )
    return pl.pallas_call(
        emit,
        out_shape=shapes,
        in_specs=[vmem] * 3,
        out_specs=(hbm, hbm, hbm),
        scratch_shapes=[pltpu.SemaphoreType.DMA((3,))],
        compiler_params=pltpu.CompilerParams(vmem_limit_bytes=4 * 1024 * 1024),
        name="emit",
    )(*results)


def solution(mesh):
    placed = (
        P(("px", "py")),
        P(("px", "py")),
        P(("px", "py")),
        P(("px", "py"), None),
        P(("px", "py")),
        P(None, "case", ("px", "py")),
        P(None, "case", ("px", "py")),
        P(),
        P(),
        P(),
    )
    return jax.shard_map(
        local,
        mesh=mesh,
        in_specs=placed,
        out_specs=(
            P(None, "case", ("px", "py")),
            P(None, "case", ("px", "py")),
            P(None, "case", ("px", "py")),
        ),
        check_vma=False,
    )
```

```python
import jax
import jax.numpy as jnp
from jax import lax
from jax.experimental import pallas as pl
from jax.experimental.pallas import tpu as pltpu
from jax.sharding import PartitionSpec as P

HIGH = lax.Precision.HIGHEST
F32 = jnp.float32
BF16 = jnp.bfloat16
MESH = pl.DeviceIdType.MESH
NT = (((1,), (1,)), ((), ()))
TN = (((0,), (0,)), ((), ()))


def split(x):
    top = x.astype(BF16)
    return top, (x - top.astype(F32)).astype(BF16)


def mm(a, b):
    return jnp.dot(a, b, preferred_element_type=F32)


def exact(a, b, dims=(((1,), (0,)), ((), ()))):
    return lax.dot_general(a, b, dims, precision=HIGH, preferred_element_type=F32)


def gauss_solve(matrix, target):
    n = matrix.shape[0]
    aug = jnp.concatenate([matrix, target], axis=1)
    rows = lax.broadcasted_iota(jnp.int32, aug.shape, 0)
    for j in range(0, n, 2):
        row0, row1 = aug[j:j + 1, :], aug[j + 1:j + 2, :]
        col0 = jnp.broadcast_to(aug[:, j:j + 1], aug.shape)
        col1 = jnp.broadcast_to(aug[:, j + 1:j + 2], aug.shape)
        a, c = col0[j:j + 1, :], col0[j + 1:j + 2, :]
        b, d = col1[j:j + 1, :], col1[j + 1:j + 2, :]
        scale = 1.0 / (a * d - b * c)
        new0 = (d * row0 - b * row1) * scale
        new1 = (a * row1 - c * row0) * scale
        rest = aug - col0 * new0 - col1 * new1
        aug = jnp.where(rows == j, new0, jnp.where(rows == j + 1, new1, rest))
    return aug[:, n:]


def kernel(
    sizes,
    kind_hbm,
    near_hbm,
    owner_hbm,
    far_hbm,
    stiff_hbm,
    bload_hbm,
    pload_hbm,
    binv_hbm,
    coup_hbm,
    pblock_hbm,
    sol_ref,
    res_ref,
    bub_ref,
    kind_ref,
    near_ref,
    owner_ref,
    far_ref,
    stiff_ref,
    bload_ref,
    pload_ref,
    binv_ref,
    coup_ref,
    pblock_ref,
    ask_send,
    ask_recv,
    far_send,
    far_recv,
    gath,
    bent_rows,
    rows_all,
    block_mine,
    block_case,
    pair_send,
    pair_recv,
    inv_keep,
    nat_far,
    in_sem,
    part_ssem,
    part_rsem,
    case_ssem,
    case_rsem,
):
    parts, npy, nq, depth, width, chunks = sizes
    my_x, my_y, my_c = lax.axis_index("px"), lax.axis_index("py"), lax.axis_index("case")
    me = my_x * npy + my_y

    def part_id(step):
        other = lax.rem(me + step + parts, parts)
        return (other // npy, lax.rem(other, npy), my_c)

    def case_to(step):
        if nq == 4:
            other = my_c + (step % 2) * (1 - 2 * lax.rem(my_c, 2))
            return other + (step // 2) * (2 - 4 * (my_c // 2))
        return lax.rem(my_c + step, nq)

    def case_from(step):
        return case_to(step) if nq == 4 else lax.rem(my_c + nq - step, nq)

    def case_id(step):
        return (my_x, my_y, case_to(step))

    direct = (1, 2) if nq == 4 else tuple(range(1, nq))

    barrier = pltpu.get_barrier_semaphore()

    def greet_part(i, _):
        pl.semaphore_signal(barrier, inc=1, device_id=part_id(i), device_id_type=MESH)
        return 0

    lax.fori_loop(1, parts, greet_part, 0)
    for i in range(1, nq):
        pl.semaphore_signal(barrier, inc=1, device_id=case_id(i), device_id_type=MESH)

    inputs = (
        (near_hbm, near_ref),
        (owner_hbm, owner_ref),
        (far_hbm, far_ref),
        (kind_hbm, kind_ref),
        (stiff_hbm, stiff_ref),
        (binv_hbm, binv_ref),
        (bload_hbm, bload_ref),
        (coup_hbm, coup_ref),
        (pload_hbm, pload_ref),
        (pblock_hbm, pblock_ref),
    )
    fetches = [
        pltpu.make_async_copy(src, dst, in_sem.at[i]) for i, (src, dst) in enumerate(inputs)
    ]
    for fetch in fetches:
        fetch.start()

    kinds = binv_ref.shape[0]
    modes, ncase, ncomp = bload_ref.shape
    pd = pload_ref.shape[0]
    nport = pload_ref.shape[2]
    slots = parts * depth
    allcase = nq * ncase

    for fetch in fetches[0:5]:
        fetch.wait()
    kind_row = kind_ref[...]
    near_row = near_ref[...]
    owner_row = owner_ref[...]
    far_row = far_ref[...]

    def as_column(row):
        return jnp.broadcast_to(row.astype(F32), (ncomp, ncomp)).T

    sub = lax.broadcasted_iota(jnp.int32, (ncomp, ncomp), 0)
    lane = lax.broadcasted_iota(jnp.int32, (ncomp, ncomp), 1)
    same = (as_column(owner_row) == owner_row.astype(F32)) & (sub < lane)
    rank = jnp.sum(jnp.where(same, 1.0, 0.0), axis=0, keepdims=True).astype(jnp.int32)
    step_row = lax.rem(owner_row - me + parts, parts)
    slot_row = step_row * depth + rank
    slot_sub = lax.broadcasted_iota(jnp.int32, (slots, ncomp), 0)
    slot_pick = jnp.where(slot_sub == slot_row, 1.0, 0.0).astype(BF16)
    step_sub = lax.broadcasted_iota(jnp.int32, (parts, ncomp), 0)
    naming = jnp.concatenate(
        [
            jnp.where(step_sub == step_row, row, 0.0)
            for row in ((far_row + 1).astype(F32), kind_row.astype(F32), stiff_ref[...])
        ],
        axis=0,
    )
    ranked = jnp.where(sub == rank, 1.0, 0.0)
    wanted = exact(naming, ranked, NT)
    wanted = jnp.concatenate([wanted[r * parts:(r + 1) * parts] for r in range(3)], axis=1)
    wanted = wanted.reshape(parts, 1, 3 * ncomp)
    ask_send[...] = wanted
    ask_recv[0] = wanted[0]
    near_in = jnp.where(sub == near_row, 1.0, 0.0).astype(BF16)
    near_out = jnp.where(lane.astype(F32) == as_column(near_row), 1.0, 0.0).astype(BF16)
    near_slots = lax.dot_general(slot_pick, near_in, NT, preferred_element_type=F32).astype(BF16)

    order = sorted(range(1, parts), key=lambda i: -min(i % npy, npy - i % npy))

    def send_parts(src, dst, e, sign):
        def body(i, _):
            pltpu.make_async_remote_copy(
                src_ref=src(i),
                dst_ref=dst(i),
                send_sem=part_ssem.at[e],
                recv_sem=part_rsem.at[e],
                device_id=part_id(i if sign > 0 else -i),
                device_id_type=MESH,
            ).start()
            return 0

        if parts <= 8:
            for i in order:
                body(i, 0)
        else:
            lax.fori_loop(1, parts, body, 0)

    def wait_on(ref, sem):
        pltpu.make_async_copy(ref, ref, sem).wait()

    rest = pl.ds(1, parts - 1)

    def tile_cases(row):
        return jnp.concatenate([row] * ncase, axis=1)

    def kind_masks(row):
        row = tile_cases(row)
        return [jnp.where(row == t, 1.0, 0.0).astype(BF16) for t in range(kinds)]

    masks = kind_masks(kind_row)

    def table(parts_of):
        top, low = split(parts_of)
        return top, jnp.concatenate([top, low], axis=0)

    def apply_tables(tab, x, masks):
        top, low = split(x)
        lanes = x.shape[1]
        xt = jnp.concatenate([top * m[:, :lanes] for m in masks], axis=0)
        xl = jnp.concatenate([low * m[:, :lanes] for m in masks], axis=0)
        lead = mm(tab[1], xt)
        rows = tab[0].shape[0]
        return lead[:rows] + lead[rows:] + mm(tab[0], xl)

    def wide(field, rows):
        return jnp.concatenate(
            [field[k * rows:(k + 1) * rows] for k in range(field.shape[0] // rows)], axis=1
        )

    def tall(x, count):
        return jnp.concatenate(
            [x[:, k * count:(k + 1) * count] for k in range(x.shape[1] // count)], axis=0
        )

    def pick(x, onehot):
        top, low = split(x)
        return mm(jnp.concatenate([top, low], axis=1), jnp.concatenate([onehot, onehot], axis=0))

    def at_slots(onehot, x):
        top, low = split(x)
        return lax.dot_general(
            jnp.concatenate([onehot, onehot], axis=1),
            jnp.concatenate([top, low], axis=1),
            NT,
            preferred_element_type=F32,
        )

    def place(x, onehot):
        top, low = split(x)
        return mm(top, onehot) + mm(low, onehot)

    def take(e, j):
        wait_on(far_recv.at[e, j, rest], part_rsem.at[3 + e * chunks + j])
        return far_recv[e, j].reshape(slots, width).T

    def post(e, j, out, sign):
        far_send[e, j] = out
        far_recv[e, j, 0] = out[0]
        send_parts(
            lambda i: far_send.at[e, j, i], lambda i: far_recv.at[e, j, i], 3 + e * chunks + j, sign
        )

    def send_case(f, src, dst, sem, step):
        pltpu.make_async_remote_copy(
            src_ref=src,
            dst_ref=dst,
            send_sem=case_ssem.at[f, sem],
            recv_sem=case_rsem.at[f, sem],
            device_id=case_id(step),
            device_id_type=MESH,
        ).start()

    def publish(f, field):
        for k in range(ncase):
            gath[f, my_c, :, k, :] = field[k * pd:(k + 1) * pd]
        for i in reversed(direct):
            send_case(f, gath.at[f, my_c], gath.at[f, my_c], i, i)

    def forward(f):
        if nq == 4:
            block = gath.at[f, case_from(2)]
            wait_on(block, case_rsem.at[f, 2])
            send_case(f, block, block, 3, 1)

    def collect(f):
        for i in range(1, nq):
            if nq != 4 or i != 2:
                wait_on(gath.at[f, case_from(i)], case_rsem.at[f, i])

        def body(d, _):
            cols = pl.ds(pl.multiple_of(d * nport, nport), nport)
            for q in range(nq):
                rows_all[pl.ds(f * allcase + q * ncase, ncase), cols] = gath[f, q, d]
            return 0

        lax.fori_loop(0, pd, body, 0, unroll=4)

    def field_rows(f, count=1):
        return rows_all[f * allcase:(f + count) * allcase, :]

    def own_rows(f):
        return jnp.concatenate([gath[f, my_c, d] for d in range(pd)], axis=1)

    def gram_out(s, block):
        block = jnp.concatenate([block, jnp.zeros((2 * ncase, 128 - allcase), F32)], axis=1)
        block_mine[s] = block
        block_case[s, my_c] = block
        for i in range(1, nq):
            send_case(5 + s, block_mine.at[s], block_case.at[s, my_c], i, i)

    def gram_on(s):
        for i in range(1, nq):
            wait_on(block_case.at[s, case_from(i)], case_rsem.at[5 + s, i])
        line = jnp.concatenate([block_case[s, q][:, 0:allcase] for q in range(nq)], axis=1)
        pair_send[s] = line
        pair_recv[s, 0] = line
        send_parts(lambda i: pair_send.at[s], lambda i: pair_recv.at[s, i], 1 + s, 1)

    def gram_in(s):
        wait_on(pair_recv.at[s, rest], part_rsem.at[1 + s])
        total = jnp.sum(pair_recv[s], axis=0)
        grams = []
        for r in range(2):
            rows = total[r * ncase:(r + 1) * ncase]
            grams.append(
                sym(
                    jnp.concatenate(
                        [rows[:, q * allcase:(q + 1) * allcase] for q in range(nq)], axis=0
                    )
                )
            )
        return grams

    def sym(g):
        return 0.5 * (g + g.T)

    def part(x, j):
        return x[j * width:(j + 1) * width]

    for fetch in fetches[5:8]:
        fetch.wait()
    inv_tab = table(jnp.concatenate([binv_ref[t] for t in range(kinds)], axis=1))
    coup_tab = table(jnp.concatenate([coup_ref[t].T for t in range(kinds)], axis=1))
    loads = jnp.concatenate([bload_ref[:, k, :] for k in range(ncase)], axis=1)
    lifted = apply_tables(inv_tab, loads, masks)
    inv_keep[...] = lifted
    condensed = -apply_tables(coup_tab, lifted, masks)
    leaving = tall(condensed[pd:], ncomp)
    pl.semaphore_wait(barrier, parts - 1 + nq - 1)
    send_parts(lambda i: ask_send.at[i], lambda i: ask_recv.at[i], 0, 1)
    for j in range(chunks):
        post(0, j, at_slots(slot_pick, part(leaving, j)).reshape(parts, depth, width), 1)
    for fetch in fetches[8:]:
        fetch.wait()
    stiff = tile_cases(stiff_ref[...])
    red_t = [exact(binv_ref[t], coup_ref[t], TN) for t in range(kinds)]
    schur = [pblock_ref[t] - exact(red_t[t], coup_ref[t], TN) for t in range(kinds)]

    def corner(a, b):
        rows, cols = slice(a * pd, (a + 1) * pd), slice(b * pd, (b + 1) * pd)
        return table(jnp.concatenate([schur[t][rows, cols] for t in range(kinds)], axis=1))

    nn_tab, nf_tab, fn_tab, ff_tab = corner(0, 0), corner(0, 1), corner(1, 0), corner(1, 1)
    red_tab = table(jnp.concatenate(red_t, axis=1))
    own = jnp.concatenate([pload_ref[:, k, :] for k in range(ncase)], axis=0)
    own = own + pick(tall(condensed[:pd], ncomp), near_out)
    wait_on(ask_recv.at[rest], part_rsem.at[0])
    asked = ask_recv[...].reshape(parts, 3 * ncomp)
    ports = jnp.concatenate([asked[:, 0:ncomp]] * (ncomp // parts), axis=0).T
    port_lane = lax.broadcasted_iota(jnp.int32, (depth, nport), 1).astype(F32)
    asked_pick = jnp.concatenate(
        [jnp.where(ports[0:depth, i:i + 1] - 1.0 == port_lane, 1.0, 0.0) for i in range(parts)],
        axis=0,
    ).astype(BF16)

    def slot_line(r):
        return jnp.concatenate(
            [asked[i:i + 1, r * ncomp:r * ncomp + depth] for i in range(parts)], axis=1
        )

    slot_masks = kind_masks(slot_line(1))
    slot_stiff = tile_cases(slot_line(2))
    both_picks = jnp.concatenate([asked_pick, near_slots], axis=0)

    def scatter(e, j, piece):
        out = at_slots(both_picks, piece)
        post(e, j, out[:slots].reshape(parts, depth, width), -1)
        return lambda: post(e + 1, j, out[slots:].reshape(parts, depth, width), 1)

    def join(a, b):
        return b if a is None else jnp.concatenate([a, b], axis=0)

    def near_side(tab, x, a, b):
        return apply_tables(tab, wide(x, pd), masks) * stiff[:, a * ncomp:b * ncomp]

    def far_side(tab, x, a, b):
        return apply_tables(tab, wide(x, pd), slot_masks) * slot_stiff[:, a * slots:b * slots]

    def near_ports(y):
        return pick(tall(y, ncomp), near_out)

    def far_ports(y):
        return place(tall(y, slots), asked_pick)

    def diagonal(e, field):
        y_near = near_side(nn_tab, pick(field, near_in), 0, ncase)
        far_at = [far_send[e, j].reshape(slots, width).T for j in range(chunks)]
        return y_near, far_side(ff_tab, jnp.concatenate(far_at, axis=0), 0, ncase)

    def take_far_values(e, j):
        return place(take(e, j), slot_pick)

    cuts = [0] + [((j + 1) * width) // pd for j in range(chunks)]

    base = None
    for j in range(chunks):
        piece = part(own, j) + place(take(0, j), asked_pick)
        scatter(1, j, piece)()
        base = join(base, piece)
    publish(0, base)

    y_near, y_far = diagonal(1, base)
    far_base, near_at, first, sent = None, None, None, 0
    for j in range(chunks):
        a, b = cuts[j], cuts[j + 1]
        if j == chunks - 1:
            forward(0)
        far_base = join(far_base, take_far_values(1, j))
        near_at = join(near_at, take(2, j))
        rows = slice(a * pd, b * pd)
        y = y_near[:, a * ncomp:b * ncomp] + near_side(nf_tab, far_base[rows], a, b)
        done = near_ports(y)
        y = y_far[:, a * slots:b * slots] + far_side(fn_tab, near_at[rows], a, b)
        first = join(first, done + far_ports(y))
        later = []
        while (sent + 1) * width <= b * pd:
            later.append(scatter(3, sent, part(first, sent)))
            sent += 1
        for post_near in later:
            post_near()
    publish(1, first)

    y_near, y_far = diagonal(3, first)
    straight = near_ports(y_near) + far_ports(y_far)
    collect(0)
    gram_out(0, exact(jnp.concatenate([own_rows(0), own_rows(1)], axis=0), field_rows(0), NT))
    publish(3, far_base)
    far_first, crossed = None, None
    for j in range(chunks):
        a, b = cuts[j], cuts[j + 1]
        if j == chunks - 1:
            gram_on(0)
        far_first = join(far_first, take_far_values(3, j))
        crossed = join(crossed, near_ports(near_side(nf_tab, far_first[a * pd:b * pd], a, b)))
        if j == 0:
            forward(1)
    collect(1)
    bent = straight + 2.0 * crossed
    for k in range(ncase):
        bent_rows[:, k, :] = bent[k * pd:(k + 1) * pd]
    lines = jnp.concatenate([bent_rows[d] for d in range(pd)], axis=1)
    gram_out(1, exact(jnp.concatenate([own_rows(1), lines], axis=0), field_rows(1), NT))
    publish(4, far_first)
    second, near_at = None, None
    for j in range(chunks):
        a, b = cuts[j], cuts[j + 1]
        if j == chunks - 1:
            forward(3)
            gram_on(1)
        near_at = join(near_at, take(4, j))
        second = join(second, far_ports(far_side(fn_tab, near_at[a * pd:b * pd], a, b)))
    second = second + straight + crossed
    publish(2, second)

    n = allcase
    g00, g01 = gram_in(0)
    eye = jnp.where(
        lax.broadcasted_iota(jnp.int32, (n, n), 0) == lax.broadcasted_iota(jnp.int32, (n, n), 1),
        1.0,
        0.0,
    )
    both = gauss_solve(g01, jnp.concatenate([g00, eye], axis=1))
    mine = jnp.where(
        lax.broadcasted_iota(jnp.int32, (n, ncase), 0)
        == lax.broadcasted_iota(jnp.int32, (n, ncase), 1) + my_c * ncase,
        1.0,
        0.0,
    )
    chosen = exact(jnp.concatenate([both[:, 0:n], g01], axis=0), mine)
    first_step, g01_mine, inverse = chosen[0:n], chosen[n:2 * n], both[:, n:2 * n]
    forward(4)
    collect(3)
    g11, g12 = gram_in(1)
    over = exact(inverse, g11)
    side = exact(g11, jnp.concatenate([over, first_step], axis=1))
    beta = gauss_solve(g12 - sym(side[:, 0:n]), side[:, n:] - g01_mine)
    alpha = first_step + exact(over, beta)
    coefs = jnp.concatenate([alpha, -beta], axis=0).T
    ctop, clow = split(coefs)
    stack = jnp.concatenate([ctop, clow], axis=0)

    def mix(f):
        vtop, vlow = split(field_rows(f, 2))
        lead = mm(stack, vtop)
        return lead[0:ncase] + lead[ncase:] + mm(ctop, vlow)

    answer_rows = mix(0)
    for d in range(pd):
        sol_ref[d] = answer_rows[:, d * nport:(d + 1) * nport]
    collect(4)
    forward(2)
    far_rows = mix(3)
    for d in range(pd):
        nat_far[d] = far_rows[:, d * nport:(d + 1) * nport]
    answer = jnp.concatenate([sol_ref[:, k, :] for k in range(ncase)], axis=0)
    near = wide(pick(answer, near_in), pd)
    ends = jnp.concatenate(
        [near, jnp.concatenate([nat_far[:, k, :] for k in range(ncase)], axis=1)], axis=0
    )
    scaled = inv_keep[...] / stiff
    back = scaled - apply_tables(red_tab, ends, masks)
    for k in range(ncase):
        bub_ref[:, k, :] = back[:, k * ncomp:(k + 1) * ncomp]
    collect(2)
    drop_rows = mix(1)
    for d in range(pd):
        res_ref[d] = gath[0, my_c, d] - drop_rows[:, d * nport:(d + 1) * nport]

    wait_on(ask_send.at[rest], part_ssem.at[0])
    for e in range(5):
        for j in range(chunks):
            wait_on(far_send.at[e, j, rest], part_ssem.at[3 + e * chunks + j])
    for s in range(2):
        wait_on(pair_recv.at[s, rest], part_ssem.at[1 + s])
    for f in range(5):
        for i in range(1, nq):
            wait_on(gath.at[f, my_c], case_ssem.at[f, i])
    for s in range(2):
        for i in range(1, nq):
            wait_on(block_mine.at[s], case_ssem.at[5 + s, i])


def emit(*refs):
    count = len(refs) // 2
    sems = refs[-1]
    copies = [
        pltpu.make_async_copy(refs[i], refs[count + i], sems.at[i]) for i in range(count)
    ]
    for copy in copies:
        copy.start()
    for copy in copies:
        copy.wait()


def local(
    comp_type,
    stiffness,
    near_port,
    far_owner,
    far_port,
    bubble_load,
    port_load,
    bubble_inverse,
    coupling,
    port_block,
):
    npy = lax.axis_size("py")
    parts = lax.axis_size("px") * npy
    nq = lax.axis_size("case")
    ncomp = comp_type.shape[0]
    modes, ncase, _ = bubble_load.shape
    pd, _, nport = port_load.shape
    kinds = bubble_inverse.shape[0]
    cap = 3 * ncomp // (2 * parts)
    depth = -(-cap // 8) * 8
    allcase = nq * ncase
    width = 128 if (ncase * pd) % 128 == 0 else ncase * pd
    chunks = ncase * pd // width
    vmem = pl.BlockSpec(memory_space=pltpu.VMEM)
    hbm = pl.BlockSpec(memory_space=pltpu.HBM)

    def body(*refs):
        kernel((parts, npy, nq, depth, width, chunks), *refs)

    shapes = (
        jax.ShapeDtypeStruct(port_load.shape, F32),
        jax.ShapeDtypeStruct(port_load.shape, F32),
        jax.ShapeDtypeStruct(bubble_load.shape, F32),
    )
    results = pl.pallas_call(
        body,
        out_shape=shapes,
        in_specs=[hbm] * 10,
        out_specs=(vmem, vmem, vmem),
        scratch_shapes=[
            pltpu.VMEM((1, ncomp), jnp.int32),
            pltpu.VMEM((1, ncomp), jnp.int32),
            pltpu.VMEM((1, ncomp), jnp.int32),
            pltpu.VMEM((1, ncomp), jnp.int32),
            pltpu.VMEM((1, ncomp), F32),
            pltpu.VMEM(bubble_load.shape, F32),
            pltpu.VMEM(port_load.shape, F32),
            pltpu.VMEM(bubble_inverse.shape, F32),
            pltpu.VMEM((kinds, modes, 2 * pd), F32),
            pltpu.VMEM(port_block.shape, F32),
            pltpu.VMEM((parts, 1, 3 * ncomp), F32),
            pltpu.VMEM((parts, 1, 3 * ncomp), F32),
            pltpu.VMEM((5, chunks, parts, depth, width), F32),
            pltpu.VMEM((5, chunks, parts, depth, width), F32),
            pltpu.VMEM((5, nq, pd, ncase, nport), F32),
            pltpu.VMEM((pd, ncase, nport), F32),
            pltpu.VMEM((5 * allcase, pd * nport), F32),
            pltpu.VMEM((2, 2 * ncase, 128), F32),
            pltpu.VMEM((2, nq, 2 * ncase, 128), F32),
            pltpu.VMEM((2, 2 * ncase, nq * allcase), F32),
            pltpu.VMEM((2, parts, 2 * ncase, nq * allcase), F32),
            pltpu.VMEM((modes, ncase * ncomp), F32),
            pltpu.VMEM((pd, ncase, nport), F32),
            pltpu.SemaphoreType.DMA((10,)),
            pltpu.SemaphoreType.DMA((3 + 5 * chunks,)),
            pltpu.SemaphoreType.DMA((3 + 5 * chunks,)),
            pltpu.SemaphoreType.DMA((7, nq)),
            pltpu.SemaphoreType.DMA((7, nq)),
        ],
        compiler_params=pltpu.CompilerParams(
            collective_id=0, has_side_effects=True, vmem_limit_bytes=32 * 1024 * 1024
        ),
        name="condensed_solve",
    )(
        *(
            pltpu.with_memory_space_constraint(x, pltpu.HBM)
            for x in (
                comp_type.reshape(1, ncomp),
                near_port.reshape(1, ncomp),
                far_owner.reshape(1, ncomp),
                far_port.reshape(1, ncomp),
                stiffness.reshape(1, ncomp),
                bubble_load,
                port_load,
                bubble_inverse,
                jnp.swapaxes(coupling, 1, 2),
                port_block,
            )
        )
    )
    return pl.pallas_call(
        emit,
        out_shape=shapes,
        in_specs=[vmem] * 3,
        out_specs=(hbm, hbm, hbm),
        scratch_shapes=[pltpu.SemaphoreType.DMA((3,))],
        compiler_params=pltpu.CompilerParams(vmem_limit_bytes=4 * 1024 * 1024),
        name="emit",
    )(*results)


def solution(mesh):
    placed = (
        P(("px", "py")),
        P(("px", "py")),
        P(("px", "py")),
        P(("px", "py"), None),
        P(("px", "py")),
        P(None, "case", ("px", "py")),
        P(None, "case", ("px", "py")),
        P(),
        P(),
        P(),
    )
    return jax.shard_map(
        local,
        mesh=mesh,
        in_specs=placed,
        out_specs=(
            P(None, "case", ("px", "py")),
            P(None, "case", ("px", "py")),
            P(None, "case", ("px", "py")),
        ),
        check_vma=False,
    )
```

```python
import jax
import jax.numpy as jnp
from jax import lax
from jax.experimental import pallas as pl
from jax.experimental.pallas import tpu as pltpu
from jax.sharding import PartitionSpec as P

HIGH = lax.Precision.HIGHEST
F32 = jnp.float32
BF16 = jnp.bfloat16
MESH = pl.DeviceIdType.MESH
NT = (((1,), (1,)), ((), ()))
TN = (((0,), (0,)), ((), ()))


def split(x):
    top = x.astype(BF16)
    return top, (x - top.astype(F32)).astype(BF16)


def mm(a, b):
    return jnp.dot(a, b, preferred_element_type=F32)


def exact(a, b, dims=(((1,), (0,)), ((), ()))):
    return lax.dot_general(a, b, dims, precision=HIGH, preferred_element_type=F32)


def gauss_solve(matrix, target):
    n = matrix.shape[0]
    aug = jnp.concatenate([matrix, target], axis=1)
    rows = lax.broadcasted_iota(jnp.int32, aug.shape, 0)
    for j in range(0, n, 2):
        row0, row1 = aug[j:j + 1, :], aug[j + 1:j + 2, :]
        col0 = jnp.broadcast_to(aug[:, j:j + 1], aug.shape)
        col1 = jnp.broadcast_to(aug[:, j + 1:j + 2], aug.shape)
        a, c = col0[j:j + 1, :], col0[j + 1:j + 2, :]
        b, d = col1[j:j + 1, :], col1[j + 1:j + 2, :]
        scale = 1.0 / (a * d - b * c)
        new0 = (d * row0 - b * row1) * scale
        new1 = (a * row1 - c * row0) * scale
        rest = aug - col0 * new0 - col1 * new1
        aug = jnp.where(rows == j, new0, jnp.where(rows == j + 1, new1, rest))
    return aug[:, n:]


def kernel(
    sizes,
    kind_hbm,
    near_hbm,
    owner_hbm,
    far_hbm,
    stiff_hbm,
    bload_hbm,
    pload_hbm,
    binv_hbm,
    coup_hbm,
    pblock_hbm,
    sol_ref,
    res_ref,
    bub_ref,
    kind_ref,
    near_ref,
    owner_ref,
    far_ref,
    stiff_ref,
    bload_ref,
    pload_ref,
    binv_ref,
    coup_ref,
    pblock_ref,
    ask_send,
    ask_recv,
    far_send,
    far_recv,
    gath,
    bent_rows,
    rows_top,
    rows_low,
    gram_send,
    gram_recv,
    inv_keep,
    nat_far,
    in_sem,
    part_ssem,
    part_rsem,
    case_ssem,
    case_rsem,
    gram_ssem,
    gram_rsem,
):
    parts, npy, nq, depth, width, chunks, fold = sizes
    my_x, my_y, my_c = lax.axis_index("px"), lax.axis_index("py"), lax.axis_index("case")
    me = my_x * npy + my_y

    def part_id(step):
        other = lax.rem(me + step + parts, parts)
        return (other // npy, lax.rem(other, npy), my_c)

    def case_to(step):
        if nq == 4:
            other = my_c + (step % 2) * (1 - 2 * lax.rem(my_c, 2))
            return other + (step // 2) * (2 - 4 * (my_c // 2))
        return lax.rem(my_c + step, nq)

    def case_from(step):
        return case_to(step) if nq == 4 else lax.rem(my_c + nq - step, nq)

    def case_id(step):
        return (my_x, my_y, case_to(step))

    direct = (1, 2) if nq == 4 else tuple(range(1, nq))

    barrier = pltpu.get_barrier_semaphore()

    order = sorted(range(1, parts), key=lambda i: -min(i % npy, npy - i % npy))

    def each_other(act):
        def per_part(i, _):
            for q in reversed(range(nq)):
                act(i, q)
            return 0

        if parts <= 8:
            for i in order:
                per_part(i, 0)
        else:
            lax.fori_loop(1, parts, per_part, 0)
        for q in reversed(range(1, nq)):
            act(0, q)

    def device(i, q):
        x, y, _ = part_id(i)
        return (x, y, case_to(q))

    def greet(i, q):
        pl.semaphore_signal(barrier, inc=1, device_id=device(i, q), device_id_type=MESH)

    each_other(greet)

    inputs = (
        (near_hbm, near_ref),
        (owner_hbm, owner_ref),
        (far_hbm, far_ref),
        (kind_hbm, kind_ref),
        (stiff_hbm, stiff_ref),
        (binv_hbm, binv_ref),
        (bload_hbm, bload_ref),
        (coup_hbm, coup_ref),
        (pload_hbm, pload_ref),
        (pblock_hbm, pblock_ref),
    )
    fetches = [
        pltpu.make_async_copy(src, dst, in_sem.at[i]) for i, (src, dst) in enumerate(inputs)
    ]
    for fetch in fetches:
        fetch.start()

    kinds = binv_ref.shape[0]
    modes, ncase, ncomp = bload_ref.shape
    pd = pload_ref.shape[0]
    nport = pload_ref.shape[2]
    slots = parts * depth
    allcase = nq * ncase

    for fetch in fetches[0:5]:
        fetch.wait()
    kind_row = kind_ref[...]
    near_row = near_ref[...]
    owner_row = owner_ref[...]
    far_row = far_ref[...]

    def as_column(row):
        return jnp.broadcast_to(row.astype(F32), (ncomp, ncomp)).T

    sub = lax.broadcasted_iota(jnp.int32, (ncomp, ncomp), 0)
    lane = lax.broadcasted_iota(jnp.int32, (ncomp, ncomp), 1)
    same = (as_column(owner_row) == owner_row.astype(F32)) & (sub < lane)
    rank = jnp.sum(jnp.where(same, 1.0, 0.0), axis=0, keepdims=True).astype(jnp.int32)
    step_row = lax.rem(owner_row - me + parts, parts)
    slot_row = step_row * depth + rank
    slot_sub = lax.broadcasted_iota(jnp.int32, (slots, ncomp), 0)
    slot_pick = jnp.where(slot_sub == slot_row, 1.0, 0.0).astype(BF16)
    step_sub = lax.broadcasted_iota(jnp.int32, (parts, ncomp), 0)
    naming = jnp.concatenate(
        [
            jnp.where(step_sub == step_row, row, 0.0)
            for row in ((far_row + 1).astype(F32), kind_row.astype(F32), stiff_ref[...])
        ],
        axis=0,
    )
    ranked = jnp.where(sub == rank, 1.0, 0.0)
    wanted = exact(naming, ranked, NT)
    wanted = jnp.concatenate([wanted[r * parts:(r + 1) * parts] for r in range(3)], axis=1)
    wanted = wanted.reshape(parts, 1, 3 * ncomp)
    ask_send[...] = wanted
    ask_recv[0] = wanted[0]
    near_in = jnp.where(sub == near_row, 1.0, 0.0).astype(BF16)
    near_out = jnp.where(lane.astype(F32) == as_column(near_row), 1.0, 0.0).astype(BF16)
    near_slots = lax.dot_general(slot_pick, near_in, NT, preferred_element_type=F32).astype(BF16)

    def send_parts(src, dst, e, sign):
        def body(i, _):
            pltpu.make_async_remote_copy(
                src_ref=src(i),
                dst_ref=dst(i),
                send_sem=part_ssem.at[e],
                recv_sem=part_rsem.at[e],
                device_id=part_id(i if sign > 0 else -i),
                device_id_type=MESH,
            ).start()
            return 0

        if parts <= 8:
            for i in order:
                body(i, 0)
        else:
            lax.fori_loop(1, parts, body, 0)

    def wait_on(ref, sem):
        pltpu.make_async_copy(ref, ref, sem).wait()

    rest = pl.ds(1, parts - 1)

    def tile_cases(row):
        return jnp.concatenate([row] * ncase, axis=1)

    def kind_masks(row):
        row = tile_cases(row)
        return [jnp.where(row == t, 1.0, 0.0).astype(BF16) for t in range(kinds)]

    masks = kind_masks(kind_row)

    def table(parts_of):
        top, low = split(parts_of)
        return top, jnp.concatenate([top, low], axis=0)

    def apply_tables(tab, x, masks):
        top, low = split(x)
        lanes = x.shape[1]
        xt = jnp.concatenate([top * m[:, :lanes] for m in masks], axis=0)
        xl = jnp.concatenate([low * m[:, :lanes] for m in masks], axis=0)
        lead = mm(tab[1], xt)
        rows = tab[0].shape[0]
        return lead[:rows] + lead[rows:] + mm(tab[0], xl)

    def wide(field, rows):
        return jnp.concatenate(
            [field[k * rows:(k + 1) * rows] for k in range(field.shape[0] // rows)], axis=1
        )

    def tall(x, count):
        return jnp.concatenate(
            [x[:, k * count:(k + 1) * count] for k in range(x.shape[1] // count)], axis=0
        )

    def pick(x, onehot):
        top, low = split(x)
        return mm(jnp.concatenate([top, low], axis=1), jnp.concatenate([onehot, onehot], axis=0))

    def at_slots(onehot, x):
        top, low = split(x)
        return lax.dot_general(
            jnp.concatenate([onehot, onehot], axis=1),
            jnp.concatenate([top, low], axis=1),
            NT,
            preferred_element_type=F32,
        )

    def place(x, onehot):
        top, low = split(x)
        return mm(top, onehot) + mm(low, onehot)

    def take(e, j):
        wait_on(far_recv.at[e, j, rest], part_rsem.at[1 + e * chunks + j])
        return far_recv[e, j].reshape(slots, width).T

    def post(e, j, out, sign):
        far_send[e, j] = out
        far_recv[e, j, 0] = out[0]
        send_parts(
            lambda i: far_send.at[e, j, i], lambda i: far_recv.at[e, j, i], 1 + e * chunks + j, sign
        )

    def send_case(f, src, dst, sem, step):
        pltpu.make_async_remote_copy(
            src_ref=src,
            dst_ref=dst,
            send_sem=case_ssem.at[f, sem],
            recv_sem=case_rsem.at[f, sem],
            device_id=case_id(step),
            device_id_type=MESH,
        ).start()

    def publish(f, field):
        for k in range(ncase):
            gath[f, my_c, :, k, :] = field[k * pd:(k + 1) * pd]
        for i in reversed(direct):
            send_case(f, gath.at[f, my_c], gath.at[f, my_c], i, i)

    def forward(f):
        if nq == 4:
            block = gath.at[f, case_from(2)]
            wait_on(block, case_rsem.at[f, 2])
            send_case(f, block, block, 3, 1)

    def collect(f):
        for i in range(1, nq):
            if nq != 4 or i != 2:
                wait_on(gath.at[f, case_from(i)], case_rsem.at[f, i])

        def body(d, _):
            cols = pl.ds(pl.multiple_of(d * nport, nport), nport)
            block = jnp.concatenate([gath[f, q, d] for q in range(nq)], axis=0)
            top, low = split(block)
            rows_top[f * allcase:(f + 1) * allcase, cols] = top
            rows_low[f * allcase:(f + 1) * allcase, cols] = low
            return 0

        lax.fori_loop(0, pd, body, 0, unroll=4)

    def against(x, f):
        top, low = split(x)
        band = slice(f * allcase, (f + 1) * allcase)
        lead = lax.dot_general(
            jnp.concatenate([top, low], axis=0),
            rows_top[band, :],
            NT,
            preferred_element_type=F32,
        )
        rest = lax.dot_general(top, rows_low[band, :], NT, preferred_element_type=F32)
        return lead[:x.shape[0]] + lead[x.shape[0]:] + rest

    def own_rows(f):
        return jnp.concatenate([gath[f, my_c, d] for d in range(pd)], axis=1)

    def gram_out(s, block):
        high = ncase // fold
        folded = jnp.concatenate([block[r * high:(r + 1) * high] for r in range(fold)], axis=1)
        gram_send[s] = folded
        gram_recv[s, my_c * parts] = folded

        def send(i, q):
            pltpu.make_async_remote_copy(
                src_ref=gram_send.at[s],
                dst_ref=gram_recv.at[s, my_c * parts + i],
                send_sem=gram_ssem.at[s],
                recv_sem=gram_rsem.at[s],
                device_id=device(i, q),
                device_id_type=MESH,
            ).start()

        each_other(send)

    others = pl.ds(1, nq * parts - 1)

    def gram_in(s):
        wait_on(gram_recv.at[s, others], gram_rsem.at[s])
        lines = []
        for q in range(nq):
            total = jnp.sum(gram_recv[s, q * parts:(q + 1) * parts], axis=0)
            for r in range(fold):
                lines.append(total[:, r * allcase:(r + 1) * allcase])
        return sym(jnp.concatenate(lines, axis=0))

    def sym(g):
        return 0.5 * (g + g.T)

    def part(x, j):
        return x[j * width:(j + 1) * width]

    for fetch in fetches[5:8]:
        fetch.wait()
    inv_tab = table(jnp.concatenate([binv_ref[t] for t in range(kinds)], axis=1))
    coup_tab = table(jnp.concatenate([coup_ref[t].T for t in range(kinds)], axis=1))
    ready = [0] + [-(-((j + 1) * width) // pd) for j in range(chunks)]
    condensed_near, leaving = [], None
    for j in range(chunks):
        a, b = ready[j], ready[j + 1]
        loads = jnp.concatenate([bload_ref[:, k, :] for k in range(a, b)], axis=1)
        lifted = apply_tables(inv_tab, loads, masks)
        inv_keep[:, a * ncomp:b * ncomp] = lifted
        condensed = -apply_tables(coup_tab, lifted, masks)
        condensed_near.append(tall(condensed[:pd], ncomp))
        out = tall(condensed[pd:], ncomp)
        leaving = out if leaving is None else jnp.concatenate([leaving, out], axis=0)
        if j == 0:
            pl.semaphore_wait(barrier, parts * nq - 1)
            send_parts(lambda i: ask_send.at[i], lambda i: ask_recv.at[i], 0, 1)
        post(0, j, at_slots(slot_pick, part(leaving, j)).reshape(parts, depth, width), 1)
    for fetch in fetches[8:]:
        fetch.wait()
    stiff = tile_cases(stiff_ref[...])
    red_t = [exact(binv_ref[t], coup_ref[t], TN) for t in range(kinds)]
    schur = [pblock_ref[t] - exact(red_t[t], coup_ref[t], TN) for t in range(kinds)]

    def corner(a, b):
        rows, cols = slice(a * pd, (a + 1) * pd), slice(b * pd, (b + 1) * pd)
        return table(jnp.concatenate([schur[t][rows, cols] for t in range(kinds)], axis=1))

    nn_tab, nf_tab, fn_tab, ff_tab = corner(0, 0), corner(0, 1), corner(1, 0), corner(1, 1)
    red_tab = table(jnp.concatenate(red_t, axis=1))
    own = jnp.concatenate([pload_ref[:, k, :] for k in range(ncase)], axis=0)
    own = own + pick(jnp.concatenate(condensed_near, axis=0), near_out)
    wait_on(ask_recv.at[rest], part_rsem.at[0])
    asked = ask_recv[...].reshape(parts, 3 * ncomp)
    ports = jnp.concatenate([asked[:, 0:ncomp]] * (ncomp // parts), axis=0).T
    port_lane = lax.broadcasted_iota(jnp.int32, (depth, nport), 1).astype(F32)
    asked_pick = jnp.concatenate(
        [jnp.where(ports[0:depth, i:i + 1] - 1.0 == port_lane, 1.0, 0.0) for i in range(parts)],
        axis=0,
    ).astype(BF16)

    def slot_line(r):
        return jnp.concatenate(
            [asked[i:i + 1, r * ncomp:r * ncomp + depth] for i in range(parts)], axis=1
        )

    slot_masks = kind_masks(slot_line(1))
    slot_stiff = tile_cases(slot_line(2))
    both_picks = jnp.concatenate([asked_pick, near_slots], axis=0)

    def scatter(e, j, piece):
        out = at_slots(both_picks, piece)
        post(e, j, out[:slots].reshape(parts, depth, width), -1)
        return lambda: post(e + 1, j, out[slots:].reshape(parts, depth, width), 1)

    def join(a, b):
        return b if a is None else jnp.concatenate([a, b], axis=0)

    def near_side(tab, x, a, b):
        return apply_tables(tab, wide(x, pd), masks) * stiff[:, a * ncomp:b * ncomp]

    def far_side(tab, x, a, b):
        return apply_tables(tab, wide(x, pd), slot_masks) * slot_stiff[:, a * slots:b * slots]

    def near_ports(y):
        return pick(tall(y, ncomp), near_out)

    def far_ports(y):
        return place(tall(y, slots), asked_pick)

    def diagonal(e, field):
        y_near = near_side(nn_tab, pick(field, near_in), 0, ncase)
        far_at = [far_send[e, j].reshape(slots, width).T for j in range(chunks)]
        return y_near, far_side(ff_tab, jnp.concatenate(far_at, axis=0), 0, ncase)

    def take_far_values(e, j):
        return place(take(e, j), slot_pick)

    cuts = [0] + [((j + 1) * width) // pd for j in range(chunks)]

    base = None
    for j in range(chunks):
        piece = part(own, j) + place(take(0, j), asked_pick)
        scatter(1, j, piece)()
        base = join(base, piece)
    publish(0, base)

    y_near, y_far = diagonal(1, base)
    far_base, near_at, first, sent, later = None, None, None, 0, []
    for j in range(chunks):
        a, b = cuts[j], cuts[j + 1]
        if j == chunks - 1:
            forward(0)
        far_base = join(far_base, take_far_values(1, j))
        near_at = join(near_at, take(2, j))
        rows = slice(a * pd, b * pd)
        y = y_near[:, a * ncomp:b * ncomp] + near_side(nf_tab, far_base[rows], a, b)
        done = near_ports(y)
        y = y_far[:, a * slots:b * slots] + far_side(fn_tab, near_at[rows], a, b)
        first = join(first, done + far_ports(y))
        while (sent + 1) * width <= b * pd:
            later.append(scatter(3, sent, part(first, sent)))
            sent += 1
    publish(1, first)

    y_near, y_far = diagonal(3, first)
    straight = near_ports(y_near) + far_ports(y_far)
    collect(0)
    early = against(jnp.concatenate([own_rows(0), own_rows(1)], axis=0), 0)
    gram_out(0, early[:ncase])
    gram_out(1, early[ncase:])
    for post_near in later:
        post_near()
    publish(3, far_base)
    far_first, crossed = None, None
    for j in range(chunks):
        a, b = cuts[j], cuts[j + 1]
        if j == chunks - 1:
            forward(1)
        far_first = join(far_first, take_far_values(3, j))
        crossed = join(crossed, near_ports(near_side(nf_tab, far_first[a * pd:b * pd], a, b)))
    collect(1)
    bent = straight + 2.0 * crossed
    for k in range(ncase):
        bent_rows[:, k, :] = bent[k * pd:(k + 1) * pd]
    lines = jnp.concatenate([bent_rows[d] for d in range(pd)], axis=1)
    late = against(jnp.concatenate([lines, own_rows(1)], axis=0), 1)
    gram_out(3, late[:ncase])
    gram_out(2, late[ncase:])
    publish(4, far_first)
    second, near_at = None, None
    for j in range(chunks):
        a, b = cuts[j], cuts[j + 1]
        if j == chunks - 1:
            forward(3)
        near_at = join(near_at, take(4, j))
        second = join(second, far_ports(far_side(fn_tab, near_at[a * pd:b * pd], a, b)))
    second = second + straight + crossed
    publish(2, second)

    n = allcase
    g00, g01 = gram_in(0), gram_in(1)
    eye = jnp.where(
        lax.broadcasted_iota(jnp.int32, (n, n), 0) == lax.broadcasted_iota(jnp.int32, (n, n), 1),
        1.0,
        0.0,
    )
    both = gauss_solve(g01, jnp.concatenate([g00, eye], axis=1))
    mine = jnp.where(
        lax.broadcasted_iota(jnp.int32, (n, ncase), 0)
        == lax.broadcasted_iota(jnp.int32, (n, ncase), 1) + my_c * ncase,
        1.0,
        0.0,
    )
    chosen = exact(jnp.concatenate([both[:, 0:n], g01], axis=0), mine)
    first_step, g01_mine, inverse = chosen[0:n], chosen[n:2 * n], both[:, n:2 * n]
    forward(4)
    collect(3)
    g11 = gram_in(2)
    over = exact(inverse, g11)
    side = exact(g11, jnp.concatenate([over, first_step], axis=1))
    wait_on(ask_send.at[rest], part_ssem.at[0])
    for e in range(5):
        for j in range(chunks):
            wait_on(far_send.at[e, j, rest], part_ssem.at[1 + e * chunks + j])
    for s in range(4):
        wait_on(gram_recv.at[s, others], gram_ssem.at[s])
    for f in (0, 1, 3):
        for i in range(1, nq):
            wait_on(gath.at[f, my_c], case_ssem.at[f, i])
    g12 = gram_in(3)
    beta = gauss_solve(g12 - sym(side[:, 0:n]), side[:, n:] - g01_mine)
    alpha = first_step + exact(over, beta)
    coefs = jnp.concatenate([alpha, -beta], axis=0).T
    ctop, clow = split(coefs)
    stack = jnp.concatenate([ctop, clow], axis=0)

    def mix(f):
        band = slice(f * allcase, (f + 2) * allcase)
        lead = mm(stack, rows_top[band, :])
        return lead[0:ncase] + lead[ncase:] + mm(ctop, rows_low[band, :])

    answer_rows = mix(0)
    for d in range(pd):
        sol_ref[d] = answer_rows[:, d * nport:(d + 1) * nport]
    collect(4)
    forward(2)
    far_rows = mix(3)
    for d in range(pd):
        nat_far[d] = far_rows[:, d * nport:(d + 1) * nport]
    answer = jnp.concatenate([sol_ref[:, k, :] for k in range(ncase)], axis=0)
    near = wide(pick(answer, near_in), pd)
    ends = jnp.concatenate(
        [near, jnp.concatenate([nat_far[:, k, :] for k in range(ncase)], axis=1)], axis=0
    )
    scaled = inv_keep[...] / stiff
    back = scaled - apply_tables(red_tab, ends, masks)
    for k in range(ncase):
        bub_ref[:, k, :] = back[:, k * ncomp:(k + 1) * ncomp]
    collect(2)
    drop_rows = mix(1)
    for d in range(pd):
        res_ref[d] = gath[0, my_c, d] - drop_rows[:, d * nport:(d + 1) * nport]

    for f in (2, 4):
        for i in range(1, nq):
            wait_on(gath.at[f, my_c], case_ssem.at[f, i])


def emit(*refs):
    count = len(refs) // 2
    sems = refs[-1]
    copies = [
        pltpu.make_async_copy(refs[i], refs[count + i], sems.at[i]) for i in range(count)
    ]
    for copy in copies:
        copy.start()
    for copy in copies:
        copy.wait()


def local(
    comp_type,
    stiffness,
    near_port,
    far_owner,
    far_port,
    bubble_load,
    port_load,
    bubble_inverse,
    coupling,
    port_block,
):
    npy = lax.axis_size("py")
    parts = lax.axis_size("px") * npy
    nq = lax.axis_size("case")
    ncomp = comp_type.shape[0]
    modes, ncase, _ = bubble_load.shape
    pd, _, nport = port_load.shape
    kinds = bubble_inverse.shape[0]
    cap = 3 * ncomp // (2 * parts)
    depth = -(-cap // 8) * 8
    allcase = nq * ncase
    width = 128 if (ncase * pd) % 128 == 0 else ncase * pd
    chunks = ncase * pd // width
    fold = max(1, 128 // allcase)
    vmem = pl.BlockSpec(memory_space=pltpu.VMEM)
    hbm = pl.BlockSpec(memory_space=pltpu.HBM)

    def body(*refs):
        kernel((parts, npy, nq, depth, width, chunks, fold), *refs)

    shapes = (
        jax.ShapeDtypeStruct(port_load.shape, F32),
        jax.ShapeDtypeStruct(port_load.shape, F32),
        jax.ShapeDtypeStruct(bubble_load.shape, F32),
    )
    results = pl.pallas_call(
        body,
        out_shape=shapes,
        in_specs=[hbm] * 10,
        out_specs=(vmem, vmem, vmem),
        scratch_shapes=[
            pltpu.VMEM((1, ncomp), jnp.int32),
            pltpu.VMEM((1, ncomp), jnp.int32),
            pltpu.VMEM((1, ncomp), jnp.int32),
            pltpu.VMEM((1, ncomp), jnp.int32),
            pltpu.VMEM((1, ncomp), F32),
            pltpu.VMEM(bubble_load.shape, F32),
            pltpu.VMEM(port_load.shape, F32),
            pltpu.VMEM(bubble_inverse.shape, F32),
            pltpu.VMEM((kinds, modes, 2 * pd), F32),
            pltpu.VMEM(port_block.shape, F32),
            pltpu.VMEM((parts, 1, 3 * ncomp), F32),
            pltpu.VMEM((parts, 1, 3 * ncomp), F32),
            pltpu.VMEM((5, chunks, parts, depth, width), F32),
            pltpu.VMEM((5, chunks, parts, depth, width), F32),
            pltpu.VMEM((5, nq, pd, ncase, nport), F32),
            pltpu.VMEM((pd, ncase, nport), F32),
            pltpu.VMEM((5 * allcase, pd * nport), BF16),
            pltpu.VMEM((5 * allcase, pd * nport), BF16),
            pltpu.VMEM((4, ncase // fold, fold * allcase), F32),
            pltpu.VMEM((4, nq * parts, ncase // fold, fold * allcase), F32),
            pltpu.VMEM((modes, ncase * ncomp), F32),
            pltpu.VMEM((pd, ncase, nport), F32),
            pltpu.SemaphoreType.DMA((10,)),
            pltpu.SemaphoreType.DMA((1 + 5 * chunks,)),
            pltpu.SemaphoreType.DMA((1 + 5 * chunks,)),
            pltpu.SemaphoreType.DMA((5, nq)),
            pltpu.SemaphoreType.DMA((5, nq)),
            pltpu.SemaphoreType.DMA((4,)),
            pltpu.SemaphoreType.DMA((4,)),
        ],
        compiler_params=pltpu.CompilerParams(
            collective_id=0, has_side_effects=True, vmem_limit_bytes=32 * 1024 * 1024
        ),
        name="condensed_solve",
    )(
        *(
            pltpu.with_memory_space_constraint(x, pltpu.HBM)
            for x in (
                comp_type.reshape(1, ncomp),
                near_port.reshape(1, ncomp),
                far_owner.reshape(1, ncomp),
                far_port.reshape(1, ncomp),
                stiffness.reshape(1, ncomp),
                bubble_load,
                port_load,
                bubble_inverse,
                jnp.swapaxes(coupling, 1, 2),
                port_block,
            )
        )
    )
    return pl.pallas_call(
        emit,
        out_shape=shapes,
        in_specs=[vmem] * 3,
        out_specs=(hbm, hbm, hbm),
        scratch_shapes=[pltpu.SemaphoreType.DMA((3,))],
        compiler_params=pltpu.CompilerParams(vmem_limit_bytes=4 * 1024 * 1024),
        name="emit",
    )(*results)


def solution(mesh):
    placed = (
        P(("px", "py")),
        P(("px", "py")),
        P(("px", "py")),
        P(("px", "py"), None),
        P(("px", "py")),
        P(None, "case", ("px", "py")),
        P(None, "case", ("px", "py")),
        P(),
        P(),
        P(),
    )
    return jax.shard_map(
        local,
        mesh=mesh,
        in_specs=placed,
        out_specs=(
            P(None, "case", ("px", "py")),
            P(None, "case", ("px", "py")),
            P(None, "case", ("px", "py")),
        ),
        check_vma=False,
    )
```

```python
import jax
import jax.numpy as jnp
from jax import lax
from jax.experimental import pallas as pl
from jax.experimental.pallas import tpu as pltpu
from jax.sharding import PartitionSpec as P

HIGH = lax.Precision.HIGHEST
F32 = jnp.float32
BF16 = jnp.bfloat16
MESH = pl.DeviceIdType.MESH
NT = (((1,), (1,)), ((), ()))
TN = (((0,), (0,)), ((), ()))


def split(x):
    top = x.astype(BF16)
    return top, (x - top.astype(F32)).astype(BF16)


def mm(a, b):
    return jnp.dot(a, b, preferred_element_type=F32)


def exact(a, b, dims=(((1,), (0,)), ((), ()))):
    return lax.dot_general(a, b, dims, precision=HIGH, preferred_element_type=F32)


def gauss_solve(matrix, target):
    n = matrix.shape[0]
    aug = jnp.concatenate([matrix, target], axis=1)
    rows = lax.broadcasted_iota(jnp.int32, aug.shape, 0)
    for j in range(0, n, 2):
        row0, row1 = aug[j:j + 1, :], aug[j + 1:j + 2, :]
        col0 = jnp.broadcast_to(aug[:, j:j + 1], aug.shape)
        col1 = jnp.broadcast_to(aug[:, j + 1:j + 2], aug.shape)
        a, c = col0[j:j + 1, :], col0[j + 1:j + 2, :]
        b, d = col1[j:j + 1, :], col1[j + 1:j + 2, :]
        scale = 1.0 / (a * d - b * c)
        new0 = (d * row0 - b * row1) * scale
        new1 = (a * row1 - c * row0) * scale
        rest = aug - col0 * new0 - col1 * new1
        aug = jnp.where(rows == j, new0, jnp.where(rows == j + 1, new1, rest))
    return aug[:, n:]


def kernel(
    sizes,
    kind_hbm,
    near_hbm,
    owner_hbm,
    far_hbm,
    stiff_hbm,
    bload_hbm,
    pload_hbm,
    binv_hbm,
    coup_hbm,
    pblock_hbm,
    sol_ref,
    res_ref,
    bub_ref,
    kind_ref,
    near_ref,
    owner_ref,
    far_ref,
    stiff_ref,
    bload_ref,
    pload_ref,
    binv_ref,
    coup_ref,
    pblock_ref,
    ask_send,
    ask_recv,
    far_send,
    far_recv,
    gath,
    bent_rows,
    rows_top,
    rows_low,
    gram_send,
    gram_recv,
    inv_keep,
    nat_far,
    in_sem,
    send_sem,
    part_rsem,
    case_rsem,
    gram_rsem,
):
    parts, npy, nq, depth, width, chunks, fold = sizes
    my_x, my_y, my_c = lax.axis_index("px"), lax.axis_index("py"), lax.axis_index("case")
    me = my_x * npy + my_y

    def part_id(step):
        other = lax.rem(me + step + parts, parts)
        return (other // npy, lax.rem(other, npy), my_c)

    def case_to(step):
        if nq == 4:
            other = my_c + (step % 2) * (1 - 2 * lax.rem(my_c, 2))
            return other + (step // 2) * (2 - 4 * (my_c // 2))
        return lax.rem(my_c + step, nq)

    def case_from(step):
        return case_to(step) if nq == 4 else lax.rem(my_c + nq - step, nq)

    def case_id(step):
        return (my_x, my_y, case_to(step))

    direct = (1, 2) if nq == 4 else tuple(range(1, nq))

    barrier = pltpu.get_barrier_semaphore()

    order = sorted(range(1, parts), key=lambda i: -min(i % npy, npy - i % npy))

    def each_other(act):
        def per_part(i, _):
            for q in reversed(range(nq)):
                act(i, q)
            return 0

        if parts <= 8:
            for i in order:
                per_part(i, 0)
        else:
            lax.fori_loop(1, parts, per_part, 0)
        for q in reversed(range(1, nq)):
            act(0, q)

    def device(i, q):
        x, y, _ = part_id(i)
        return (x, y, case_to(q))

    def greet_part(i, _):
        pl.semaphore_signal(barrier, inc=1, device_id=part_id(i), device_id_type=MESH)
        return 0

    lax.fori_loop(1, parts, greet_part, 0)
    for i in range(1, nq):
        pl.semaphore_signal(barrier, inc=1, device_id=case_id(i), device_id_type=MESH)

    inputs = (
        (near_hbm, near_ref),
        (owner_hbm, owner_ref),
        (far_hbm, far_ref),
        (kind_hbm, kind_ref),
        (stiff_hbm, stiff_ref),
        (binv_hbm, binv_ref),
        (bload_hbm, bload_ref),
        (coup_hbm, coup_ref),
        (pload_hbm, pload_ref),
        (pblock_hbm, pblock_ref),
    )
    fetches = [
        pltpu.make_async_copy(src, dst, in_sem.at[i]) for i, (src, dst) in enumerate(inputs)
    ]
    for fetch in fetches:
        fetch.start()

    kinds = binv_ref.shape[0]
    modes, ncase, ncomp = bload_ref.shape
    pd = pload_ref.shape[0]
    nport = pload_ref.shape[2]
    slots = parts * depth
    allcase = nq * ncase

    for fetch in fetches[0:5]:
        fetch.wait()
    kind_row = kind_ref[...]
    near_row = near_ref[...]
    owner_row = owner_ref[...]
    far_row = far_ref[...]

    def as_column(row):
        return jnp.broadcast_to(row.astype(F32), (ncomp, ncomp)).T

    sub = lax.broadcasted_iota(jnp.int32, (ncomp, ncomp), 0)
    lane = lax.broadcasted_iota(jnp.int32, (ncomp, ncomp), 1)
    same = (as_column(owner_row) == owner_row.astype(F32)) & (sub < lane)
    rank = jnp.sum(jnp.where(same, 1.0, 0.0), axis=0, keepdims=True).astype(jnp.int32)
    step_row = lax.rem(owner_row - me + parts, parts)
    slot_row = step_row * depth + rank
    slot_sub = lax.broadcasted_iota(jnp.int32, (slots, ncomp), 0)
    slot_pick = jnp.where(slot_sub == slot_row, 1.0, 0.0).astype(BF16)
    step_sub = lax.broadcasted_iota(jnp.int32, (parts, ncomp), 0)
    def send_parts(src, dst, e, sign):
        def body(i, _):
            pltpu.make_async_remote_copy(
                src_ref=src(i),
                dst_ref=dst(i),
                send_sem=send_sem.at[0 if e else 3],
                recv_sem=part_rsem.at[e],
                device_id=part_id(i if sign > 0 else -i),
                device_id_type=MESH,
            ).start()
            return 0

        if parts <= 8:
            for i in order:
                body(i, 0)
        else:
            lax.fori_loop(1, parts, body, 0)

    def wait_on(ref, sem):
        pltpu.make_async_copy(ref, ref, sem).wait()

    rest = pl.ds(1, parts - 1)

    def tile_cases(row):
        return jnp.concatenate([row] * ncase, axis=1)

    def kind_masks(row):
        row = tile_cases(row)
        return [jnp.where(row == t, 1.0, 0.0).astype(BF16) for t in range(kinds)]

    masks = kind_masks(kind_row)

    def table(parts_of):
        top, low = split(parts_of)
        return top, jnp.concatenate([top, low], axis=0)

    def apply_tables(tab, x, masks):
        top, low = split(x)
        lanes = x.shape[1]
        xt = jnp.concatenate([top * m[:, :lanes] for m in masks], axis=0)
        xl = jnp.concatenate([low * m[:, :lanes] for m in masks], axis=0)
        lead = mm(tab[1], xt)
        rows = tab[0].shape[0]
        return lead[:rows] + lead[rows:] + mm(tab[0], xl)

    def wide(field, rows):
        return jnp.concatenate(
            [field[k * rows:(k + 1) * rows] for k in range(field.shape[0] // rows)], axis=1
        )

    def tall(x, count):
        return jnp.concatenate(
            [x[:, k * count:(k + 1) * count] for k in range(x.shape[1] // count)], axis=0
        )

    def pick(x, onehot):
        top, low = split(x)
        return mm(jnp.concatenate([top, low], axis=1), jnp.concatenate([onehot, onehot], axis=0))

    def at_slots(onehot, x):
        top, low = split(x)
        return lax.dot_general(
            jnp.concatenate([onehot, onehot], axis=1),
            jnp.concatenate([top, low], axis=1),
            NT,
            preferred_element_type=F32,
        )

    def place(x, onehot):
        top, low = split(x)
        return mm(top, onehot) + mm(low, onehot)

    def take(e, j):
        wait_on(far_recv.at[e, j, rest], part_rsem.at[1 + e * chunks + j])
        return far_recv[e, j].reshape(slots, width).T

    def post(e, j, out, sign):
        far_send[e, j] = out
        far_recv[e, j, 0] = out[0]
        send_parts(
            lambda i: far_send.at[e, j, i], lambda i: far_recv.at[e, j, i], 1 + e * chunks + j, sign
        )

    def send_case(f, src, dst, sem, step):
        pltpu.make_async_remote_copy(
            src_ref=src,
            dst_ref=dst,
            send_sem=send_sem.at[1],
            recv_sem=case_rsem.at[f, sem],
            device_id=case_id(step),
            device_id_type=MESH,
        ).start()

    def publish(f, field):
        for k in range(ncase):
            gath[f, my_c, :, k, :] = field[k * pd:(k + 1) * pd]
        for i in reversed(direct):
            send_case(f, gath.at[f, my_c], gath.at[f, my_c], i, i)

    def forward(f):
        if nq == 4:
            block = gath.at[f, case_from(2)]
            wait_on(block, case_rsem.at[f, 2])
            send_case(f, block, block, 3, 1)

    def collect(f):
        for i in range(1, nq):
            if nq != 4 or i != 2:
                wait_on(gath.at[f, case_from(i)], case_rsem.at[f, i])

        def body(d, _):
            cols = pl.ds(pl.multiple_of(d * nport, nport), nport)
            block = jnp.concatenate([gath[f, q, d] for q in range(nq)], axis=0)
            top, low = split(block)
            rows_top[f * allcase:(f + 1) * allcase, cols] = top
            rows_low[f * allcase:(f + 1) * allcase, cols] = low
            return 0

        lax.fori_loop(0, pd, body, 0, unroll=4)

    def against(x, f):
        top, low = split(x)
        band = slice(f * allcase, (f + 1) * allcase)
        lead = lax.dot_general(
            jnp.concatenate([top, low], axis=0),
            rows_top[band, :],
            NT,
            preferred_element_type=F32,
        )
        low_lead = lax.dot_general(
            jnp.concatenate([top, low], axis=0),
            rows_low[band, :],
            NT,
            preferred_element_type=F32,
        )
        total = lead + low_lead
        return total[:x.shape[0]] + total[x.shape[0]:]

    def own_rows(f):
        return jnp.concatenate([gath[f, my_c, d] for d in range(pd)], axis=1)

    def gram_out(s, block):
        high = ncase // fold
        folded = jnp.concatenate([block[r * high:(r + 1) * high] for r in range(fold)], axis=1)
        gram_send[s] = folded
        gram_recv[s, my_c * parts] = folded

        def send(i, q):
            pltpu.make_async_remote_copy(
                src_ref=gram_send.at[s],
                dst_ref=gram_recv.at[s, my_c * parts + i],
                send_sem=send_sem.at[2],
                recv_sem=gram_rsem.at[s],
                device_id=device(i, q),
                device_id_type=MESH,
            ).start()

        each_other(send)

    others = pl.ds(1, nq * parts - 1)

    def gram_in(s):
        wait_on(gram_recv.at[s, others], gram_rsem.at[s])
        lines = []
        for q in range(nq):
            total = jnp.sum(gram_recv[s, q * parts:(q + 1) * parts], axis=0)
            for r in range(fold):
                lines.append(total[:, r * allcase:(r + 1) * allcase])
        return sym(jnp.concatenate(lines, axis=0))

    def sym(g):
        return 0.5 * (g + g.T)

    def part(x, j):
        return x[j * width:(j + 1) * width]

    for fetch in fetches[5:8]:
        fetch.wait()
    inv_tab = table(jnp.concatenate([binv_ref[t] for t in range(kinds)], axis=1))
    coup_tab = table(jnp.concatenate([coup_ref[t].T for t in range(kinds)], axis=1))
    def ask():
        naming = jnp.concatenate(
            [
                jnp.where(step_sub == step_row, row, 0.0)
                for row in ((far_row + 1).astype(F32), kind_row.astype(F32), stiff_ref[...])
            ],
            axis=0,
        )
        ranked = jnp.where(sub == rank, 1.0, 0.0)
        wanted = exact(naming, ranked, NT)
        wanted = jnp.concatenate([wanted[r * parts:(r + 1) * parts] for r in range(3)], axis=1)
        wanted = wanted.reshape(parts, 1, 3 * ncomp)
        ask_send[...] = wanted
        ask_recv[0] = wanted[0]
        send_parts(lambda i: ask_send.at[i], lambda i: ask_recv.at[i], 0, 1)

    ready = [0] + [-(-((j + 1) * width) // pd) for j in range(chunks)]
    condensed_near, leaving = [], None
    for j in range(chunks):
        a, b = ready[j], ready[j + 1]
        loads = jnp.concatenate([bload_ref[:, k, :] for k in range(a, b)], axis=1)
        lifted = apply_tables(inv_tab, loads, masks)
        inv_keep[:, a * ncomp:b * ncomp] = lifted
        condensed = -apply_tables(coup_tab, lifted, masks)
        condensed_near.append(tall(condensed[:pd], ncomp))
        out = tall(condensed[pd:], ncomp)
        leaving = out if leaving is None else jnp.concatenate([leaving, out], axis=0)
        if j == 0:
            pl.semaphore_wait(barrier, parts + nq - 2)
        post(0, j, at_slots(slot_pick, part(leaving, j)).reshape(parts, depth, width), 1)
        if j == 0:
            ask()
    for fetch in fetches[8:]:
        fetch.wait()
    near_in = jnp.where(sub == near_row, 1.0, 0.0).astype(BF16)
    near_out = jnp.where(lane.astype(F32) == as_column(near_row), 1.0, 0.0).astype(BF16)
    near_slots = lax.dot_general(slot_pick, near_in, NT, preferred_element_type=F32).astype(BF16)

    stiff = tile_cases(stiff_ref[...])
    red_t = [exact(binv_ref[t], coup_ref[t], TN) for t in range(kinds)]
    schur = [pblock_ref[t] - exact(red_t[t], coup_ref[t], TN) for t in range(kinds)]

    def corner(a, b):
        rows, cols = slice(a * pd, (a + 1) * pd), slice(b * pd, (b + 1) * pd)
        return table(jnp.concatenate([schur[t][rows, cols] for t in range(kinds)], axis=1))

    nn_tab, nf_tab, fn_tab, ff_tab = corner(0, 0), corner(0, 1), corner(1, 0), corner(1, 1)
    red_tab = table(jnp.concatenate(red_t, axis=1))
    own = jnp.concatenate([pload_ref[:, k, :] for k in range(ncase)], axis=0)
    own = own + pick(jnp.concatenate(condensed_near, axis=0), near_out)
    wait_on(ask_recv.at[rest], part_rsem.at[0])
    asked = ask_recv[...].reshape(parts, 3 * ncomp)
    ports = jnp.concatenate([asked[:, 0:ncomp]] * (ncomp // parts), axis=0).T
    port_lane = lax.broadcasted_iota(jnp.int32, (depth, nport), 1).astype(F32)
    asked_pick = jnp.concatenate(
        [jnp.where(ports[0:depth, i:i + 1] - 1.0 == port_lane, 1.0, 0.0) for i in range(parts)],
        axis=0,
    ).astype(BF16)

    def slot_line(r):
        return jnp.concatenate(
            [asked[i:i + 1, r * ncomp:r * ncomp + depth] for i in range(parts)], axis=1
        )

    slot_masks = kind_masks(slot_line(1))
    slot_stiff = tile_cases(slot_line(2))
    both_picks = jnp.concatenate([asked_pick, near_slots], axis=0)

    def scatter(e, j, piece):
        out = at_slots(both_picks, piece)
        post(e, j, out[:slots].reshape(parts, depth, width), -1)
        return lambda: post(e + 1, j, out[slots:].reshape(parts, depth, width), 1)

    def join(a, b):
        return b if a is None else jnp.concatenate([a, b], axis=0)

    def near_side(tab, x, a, b):
        return apply_tables(tab, wide(x, pd), masks) * stiff[:, a * ncomp:b * ncomp]

    def far_side(tab, x, a, b):
        return apply_tables(tab, wide(x, pd), slot_masks) * slot_stiff[:, a * slots:b * slots]

    def near_ports(y):
        return pick(tall(y, ncomp), near_out)

    def far_ports(y):
        return place(tall(y, slots), asked_pick)

    def diagonal(e, field):
        y_near = near_side(nn_tab, pick(field, near_in), 0, ncase)
        far_at = [far_send[e, j].reshape(slots, width).T for j in range(chunks)]
        return y_near, far_side(ff_tab, jnp.concatenate(far_at, axis=0), 0, ncase)

    def take_far_values(e, j):
        return place(take(e, j), slot_pick)

    cuts = [0] + [((j + 1) * width) // pd for j in range(chunks)]

    base = None
    for j in range(chunks):
        piece = part(own, j) + place(take(0, j), asked_pick)
        scatter(1, j, piece)()
        base = join(base, piece)
    publish(0, base)

    y_near, y_far = diagonal(1, base)
    far_base, near_at, first, sent, later = None, None, None, 0, []
    for j in range(chunks):
        a, b = cuts[j], cuts[j + 1]
        if j == chunks - 1:
            forward(0)
        far_base = join(far_base, take_far_values(1, j))
        near_at = join(near_at, take(2, j))
        rows = slice(a * pd, b * pd)
        y = y_near[:, a * ncomp:b * ncomp] + near_side(nf_tab, far_base[rows], a, b)
        done = near_ports(y)
        y = y_far[:, a * slots:b * slots] + far_side(fn_tab, near_at[rows], a, b)
        first = join(first, done + far_ports(y))
        while (sent + 1) * width <= b * pd:
            later.append(scatter(3, sent, part(first, sent)))
            sent += 1
    publish(1, first)

    y_near, y_far = diagonal(3, first)
    straight = near_ports(y_near) + far_ports(y_far)
    collect(0)
    early = against(jnp.concatenate([own_rows(0), own_rows(1)], axis=0), 0)
    gram_out(0, early[:ncase])
    gram_out(1, early[ncase:])
    for post_near in later:
        post_near()
    publish(3, far_base)
    far_first, crossed = None, None
    for j in range(chunks):
        a, b = cuts[j], cuts[j + 1]
        if j == chunks - 1:
            forward(1)
        far_first = join(far_first, take_far_values(3, j))
        crossed = join(crossed, near_ports(near_side(nf_tab, far_first[a * pd:b * pd], a, b)))
    collect(1)
    bent = straight + 2.0 * crossed
    for k in range(ncase):
        bent_rows[:, k, :] = bent[k * pd:(k + 1) * pd]
    lines = jnp.concatenate([bent_rows[d] for d in range(pd)], axis=1)
    late = against(jnp.concatenate([lines, own_rows(1)], axis=0), 1)
    gram_out(3, late[:ncase])
    gram_out(2, late[ncase:])
    publish(4, far_first)
    n = allcase
    g00, g01 = gram_in(0), gram_in(1)
    eye = jnp.where(
        lax.broadcasted_iota(jnp.int32, (n, n), 0) == lax.broadcasted_iota(jnp.int32, (n, n), 1),
        1.0,
        0.0,
    )
    both = gauss_solve(g01, jnp.concatenate([g00, eye], axis=1))
    mine = jnp.where(
        lax.broadcasted_iota(jnp.int32, (n, ncase), 0)
        == lax.broadcasted_iota(jnp.int32, (n, ncase), 1) + my_c * ncase,
        1.0,
        0.0,
    )
    chosen = exact(jnp.concatenate([both[:, 0:n], g01], axis=0), mine)
    first_step, g01_mine, inverse = chosen[0:n], chosen[n:2 * n], both[:, n:2 * n]
    second, near_at = None, None
    for j in range(chunks):
        a, b = cuts[j], cuts[j + 1]
        if j == chunks - 1:
            forward(3)
        near_at = join(near_at, take(4, j))
        second = join(second, far_ports(far_side(fn_tab, near_at[a * pd:b * pd], a, b)))
    second = second + straight + crossed
    publish(2, second)

    g11 = gram_in(2)
    over = exact(inverse, g11)
    side = exact(g11, jnp.concatenate([over, first_step], axis=1))
    collect(3)
    forward(4)
    g12 = gram_in(3)
    beta = gauss_solve(g12 - sym(side[:, 0:n]), side[:, n:] - g01_mine)
    alpha = first_step + exact(over, beta)
    coefs = jnp.concatenate([alpha, -beta], axis=0).T
    ctop, clow = split(coefs)
    stack = jnp.concatenate([ctop, clow], axis=0)

    def mix(f):
        band = slice(f * allcase, (f + 2) * allcase)
        lead = mm(stack, rows_top[band, :])
        return lead[0:ncase] + lead[ncase:] + mm(ctop, rows_low[band, :])

    answer_rows = mix(0)
    for d in range(pd):
        sol_ref[d] = answer_rows[:, d * nport:(d + 1) * nport]
    collect(4)
    forward(2)
    far_rows = mix(3)
    for d in range(pd):
        nat_far[d] = far_rows[:, d * nport:(d + 1) * nport]
    answer = jnp.concatenate([sol_ref[:, k, :] for k in range(ncase)], axis=0)
    near = wide(pick(answer, near_in), pd)
    ends = jnp.concatenate(
        [near, jnp.concatenate([nat_far[:, k, :] for k in range(ncase)], axis=1)], axis=0
    )
    scaled = inv_keep[...] / stiff
    back = scaled - apply_tables(red_tab, ends, masks)
    for k in range(ncase):
        bub_ref[:, k, :] = back[:, k * ncomp:(k + 1) * ncomp]
    collect(2)
    drop_rows = mix(1)
    for d in range(pd):
        res_ref[d] = gath[0, my_c, d] - drop_rows[:, d * nport:(d + 1) * nport]

    wait_on(far_send.at[:, :, rest], send_sem.at[0])
    wait_on(gath.at[:, pl.ds(1, nq - 1)], send_sem.at[1])
    wait_on(gram_recv.at[:, others], send_sem.at[2])
    wait_on(ask_send.at[rest], send_sem.at[3])


def emit(*refs):
    count = len(refs) // 2
    sems = refs[-1]
    copies = [
        pltpu.make_async_copy(refs[i], refs[count + i], sems.at[i]) for i in range(count)
    ]
    for copy in copies:
        copy.start()
    for copy in copies:
        copy.wait()


def local(
    comp_type,
    stiffness,
    near_port,
    far_owner,
    far_port,
    bubble_load,
    port_load,
    bubble_inverse,
    coupling,
    port_block,
):
    npy = lax.axis_size("py")
    parts = lax.axis_size("px") * npy
    nq = lax.axis_size("case")
    ncomp = comp_type.shape[0]
    modes, ncase, _ = bubble_load.shape
    pd, _, nport = port_load.shape
    kinds = bubble_inverse.shape[0]
    cap = 3 * ncomp // (2 * parts)
    depth = -(-cap // 8) * 8
    allcase = nq * ncase
    width = 128 if (ncase * pd) % 128 == 0 else ncase * pd
    chunks = ncase * pd // width
    fold = max(1, 128 // allcase)
    vmem = pl.BlockSpec(memory_space=pltpu.VMEM)
    hbm = pl.BlockSpec(memory_space=pltpu.HBM)

    def body(*refs):
        kernel((parts, npy, nq, depth, width, chunks, fold), *refs)

    shapes = (
        jax.ShapeDtypeStruct(port_load.shape, F32),
        jax.ShapeDtypeStruct(port_load.shape, F32),
        jax.ShapeDtypeStruct(bubble_load.shape, F32),
    )
    results = pl.pallas_call(
        body,
        out_shape=shapes,
        in_specs=[hbm] * 10,
        out_specs=(vmem, vmem, vmem),
        scratch_shapes=[
            pltpu.VMEM((1, ncomp), jnp.int32),
            pltpu.VMEM((1, ncomp), jnp.int32),
            pltpu.VMEM((1, ncomp), jnp.int32),
            pltpu.VMEM((1, ncomp), jnp.int32),
            pltpu.VMEM((1, ncomp), F32),
            pltpu.VMEM(bubble_load.shape, F32),
            pltpu.VMEM(port_load.shape, F32),
            pltpu.VMEM(bubble_inverse.shape, F32),
            pltpu.VMEM((kinds, modes, 2 * pd), F32),
            pltpu.VMEM(port_block.shape, F32),
            pltpu.VMEM((parts, 1, 3 * ncomp), F32),
            pltpu.VMEM((parts, 1, 3 * ncomp), F32),
            pltpu.VMEM((5, chunks, parts, depth, width), F32),
            pltpu.VMEM((5, chunks, parts, depth, width), F32),
            pltpu.VMEM((5, nq, pd, ncase, nport), F32),
            pltpu.VMEM((pd, ncase, nport), F32),
            pltpu.VMEM((5 * allcase, pd * nport), BF16),
            pltpu.VMEM((5 * allcase, pd * nport), BF16),
            pltpu.VMEM((4, ncase // fold, fold * allcase), F32),
            pltpu.VMEM((4, nq * parts, ncase // fold, fold * allcase), F32),
            pltpu.VMEM((modes, ncase * ncomp), F32),
            pltpu.VMEM((pd, ncase, nport), F32),
            pltpu.SemaphoreType.DMA((10,)),
            pltpu.SemaphoreType.DMA((4,)),
            pltpu.SemaphoreType.DMA((1 + 5 * chunks,)),
            pltpu.SemaphoreType.DMA((5, nq)),
            pltpu.SemaphoreType.DMA((4,)),
        ],
        compiler_params=pltpu.CompilerParams(
            collective_id=0, has_side_effects=True, vmem_limit_bytes=32 * 1024 * 1024
        ),
        name="condensed_solve",
    )(
        *(
            pltpu.with_memory_space_constraint(x, pltpu.HBM)
            for x in (
                comp_type.reshape(1, ncomp),
                near_port.reshape(1, ncomp),
                far_owner.reshape(1, ncomp),
                far_port.reshape(1, ncomp),
                stiffness.reshape(1, ncomp),
                bubble_load,
                port_load,
                bubble_inverse,
                jnp.swapaxes(coupling, 1, 2),
                port_block,
            )
        )
    )
    return pl.pallas_call(
        emit,
        out_shape=shapes,
        in_specs=[vmem] * 3,
        out_specs=(hbm, hbm, hbm),
        scratch_shapes=[pltpu.SemaphoreType.DMA((3,))],
        compiler_params=pltpu.CompilerParams(vmem_limit_bytes=4 * 1024 * 1024),
        name="emit",
    )(*results)


def solution(mesh):
    placed = (
        P(("px", "py")),
        P(("px", "py")),
        P(("px", "py")),
        P(("px", "py"), None),
        P(("px", "py")),
        P(None, "case", ("px", "py")),
        P(None, "case", ("px", "py")),
        P(),
        P(),
        P(),
    )
    return jax.shard_map(
        local,
        mesh=mesh,
        in_specs=placed,
        out_specs=(
            P(None, "case", ("px", "py")),
            P(None, "case", ("px", "py")),
            P(None, "case", ("px", "py")),
        ),
        check_vma=False,
    )
```

```python
import jax
import jax.numpy as jnp
from jax import lax
from jax.experimental import pallas as pl
from jax.experimental.pallas import tpu as pltpu
from jax.sharding import PartitionSpec as P

HIGH = lax.Precision.HIGHEST
F32 = jnp.float32
BF16 = jnp.bfloat16
MESH = pl.DeviceIdType.MESH
NT = (((1,), (1,)), ((), ()))
TN = (((0,), (0,)), ((), ()))


def split(x):
    top = x.astype(BF16)
    return top, (x - top.astype(F32)).astype(BF16)


def mm(a, b):
    return jnp.dot(a, b, preferred_element_type=F32)


def exact(a, b, dims=(((1,), (0,)), ((), ()))):
    return lax.dot_general(a, b, dims, precision=HIGH, preferred_element_type=F32)


def gauss_solve(matrix, target):
    n = matrix.shape[0]
    aug = jnp.concatenate([matrix, target], axis=1)
    rows = lax.broadcasted_iota(jnp.int32, aug.shape, 0)
    for j in range(0, n, 2):
        row0, row1 = aug[j:j + 1, :], aug[j + 1:j + 2, :]
        col0 = jnp.broadcast_to(aug[:, j:j + 1], aug.shape)
        col1 = jnp.broadcast_to(aug[:, j + 1:j + 2], aug.shape)
        a, c = col0[j:j + 1, :], col0[j + 1:j + 2, :]
        b, d = col1[j:j + 1, :], col1[j + 1:j + 2, :]
        scale = 1.0 / (a * d - b * c)
        new0 = (d * row0 - b * row1) * scale
        new1 = (a * row1 - c * row0) * scale
        rest = aug - col0 * new0 - col1 * new1
        aug = jnp.where(rows == j, new0, jnp.where(rows == j + 1, new1, rest))
    return aug[:, n:]


def kernel(
    sizes,
    kind_hbm,
    near_hbm,
    owner_hbm,
    far_hbm,
    stiff_hbm,
    bload_hbm,
    pload_hbm,
    binv_hbm,
    coup_hbm,
    pblock_hbm,
    sol_ref,
    res_ref,
    bub_ref,
    kind_ref,
    near_ref,
    owner_ref,
    far_ref,
    stiff_ref,
    bload_ref,
    pload_ref,
    binv_ref,
    coup_ref,
    pblock_ref,
    ask_send,
    ask_recv,
    far_send,
    far_recv,
    gath,
    bent_rows,
    rows_top,
    rows_low,
    gram_send,
    gram_recv,
    inv_keep,
    nat_far,
    in_sem,
    send_sem,
    part_rsem,
    case_rsem,
    gram_rsem,
):
    parts, npy, nq, depth, width, chunks, fold = sizes
    my_x, my_y, my_c = lax.axis_index("px"), lax.axis_index("py"), lax.axis_index("case")
    me = my_x * npy + my_y

    def part_id(step):
        other = lax.rem(me + step + parts, parts)
        return (other // npy, lax.rem(other, npy), my_c)

    def case_to(step):
        if nq == 4:
            other = my_c + (step % 2) * (1 - 2 * lax.rem(my_c, 2))
            return other + (step // 2) * (2 - 4 * (my_c // 2))
        return lax.rem(my_c + step, nq)

    def case_from(step):
        return case_to(step) if nq == 4 else lax.rem(my_c + nq - step, nq)

    def case_id(step):
        return (my_x, my_y, case_to(step))

    direct = (1, 2) if nq == 4 else tuple(range(1, nq))

    barrier = pltpu.get_barrier_semaphore()

    order = sorted(range(1, parts), key=lambda i: -min(i % npy, npy - i % npy))

    def each_other(act):
        def per_part(i, _):
            for q in reversed(range(nq)):
                act(i, q)
            return 0

        if parts <= 8:
            for i in order:
                per_part(i, 0)
        else:
            lax.fori_loop(1, parts, per_part, 0)
        for q in reversed(range(1, nq)):
            act(0, q)

    def device(i, q):
        x, y, _ = part_id(i)
        return (x, y, case_to(q))

    def greet_part(i, _):
        pl.semaphore_signal(barrier, inc=1, device_id=part_id(i), device_id_type=MESH)
        return 0

    lax.fori_loop(1, parts, greet_part, 0)
    for i in range(1, nq):
        pl.semaphore_signal(barrier, inc=1, device_id=case_id(i), device_id_type=MESH)

    inputs = (
        (near_hbm, near_ref),
        (owner_hbm, owner_ref),
        (far_hbm, far_ref),
        (kind_hbm, kind_ref),
        (stiff_hbm, stiff_ref),
        (binv_hbm, binv_ref),
        (bload_hbm, bload_ref),
        (coup_hbm, coup_ref),
        (pload_hbm, pload_ref),
        (pblock_hbm, pblock_ref),
    )
    fetches = [
        pltpu.make_async_copy(src, dst, in_sem.at[i]) for i, (src, dst) in enumerate(inputs)
    ]
    for fetch in fetches:
        fetch.start()

    kinds = binv_ref.shape[0]
    modes, ncase, ncomp = bload_ref.shape
    pd = pload_ref.shape[0]
    nport = pload_ref.shape[2]
    slots = parts * depth
    allcase = nq * ncase

    for fetch in fetches[0:5]:
        fetch.wait()
    kind_row = kind_ref[...]
    near_row = near_ref[...]
    owner_row = owner_ref[...]
    far_row = far_ref[...]

    def as_column(row):
        return jnp.broadcast_to(row.astype(F32), (ncomp, ncomp)).T

    sub = lax.broadcasted_iota(jnp.int32, (ncomp, ncomp), 0)
    lane = lax.broadcasted_iota(jnp.int32, (ncomp, ncomp), 1)
    same = (as_column(owner_row) == owner_row.astype(F32)) & (sub < lane)
    rank = jnp.sum(jnp.where(same, 1.0, 0.0), axis=0, keepdims=True).astype(jnp.int32)
    step_row = lax.rem(owner_row - me + parts, parts)
    slot_row = step_row * depth + rank
    slot_sub = lax.broadcasted_iota(jnp.int32, (slots, ncomp), 0)
    slot_pick = jnp.where(slot_sub == slot_row, 1.0, 0.0).astype(BF16)
    step_sub = lax.broadcasted_iota(jnp.int32, (parts, ncomp), 0)
    def send_parts(src, dst, e, sign):
        def body(i, _):
            pltpu.make_async_remote_copy(
                src_ref=src(i),
                dst_ref=dst(i),
                send_sem=send_sem.at[0 if e else 3],
                recv_sem=part_rsem.at[e],
                device_id=part_id(i if sign > 0 else -i),
                device_id_type=MESH,
            ).start()
            return 0

        if parts <= 8:
            for i in order:
                body(i, 0)
        else:
            lax.fori_loop(1, parts, body, 0)

    def wait_on(ref, sem):
        pltpu.make_async_copy(ref, ref, sem).wait()

    rest = pl.ds(1, parts - 1)

    def tile_cases(row):
        return jnp.concatenate([row] * ncase, axis=1)

    def kind_masks(row):
        row = tile_cases(row)
        return [jnp.where(row == t, 1.0, 0.0).astype(BF16) for t in range(kinds)]

    masks = kind_masks(kind_row)

    def table(parts_of):
        top, low = split(parts_of)
        return top, jnp.concatenate([top, low], axis=0)

    def apply_tables(tab, x, masks):
        top, low = split(x)
        lanes = x.shape[1]
        xt = jnp.concatenate([top * m[:, :lanes] for m in masks], axis=0)
        xl = jnp.concatenate([low * m[:, :lanes] for m in masks], axis=0)
        lead = mm(tab[1], xt)
        rows = tab[0].shape[0]
        return lead[:rows] + lead[rows:] + mm(tab[0], xl)

    def wide(field, rows):
        return jnp.concatenate(
            [field[k * rows:(k + 1) * rows] for k in range(field.shape[0] // rows)], axis=1
        )

    def tall(x, count):
        return jnp.concatenate(
            [x[:, k * count:(k + 1) * count] for k in range(x.shape[1] // count)], axis=0
        )

    def pick(x, onehot):
        top, low = split(x)
        return mm(jnp.concatenate([top, low], axis=1), jnp.concatenate([onehot, onehot], axis=0))

    def at_slots(onehot, x):
        top, low = split(x)
        return lax.dot_general(
            jnp.concatenate([onehot, onehot], axis=1),
            jnp.concatenate([top, low], axis=1),
            NT,
            preferred_element_type=F32,
        )

    def place(x, onehot):
        top, low = split(x)
        return mm(top, onehot) + mm(low, onehot)

    def take(e, j):
        wait_on(far_recv.at[e, j, rest], part_rsem.at[1 + e * chunks + j])
        return far_recv[e, j].reshape(slots, width).T

    def post(e, j, out, sign):
        far_send[e, j] = out
        far_recv[e, j, 0] = out[0]
        send_parts(
            lambda i: far_send.at[e, j, i], lambda i: far_recv.at[e, j, i], 1 + e * chunks + j, sign
        )

    cuts = [0] + [((j + 1) * width) // pd for j in range(chunks)]

    def span(f, j):
        if f in (1, 2):
            return pl.ds(cuts[j] * pd, (cuts[j + 1] - cuts[j]) * pd)
        return pl.ds(j * width, width)

    def send_case(f, j, block, sem, step):
        pltpu.make_async_remote_copy(
            src_ref=block,
            dst_ref=block,
            send_sem=send_sem.at[1],
            recv_sem=case_rsem.at[f, j, sem],
            device_id=case_id(step),
            device_id_type=MESH,
        ).start()

    def publish(f, j, rows):
        gath[f, my_c, span(f, j)] = rows
        for i in reversed(direct):
            send_case(f, j, gath.at[f, my_c, span(f, j)], i, i)

    def forward(f, *pieces):
        if nq == 4:
            for j in pieces or range(chunks):
                block = gath.at[f, case_from(2), span(f, j)]
                wait_on(block, case_rsem.at[f, j, 2])
                send_case(f, j, block, 3, 1)

    def lines(ref, d):
        return ref[pl.ds(d, ncase, stride=pd), :]

    def collect(f):
        for i in range(1, nq):
            if nq != 4 or i != 2:
                for j in range(chunks):
                    wait_on(gath.at[f, case_from(i), span(f, j)], case_rsem.at[f, j, i])

        def body(d, _):
            cols = pl.ds(pl.multiple_of(d * nport, nport), nport)
            block = jnp.concatenate([lines(gath.at[f, q], d) for q in range(nq)], axis=0)
            top, low = split(block)
            rows_top[f * allcase:(f + 1) * allcase, cols] = top
            rows_low[f * allcase:(f + 1) * allcase, cols] = low
            return 0

        lax.fori_loop(0, pd, body, 0, unroll=4)

    def against(x, f):
        top, low = split(x)
        band = slice(f * allcase, (f + 1) * allcase)
        lead = lax.dot_general(
            jnp.concatenate([top, low], axis=0),
            rows_top[band, :],
            NT,
            preferred_element_type=F32,
        )
        low_lead = lax.dot_general(
            jnp.concatenate([top, low], axis=0),
            rows_low[band, :],
            NT,
            preferred_element_type=F32,
        )
        total = lead + low_lead
        return total[:x.shape[0]] + total[x.shape[0]:]

    def own_rows(f):
        return jnp.concatenate([lines(gath.at[f, my_c], d) for d in range(pd)], axis=1)

    def gram_out(s, block):
        high = ncase // fold
        folded = jnp.concatenate([block[r * high:(r + 1) * high] for r in range(fold)], axis=1)
        gram_send[s] = folded
        gram_recv[s, my_c * parts] = folded

        def send(i, q):
            pltpu.make_async_remote_copy(
                src_ref=gram_send.at[s],
                dst_ref=gram_recv.at[s, my_c * parts + i],
                send_sem=send_sem.at[2],
                recv_sem=gram_rsem.at[s],
                device_id=device(i, q),
                device_id_type=MESH,
            ).start()

        each_other(send)

    others = pl.ds(1, nq * parts - 1)

    def gram_in(s):
        wait_on(gram_recv.at[s, others], gram_rsem.at[s])
        rows = []
        for q in range(nq):
            total = jnp.sum(gram_recv[s, q * parts:(q + 1) * parts], axis=0)
            for r in range(fold):
                rows.append(total[:, r * allcase:(r + 1) * allcase])
        return sym(jnp.concatenate(rows, axis=0))

    def sym(g):
        return 0.5 * (g + g.T)

    def part(x, j):
        return x[j * width:(j + 1) * width]

    for fetch in fetches[5:8]:
        fetch.wait()
    inv_tab = table(jnp.concatenate([binv_ref[t] for t in range(kinds)], axis=1))
    coup_tab = table(jnp.concatenate([coup_ref[t].T for t in range(kinds)], axis=1))
    ready = [0] + [-(-((j + 1) * width) // pd) for j in range(chunks)]
    condensed_near, leaving = [], None
    for j in range(chunks):
        a, b = ready[j], ready[j + 1]
        loads = jnp.concatenate([bload_ref[:, k, :] for k in range(a, b)], axis=1)
        lifted = apply_tables(inv_tab, loads, masks)
        inv_keep[:, a * ncomp:b * ncomp] = lifted
        condensed = -apply_tables(coup_tab, lifted, masks)
        condensed_near.append(tall(condensed[:pd], ncomp))
        out = tall(condensed[pd:], ncomp)
        leaving = out if leaving is None else jnp.concatenate([leaving, out], axis=0)
        if j == 0:
            naming = jnp.concatenate(
                [
                    jnp.where(step_sub == step_row, row, 0.0)
                    for row in ((far_row + 1).astype(F32), kind_row.astype(F32), stiff_ref[...])
                ],
                axis=0,
            )
            ranked = jnp.where(sub == rank, 1.0, 0.0)
            wanted = exact(naming, ranked, NT)
            wanted = jnp.concatenate([wanted[r * parts:(r + 1) * parts] for r in range(3)], axis=1)
            wanted = wanted.reshape(parts, 1, 3 * ncomp)
            ask_send[...] = wanted
            ask_recv[0] = wanted[0]
            pl.semaphore_wait(barrier, parts + nq - 2)
            send_parts(lambda i: ask_send.at[i], lambda i: ask_recv.at[i], 0, 1)
        post(0, j, at_slots(slot_pick, part(leaving, j)).reshape(parts, depth, width), 1)
    for fetch in fetches[8:]:
        fetch.wait()
    near_in = jnp.where(sub == near_row, 1.0, 0.0).astype(BF16)
    near_out = jnp.where(lane.astype(F32) == as_column(near_row), 1.0, 0.0).astype(BF16)
    near_slots = lax.dot_general(slot_pick, near_in, NT, preferred_element_type=F32).astype(BF16)

    stiff = tile_cases(stiff_ref[...])
    red_t = [exact(binv_ref[t], coup_ref[t], TN) for t in range(kinds)]
    schur = [pblock_ref[t] - exact(red_t[t], coup_ref[t], TN) for t in range(kinds)]

    def corner(a, b):
        rows, cols = slice(a * pd, (a + 1) * pd), slice(b * pd, (b + 1) * pd)
        return table(jnp.concatenate([schur[t][rows, cols] for t in range(kinds)], axis=1))

    nn_tab, nf_tab, fn_tab, ff_tab = corner(0, 0), corner(0, 1), corner(1, 0), corner(1, 1)
    red_tab = table(jnp.concatenate(red_t, axis=1))
    own = jnp.concatenate([pload_ref[:, k, :] for k in range(ncase)], axis=0)
    own = own + pick(jnp.concatenate(condensed_near, axis=0), near_out)
    wait_on(ask_recv.at[rest], part_rsem.at[0])
    asked = ask_recv[...].reshape(parts, 3 * ncomp)
    ports = jnp.concatenate([asked[:, 0:ncomp]] * (ncomp // parts), axis=0).T
    port_lane = lax.broadcasted_iota(jnp.int32, (depth, nport), 1).astype(F32)
    asked_pick = jnp.concatenate(
        [jnp.where(ports[0:depth, i:i + 1] - 1.0 == port_lane, 1.0, 0.0) for i in range(parts)],
        axis=0,
    ).astype(BF16)

    def slot_line(r):
        return jnp.concatenate(
            [asked[i:i + 1, r * ncomp:r * ncomp + depth] for i in range(parts)], axis=1
        )

    slot_masks = kind_masks(slot_line(1))
    slot_stiff = tile_cases(slot_line(2))

    def scatter(e, j, piece):
        post(e, j, at_slots(asked_pick, piece).reshape(parts, depth, width), -1)

        def rest_of_it():
            post(e + 1, j, at_slots(near_slots, piece).reshape(parts, depth, width), 1)

        return rest_of_it

    def join(a, b):
        return b if a is None else jnp.concatenate([a, b], axis=0)

    def near_side(tab, x, a, b):
        return apply_tables(tab, wide(x, pd), masks) * stiff[:, a * ncomp:b * ncomp]

    def far_side(tab, x, a, b):
        return apply_tables(tab, wide(x, pd), slot_masks) * slot_stiff[:, a * slots:b * slots]

    def near_ports(y):
        return pick(tall(y, ncomp), near_out)

    def far_ports(y):
        return place(tall(y, slots), asked_pick)

    def diagonal(e, field):
        y_near = near_side(nn_tab, pick(field, near_in), 0, ncase)
        far_at = [far_send[e, j].reshape(slots, width).T for j in range(chunks)]
        return y_near, far_side(ff_tab, jnp.concatenate(far_at, axis=0), 0, ncase)

    def take_far_values(e, j):
        return place(take(e, j), slot_pick)

    base = None
    for j in range(chunks):
        piece = part(own, j) + place(take(0, j), asked_pick)
        scatter(1, j, piece)()
        publish(0, j, piece)
        base = join(base, piece)

    y_near, y_far = diagonal(1, base)
    far_base, near_at, first, sent, later = None, None, None, 0, []
    for j in range(chunks):
        a, b = cuts[j], cuts[j + 1]
        if j == chunks - 1:
            forward(0)
        piece = take_far_values(1, j)
        publish(3, j, piece)
        far_base = join(far_base, piece)
        near_at = join(near_at, take(2, j))
        rows = slice(a * pd, b * pd)
        y = y_near[:, a * ncomp:b * ncomp] + near_side(nf_tab, far_base[rows], a, b)
        done = near_ports(y)
        y = y_far[:, a * slots:b * slots] + far_side(fn_tab, near_at[rows], a, b)
        done = done + far_ports(y)
        first = join(first, done)
        while (sent + 1) * width <= b * pd:
            later.append(scatter(3, sent, part(first, sent)))
            sent += 1
        publish(1, j, done)

    y_near, y_far = diagonal(3, first)
    straight = near_ports(y_near) + far_ports(y_far)
    collect(0)
    early = against(jnp.concatenate([own_rows(0), own_rows(1)], axis=0), 0)
    gram_out(1, early[ncase:])
    gram_out(0, early[:ncase])
    forward(3)
    forward(1)
    far_first, crossed = None, None
    for j in range(chunks):
        a, b = cuts[j], cuts[j + 1]
        if j == chunks - 1:
            collect(1)
            gram_out(2, against(own_rows(1), 1))
        piece = take_far_values(3, j)
        far_first = join(far_first, piece)
        crossed = join(crossed, near_ports(near_side(nf_tab, far_first[a * pd:b * pd], a, b)))
        if j == 0:
            for post_near in later:
                post_near()
        if j < chunks - 1:
            publish(4, j, piece)
    bent_rows[...] = straight + 2.0 * crossed
    bent = jnp.concatenate([lines(bent_rows, d) for d in range(pd)], axis=1)
    gram_out(3, against(bent, 1))
    publish(4, chunks - 1, piece)

    n = allcase
    eye = jnp.where(
        lax.broadcasted_iota(jnp.int32, (n, n), 0) == lax.broadcasted_iota(jnp.int32, (n, n), 1),
        1.0,
        0.0,
    )
    near_at = None

    def finish_second(j, near_at):
        a, b = cuts[j], cuts[j + 1]
        rows = slice(a * pd, b * pd)
        near_at = join(near_at, take(4, j))
        y = far_side(fn_tab, near_at[rows], a, b)
        publish(2, j, straight[rows] + crossed[rows] + far_ports(y))
        return near_at

    for j in range(chunks // 2):
        near_at = finish_second(j, near_at)
    g00, g01 = gram_in(0), gram_in(1)
    both = gauss_solve(g01, jnp.concatenate([g00, eye], axis=1))
    mine = jnp.where(
        lax.broadcasted_iota(jnp.int32, (n, ncase), 0)
        == lax.broadcasted_iota(jnp.int32, (n, ncase), 1) + my_c * ncase,
        1.0,
        0.0,
    )
    chosen = exact(jnp.concatenate([both[:, 0:n], g01], axis=0), mine)
    first_step, g01_mine, inverse = chosen[0:n], chosen[n:2 * n], both[:, n:2 * n]
    for j in range(chunks // 2, chunks):
        near_at = finish_second(j, near_at)
    forward(4)
    collect(3)
    g11 = gram_in(2)
    over = exact(inverse, g11)
    side = exact(g11, jnp.concatenate([over, first_step], axis=1))
    collect(4)
    g12 = gram_in(3)
    beta = gauss_solve(g12 - sym(side[:, 0:n]), side[:, n:] - g01_mine)
    alpha = first_step + exact(over, beta)
    coefs = jnp.concatenate([alpha, -beta], axis=0).T
    ctop, clow = split(coefs)
    stack = jnp.concatenate([ctop, clow], axis=0)

    def mix(f):
        band = slice(f * allcase, (f + 2) * allcase)
        lead = mm(stack, rows_top[band, :])
        return lead[0:ncase] + lead[ncase:] + mm(ctop, rows_low[band, :])

    answer_rows = mix(0)
    for d in range(pd):
        sol_ref[d] = answer_rows[:, d * nport:(d + 1) * nport]
    far_rows = mix(3)
    for d in range(pd):
        nat_far[d] = far_rows[:, d * nport:(d + 1) * nport]
    answer = jnp.concatenate([sol_ref[:, k, :] for k in range(ncase)], axis=0)
    near = wide(pick(answer, near_in), pd)
    ends = jnp.concatenate(
        [near, jnp.concatenate([nat_far[:, k, :] for k in range(ncase)], axis=1)], axis=0
    )
    scaled = inv_keep[...] / stiff
    forward(2)
    back = scaled - apply_tables(red_tab, ends, masks)
    for k in range(ncase):
        bub_ref[:, k, :] = back[:, k * ncomp:(k + 1) * ncomp]
    collect(2)
    drop_rows = mix(1)
    for d in range(pd):
        res_ref[d] = lines(gath.at[0, my_c], d) - drop_rows[:, d * nport:(d + 1) * nport]

    wait_on(far_send.at[:, :, rest], send_sem.at[0])
    wait_on(gath.at[:, pl.ds(1, nq - 1)], send_sem.at[1])
    wait_on(gram_recv.at[:, others], send_sem.at[2])
    wait_on(ask_send.at[rest], send_sem.at[3])


def emit(*refs):
    count = len(refs) // 2
    sems = refs[-1]
    copies = [
        pltpu.make_async_copy(refs[i], refs[count + i], sems.at[i]) for i in range(count)
    ]
    for copy in copies:
        copy.start()
    for copy in copies:
        copy.wait()


def local(
    comp_type,
    stiffness,
    near_port,
    far_owner,
    far_port,
    bubble_load,
    port_load,
    bubble_inverse,
    coupling,
    port_block,
):
    npy = lax.axis_size("py")
    parts = lax.axis_size("px") * npy
    nq = lax.axis_size("case")
    ncomp = comp_type.shape[0]
    modes, ncase, _ = bubble_load.shape
    pd, _, nport = port_load.shape
    kinds = bubble_inverse.shape[0]
    cap = 3 * ncomp // (2 * parts)
    depth = -(-cap // 8) * 8
    allcase = nq * ncase
    width = 128 if (ncase * pd) % 128 == 0 else ncase * pd
    chunks = ncase * pd // width
    fold = max(1, 128 // allcase)
    vmem = pl.BlockSpec(memory_space=pltpu.VMEM)
    hbm = pl.BlockSpec(memory_space=pltpu.HBM)

    def body(*refs):
        kernel((parts, npy, nq, depth, width, chunks, fold), *refs)

    shapes = (
        jax.ShapeDtypeStruct(port_load.shape, F32),
        jax.ShapeDtypeStruct(port_load.shape, F32),
        jax.ShapeDtypeStruct(bubble_load.shape, F32),
    )
    results = pl.pallas_call(
        body,
        out_shape=shapes,
        in_specs=[hbm] * 10,
        out_specs=(vmem, vmem, vmem),
        scratch_shapes=[
            pltpu.VMEM((1, ncomp), jnp.int32),
            pltpu.VMEM((1, ncomp), jnp.int32),
            pltpu.VMEM((1, ncomp), jnp.int32),
            pltpu.VMEM((1, ncomp), jnp.int32),
            pltpu.VMEM((1, ncomp), F32),
            pltpu.VMEM(bubble_load.shape, F32),
            pltpu.VMEM(port_load.shape, F32),
            pltpu.VMEM(bubble_inverse.shape, F32),
            pltpu.VMEM((kinds, modes, 2 * pd), F32),
            pltpu.VMEM(port_block.shape, F32),
            pltpu.VMEM((parts, 1, 3 * ncomp), F32),
            pltpu.VMEM((parts, 1, 3 * ncomp), F32),
            pltpu.VMEM((5, chunks, parts, depth, width), F32),
            pltpu.VMEM((5, chunks, parts, depth, width), F32),
            pltpu.VMEM((5, nq, ncase * pd, nport), F32),
            pltpu.VMEM((ncase * pd, nport), F32),
            pltpu.VMEM((5 * allcase, pd * nport), BF16),
            pltpu.VMEM((5 * allcase, pd * nport), BF16),
            pltpu.VMEM((4, ncase // fold, fold * allcase), F32),
            pltpu.VMEM((4, nq * parts, ncase // fold, fold * allcase), F32),
            pltpu.VMEM((modes, ncase * ncomp), F32),
            pltpu.VMEM((pd, ncase, nport), F32),
            pltpu.SemaphoreType.DMA((10,)),
            pltpu.SemaphoreType.DMA((4,)),
            pltpu.SemaphoreType.DMA((1 + 5 * chunks,)),
            pltpu.SemaphoreType.DMA((5, chunks, nq)),
            pltpu.SemaphoreType.DMA((4,)),
        ],
        compiler_params=pltpu.CompilerParams(
            collective_id=0, has_side_effects=True, vmem_limit_bytes=32 * 1024 * 1024
        ),
        name="condensed_solve",
    )(
        *(
            pltpu.with_memory_space_constraint(x, pltpu.HBM)
            for x in (
                comp_type.reshape(1, ncomp),
                near_port.reshape(1, ncomp),
                far_owner.reshape(1, ncomp),
                far_port.reshape(1, ncomp),
                stiffness.reshape(1, ncomp),
                bubble_load,
                port_load,
                bubble_inverse,
                jnp.swapaxes(coupling, 1, 2),
                port_block,
            )
        )
    )
    return pl.pallas_call(
        emit,
        out_shape=shapes,
        in_specs=[vmem] * 3,
        out_specs=(hbm, hbm, hbm),
        scratch_shapes=[pltpu.SemaphoreType.DMA((3,))],
        compiler_params=pltpu.CompilerParams(vmem_limit_bytes=4 * 1024 * 1024),
        name="emit",
    )(*results)


def solution(mesh):
    placed = (
        P(("px", "py")),
        P(("px", "py")),
        P(("px", "py")),
        P(("px", "py"), None),
        P(("px", "py")),
        P(None, "case", ("px", "py")),
        P(None, "case", ("px", "py")),
        P(),
        P(),
        P(),
    )
    return jax.shard_map(
        local,
        mesh=mesh,
        in_specs=placed,
        out_specs=(
            P(None, "case", ("px", "py")),
            P(None, "case", ("px", "py")),
            P(None, "case", ("px", "py")),
        ),
        check_vma=False,
    )
```

```python
import jax
import jax.numpy as jnp
from jax import lax
from jax.experimental import pallas as pl
from jax.experimental.pallas import tpu as pltpu
from jax.sharding import PartitionSpec as P

HIGH = lax.Precision.HIGHEST
F32 = jnp.float32
BF16 = jnp.bfloat16
MESH = pl.DeviceIdType.MESH
NT = (((1,), (1,)), ((), ()))
TN = (((0,), (0,)), ((), ()))


def split(x):
    top = x.astype(BF16)
    return top, (x - top.astype(F32)).astype(BF16)


def mm(a, b):
    return jnp.dot(a, b, preferred_element_type=F32)


def exact(a, b, dims=(((1,), (0,)), ((), ()))):
    return lax.dot_general(a, b, dims, precision=HIGH, preferred_element_type=F32)


def gauss_solve(matrix, target):
    n = matrix.shape[0]
    aug = jnp.concatenate([matrix, target], axis=1)
    rows = lax.broadcasted_iota(jnp.int32, aug.shape, 0)
    for j in range(0, n, 2):
        row0, row1 = aug[j:j + 1, :], aug[j + 1:j + 2, :]
        col0 = jnp.broadcast_to(aug[:, j:j + 1], aug.shape)
        col1 = jnp.broadcast_to(aug[:, j + 1:j + 2], aug.shape)
        a, c = col0[j:j + 1, :], col0[j + 1:j + 2, :]
        b, d = col1[j:j + 1, :], col1[j + 1:j + 2, :]
        scale = 1.0 / (a * d - b * c)
        new0 = (d * row0 - b * row1) * scale
        new1 = (a * row1 - c * row0) * scale
        rest = aug - col0 * new0 - col1 * new1
        aug = jnp.where(rows == j, new0, jnp.where(rows == j + 1, new1, rest))
    return aug[:, n:]


def kernel(
    sizes,
    kind_hbm,
    near_hbm,
    owner_hbm,
    far_hbm,
    stiff_hbm,
    bload_hbm,
    pload_hbm,
    binv_hbm,
    coup_hbm,
    pblock_hbm,
    sol_ref,
    res_ref,
    bub_ref,
    kind_ref,
    near_ref,
    owner_ref,
    far_ref,
    stiff_ref,
    bload_ref,
    pload_ref,
    binv_ref,
    coup_ref,
    pblock_ref,
    ask_send,
    ask_recv,
    far_send,
    far_recv,
    gath,
    bent_rows,
    rows_top,
    rows_low,
    gram_send,
    gram_recv,
    inv_keep,
    nat_far,
    in_sem,
    send_sem,
    part_rsem,
    case_rsem,
    gram_rsem,
):
    parts, npy, nq, depth, width, chunks, fold = sizes
    my_x, my_y, my_c = lax.axis_index("px"), lax.axis_index("py"), lax.axis_index("case")
    me = my_x * npy + my_y

    def part_id(step):
        other = lax.rem(me + step + parts, parts)
        return (other // npy, lax.rem(other, npy), my_c)

    def case_to(step):
        if nq == 4:
            other = my_c + (step % 2) * (1 - 2 * lax.rem(my_c, 2))
            return other + (step // 2) * (2 - 4 * (my_c // 2))
        return lax.rem(my_c + step, nq)

    def case_from(step):
        return case_to(step) if nq == 4 else lax.rem(my_c + nq - step, nq)

    def case_id(step):
        return (my_x, my_y, case_to(step))

    direct = (1, 2) if nq == 4 else tuple(range(1, nq))

    barrier = pltpu.get_barrier_semaphore()

    order = sorted(range(1, parts), key=lambda i: -min(i % npy, npy - i % npy))

    def each_other(act):
        def per_part(i, _):
            for q in reversed(range(nq)):
                act(i, q)
            return 0

        if parts <= 8:
            for i in order:
                per_part(i, 0)
        else:
            lax.fori_loop(1, parts, per_part, 0)
        for q in reversed(range(1, nq)):
            act(0, q)

    def device(i, q):
        x, y, _ = part_id(i)
        return (x, y, case_to(q))

    def greet_part(i, _):
        pl.semaphore_signal(barrier, inc=1, device_id=part_id(i), device_id_type=MESH)
        return 0

    lax.fori_loop(1, parts, greet_part, 0)
    for i in range(1, nq):
        pl.semaphore_signal(barrier, inc=1, device_id=case_id(i), device_id_type=MESH)

    inputs = (
        (near_hbm, near_ref),
        (owner_hbm, owner_ref),
        (far_hbm, far_ref),
        (kind_hbm, kind_ref),
        (stiff_hbm, stiff_ref),
        (binv_hbm, binv_ref),
        (bload_hbm, bload_ref),
        (coup_hbm, coup_ref),
        (pload_hbm, pload_ref),
        (pblock_hbm, pblock_ref),
    )
    fetches = [
        pltpu.make_async_copy(src, dst, in_sem.at[i]) for i, (src, dst) in enumerate(inputs)
    ]
    for fetch in fetches:
        fetch.start()

    kinds = binv_ref.shape[0]
    modes, ncase, ncomp = bload_ref.shape
    pd = pload_ref.shape[0]
    nport = pload_ref.shape[2]
    slots = parts * depth
    allcase = nq * ncase

    for fetch in fetches[0:8]:
        fetch.wait()
    kind_row = kind_ref[...]
    near_row = near_ref[...]
    owner_row = owner_ref[...]
    far_row = far_ref[...]

    def as_column(row):
        return jnp.broadcast_to(row.astype(F32), (ncomp, ncomp)).T

    sub = lax.broadcasted_iota(jnp.int32, (ncomp, ncomp), 0)
    lane = lax.broadcasted_iota(jnp.int32, (ncomp, ncomp), 1)
    same = (as_column(owner_row) == owner_row.astype(F32)) & (sub < lane)
    rank = jnp.sum(jnp.where(same, 1.0, 0.0), axis=0, keepdims=True).astype(jnp.int32)
    step_row = lax.rem(owner_row - me + parts, parts)
    slot_row = step_row * depth + rank
    slot_sub = lax.broadcasted_iota(jnp.int32, (slots, ncomp), 0)
    slot_pick = jnp.where(slot_sub == slot_row, 1.0, 0.0).astype(BF16)
    step_sub = lax.broadcasted_iota(jnp.int32, (parts, ncomp), 0)
    def send_parts(src, dst, e, sign):
        def body(i, _):
            pltpu.make_async_remote_copy(
                src_ref=src(i),
                dst_ref=dst(i),
                send_sem=send_sem.at[0 if e else 3],
                recv_sem=part_rsem.at[e],
                device_id=part_id(i if sign > 0 else -i),
                device_id_type=MESH,
            ).start()
            return 0

        if parts <= 8:
            for i in order:
                body(i, 0)
        else:
            lax.fori_loop(1, parts, body, 0)

    def wait_on(ref, sem):
        pltpu.make_async_copy(ref, ref, sem).wait()

    rest = pl.ds(1, parts - 1)

    def tile_cases(row):
        return jnp.concatenate([row] * ncase, axis=1)

    def kind_masks(row):
        row = tile_cases(row)
        return [jnp.where(row == t, 1.0, 0.0).astype(BF16) for t in range(kinds)]

    masks = kind_masks(kind_row)

    def table(parts_of):
        top, low = split(parts_of)
        return top, jnp.concatenate([top, low], axis=0)

    def apply_tables(tab, x, masks):
        top, low = split(x)
        lanes = x.shape[1]
        xt = jnp.concatenate([top * m[:, :lanes] for m in masks], axis=0)
        xl = jnp.concatenate([low * m[:, :lanes] for m in masks], axis=0)
        lead = mm(tab[1], xt)
        rows = tab[0].shape[0]
        return lead[:rows] + lead[rows:] + mm(tab[0], xl)

    def wide(field, rows):
        return jnp.concatenate(
            [field[k * rows:(k + 1) * rows] for k in range(field.shape[0] // rows)], axis=1
        )

    def tall(x, count):
        return jnp.concatenate(
            [x[:, k * count:(k + 1) * count] for k in range(x.shape[1] // count)], axis=0
        )

    def pick(x, onehot):
        top, low = split(x)
        return mm(jnp.concatenate([top, low], axis=1), jnp.concatenate([onehot, onehot], axis=0))

    def at_slots(onehot, x):
        top, low = split(x)
        return lax.dot_general(
            jnp.concatenate([onehot, onehot], axis=1),
            jnp.concatenate([top, low], axis=1),
            NT,
            preferred_element_type=F32,
        )

    def place(x, onehot):
        top, low = split(x)
        return mm(top, onehot) + mm(low, onehot)

    def take(e, j):
        wait_on(far_recv.at[e, j, rest], part_rsem.at[1 + e * chunks + j])
        return far_recv[e, j].reshape(slots, width).T

    def post(e, j, out, sign):
        far_send[e, j] = out
        far_recv[e, j, 0] = out[0]
        send_parts(
            lambda i: far_send.at[e, j, i], lambda i: far_recv.at[e, j, i], 1 + e * chunks + j, sign
        )

    cuts = [0] + [((j + 1) * width) // pd for j in range(chunks)]

    def span(f, j):
        if f in (1, 2):
            return pl.ds(cuts[j] * pd, (cuts[j + 1] - cuts[j]) * pd)
        return pl.ds(j * width, width)

    def send_case(f, j, block, sem, step):
        pltpu.make_async_remote_copy(
            src_ref=block,
            dst_ref=block,
            send_sem=send_sem.at[1],
            recv_sem=case_rsem.at[f, j, sem],
            device_id=case_id(step),
            device_id_type=MESH,
        ).start()

    def publish(f, j, rows):
        gath[f, my_c, span(f, j)] = rows
        for i in reversed(direct):
            send_case(f, j, gath.at[f, my_c, span(f, j)], i, i)

    def forward(f, *pieces):
        if nq == 4:
            for j in pieces or range(chunks):
                block = gath.at[f, case_from(2), span(f, j)]
                wait_on(block, case_rsem.at[f, j, 2])
                send_case(f, j, block, 3, 1)

    def lines(ref, d):
        return ref[pl.ds(d, ncase, stride=pd), :]

    def collect(f):
        for i in range(1, nq):
            if nq != 4 or i != 2:
                for j in range(chunks):
                    wait_on(gath.at[f, case_from(i), span(f, j)], case_rsem.at[f, j, i])

        def body(d, _):
            cols = pl.ds(pl.multiple_of(d * nport, nport), nport)
            block = jnp.concatenate([lines(gath.at[f, q], d) for q in range(nq)], axis=0)
            top, low = split(block)
            rows_top[f * allcase:(f + 1) * allcase, cols] = top
            rows_low[f * allcase:(f + 1) * allcase, cols] = low
            return 0

        lax.fori_loop(0, pd, body, 0, unroll=4)

    def against(x, f):
        top, low = split(x)
        band = slice(f * allcase, (f + 1) * allcase)
        lead = lax.dot_general(
            jnp.concatenate([top, low], axis=0),
            rows_top[band, :],
            NT,
            preferred_element_type=F32,
        )
        low_lead = lax.dot_general(
            jnp.concatenate([top, low], axis=0),
            rows_low[band, :],
            NT,
            preferred_element_type=F32,
        )
        total = lead + low_lead
        return total[:x.shape[0]] + total[x.shape[0]:]

    def own_rows(f):
        return jnp.concatenate([lines(gath.at[f, my_c], d) for d in range(pd)], axis=1)

    def gram_out(s, block):
        high = block.shape[0] // fold
        folded = jnp.concatenate([block[r * high:(r + 1) * high] for r in range(fold)], axis=1)
        gram_send[s] = folded
        gram_recv[s, my_c * parts] = folded

        def send(i, q):
            pltpu.make_async_remote_copy(
                src_ref=gram_send.at[s],
                dst_ref=gram_recv.at[s, my_c * parts + i],
                send_sem=send_sem.at[2],
                recv_sem=gram_rsem.at[s],
                device_id=device(i, q),
                device_id_type=MESH,
            ).start()

        each_other(send)

    others = pl.ds(1, nq * parts - 1)

    def gram_in(s):
        wait_on(gram_recv.at[s, others], gram_rsem.at[s])
        blocks = []
        for q in range(nq):
            total = jnp.sum(gram_recv[s, q * parts:(q + 1) * parts], axis=0)
            blocks.append(
                jnp.concatenate(
                    [total[:, r * allcase:(r + 1) * allcase] for r in range(fold)], axis=0
                )
            )
        return (
            sym(jnp.concatenate([block[:ncase] for block in blocks], axis=0)),
            sym(jnp.concatenate([block[ncase:] for block in blocks], axis=0)),
        )

    def sym(g):
        return 0.5 * (g + g.T)

    def part(x, j):
        return x[j * width:(j + 1) * width]

    inv_tab = table(jnp.concatenate([binv_ref[t] for t in range(kinds)], axis=1))
    coup_tab = table(jnp.concatenate([coup_ref[t].T for t in range(kinds)], axis=1))
    ready = [0] + [-(-((j + 1) * width) // pd) for j in range(chunks)]
    condensed_near, leaving = [], None
    for j in range(chunks):
        a, b = ready[j], ready[j + 1]
        loads = jnp.concatenate([bload_ref[:, k, :] for k in range(a, b)], axis=1)
        lifted = apply_tables(inv_tab, loads, masks)
        inv_keep[:, a * ncomp:b * ncomp] = lifted
        condensed = -apply_tables(coup_tab, lifted, masks)
        condensed_near.append(tall(condensed[:pd], ncomp))
        out = tall(condensed[pd:], ncomp)
        leaving = out if leaving is None else jnp.concatenate([leaving, out], axis=0)
        if j == 0:
            naming = jnp.concatenate(
                [
                    jnp.where(step_sub == step_row, row, 0.0)
                    for row in ((far_row + 1).astype(F32), kind_row.astype(F32), stiff_ref[...])
                ],
                axis=0,
            )
            ranked = jnp.where(sub == rank, 1.0, 0.0)
            wanted = exact(naming, ranked, NT)
            wanted = jnp.concatenate([wanted[r * parts:(r + 1) * parts] for r in range(3)], axis=1)
            wanted = wanted.reshape(parts, 1, 3 * ncomp)
            ask_send[...] = wanted
            ask_recv[0] = wanted[0]
            pl.semaphore_wait(barrier, parts + nq - 2)
            send_parts(lambda i: ask_send.at[i], lambda i: ask_recv.at[i], 0, 1)
        post(0, j, at_slots(slot_pick, part(leaving, j)).reshape(parts, depth, width), 1)
    for fetch in fetches[8:]:
        fetch.wait()
    near_in = jnp.where(sub == near_row, 1.0, 0.0).astype(BF16)
    near_out = jnp.where(lane.astype(F32) == as_column(near_row), 1.0, 0.0).astype(BF16)
    near_slots = lax.dot_general(slot_pick, near_in, NT, preferred_element_type=F32).astype(BF16)

    stiff = tile_cases(stiff_ref[...])
    red_t = [exact(binv_ref[t], coup_ref[t], TN) for t in range(kinds)]
    schur = [pblock_ref[t] - exact(red_t[t], coup_ref[t], TN) for t in range(kinds)]

    def corner(a, b):
        rows, cols = slice(a * pd, (a + 1) * pd), slice(b * pd, (b + 1) * pd)
        return table(jnp.concatenate([schur[t][rows, cols] for t in range(kinds)], axis=1))

    nn_tab, nf_tab, fn_tab, ff_tab = corner(0, 0), corner(0, 1), corner(1, 0), corner(1, 1)
    red_tab = table(jnp.concatenate(red_t, axis=1))
    own = jnp.concatenate([pload_ref[:, k, :] for k in range(ncase)], axis=0)
    own = own + pick(jnp.concatenate(condensed_near, axis=0), near_out)
    wait_on(ask_recv.at[rest], part_rsem.at[0])
    asked = ask_recv[...].reshape(parts, 3 * ncomp)
    ports = jnp.concatenate([asked[:, 0:ncomp]] * (ncomp // parts), axis=0).T
    port_lane = lax.broadcasted_iota(jnp.int32, (depth, nport), 1).astype(F32)
    asked_pick = jnp.concatenate(
        [jnp.where(ports[0:depth, i:i + 1] - 1.0 == port_lane, 1.0, 0.0) for i in range(parts)],
        axis=0,
    ).astype(BF16)

    def slot_line(r):
        return jnp.concatenate(
            [asked[i:i + 1, r * ncomp:r * ncomp + depth] for i in range(parts)], axis=1
        )

    slot_masks = kind_masks(slot_line(1))
    slot_stiff = tile_cases(slot_line(2))

    def scatter(e, j, piece):
        post(e, j, at_slots(asked_pick, piece).reshape(parts, depth, width), -1)

        def rest_of_it():
            post(e + 1, j, at_slots(near_slots, piece).reshape(parts, depth, width), 1)

        return rest_of_it

    def join(a, b):
        return b if a is None else jnp.concatenate([a, b], axis=0)

    def near_side(tab, x, a, b):
        return apply_tables(tab, wide(x, pd), masks) * stiff[:, a * ncomp:b * ncomp]

    def far_side(tab, x, a, b):
        return apply_tables(tab, wide(x, pd), slot_masks) * slot_stiff[:, a * slots:b * slots]

    def near_ports(y):
        return pick(tall(y, ncomp), near_out)

    def far_ports(y):
        return place(tall(y, slots), asked_pick)

    def diagonal(e, field):
        y_near = near_side(nn_tab, pick(field, near_in), 0, ncase)
        far_at = [far_send[e, j].reshape(slots, width).T for j in range(chunks)]
        return y_near, far_side(ff_tab, jnp.concatenate(far_at, axis=0), 0, ncase)

    def take_far_values(e, j):
        return place(take(e, j), slot_pick)

    base = None
    for j in range(chunks):
        piece = part(own, j) + place(take(0, j), asked_pick)
        scatter(1, j, piece)()
        publish(0, j, piece)
        base = join(base, piece)

    y_near, y_far = diagonal(1, base)
    far_base, near_at, first, sent, later = None, None, None, 0, []
    for j in range(chunks):
        a, b = cuts[j], cuts[j + 1]
        if j == chunks - 1:
            forward(0)
        piece = take_far_values(1, j)
        publish(3, j, piece)
        far_base = join(far_base, piece)
        near_at = join(near_at, take(2, j))
        rows = slice(a * pd, b * pd)
        y = y_near[:, a * ncomp:b * ncomp] + near_side(nf_tab, far_base[rows], a, b)
        done = near_ports(y)
        y = y_far[:, a * slots:b * slots] + far_side(fn_tab, near_at[rows], a, b)
        done = done + far_ports(y)
        first = join(first, done)
        while (sent + 1) * width <= b * pd:
            later.append(scatter(3, sent, part(first, sent)))
            sent += 1
        publish(1, j, done)

    y_near, y_far = diagonal(3, first)
    straight = near_ports(y_near) + far_ports(y_far)
    collect(0)
    gram_out(0, against(jnp.concatenate([own_rows(0), own_rows(1)], axis=0), 0))
    far_first, crossed = None, None
    for j in range(chunks):
        a, b = cuts[j], cuts[j + 1]
        if j == chunks - 1:
            forward(1)
            forward(3)
            collect(1)
        piece = take_far_values(3, j)
        far_first = join(far_first, piece)
        crossed = join(crossed, near_ports(near_side(nf_tab, far_first[a * pd:b * pd], a, b)))
        if j < chunks - 1:
            later[j]()
            publish(4, j, piece)
    bent_rows[...] = straight + 2.0 * crossed
    bent = jnp.concatenate([lines(bent_rows, d) for d in range(pd)], axis=1)
    gram_out(1, against(jnp.concatenate([own_rows(1), bent], axis=0), 1))
    later[chunks - 1]()
    publish(4, chunks - 1, piece)

    n = allcase
    eye = jnp.where(
        lax.broadcasted_iota(jnp.int32, (n, n), 0) == lax.broadcasted_iota(jnp.int32, (n, n), 1),
        1.0,
        0.0,
    )
    near_at = None

    def finish_second(j, near_at):
        a, b = cuts[j], cuts[j + 1]
        rows = slice(a * pd, b * pd)
        near_at = join(near_at, take(4, j))
        y = far_side(fn_tab, near_at[rows], a, b)
        publish(2, j, straight[rows] + crossed[rows] + far_ports(y))
        return near_at

    g00, g01 = gram_in(0)
    both = gauss_solve(g01, jnp.concatenate([g00, eye], axis=1))
    mine = jnp.where(
        lax.broadcasted_iota(jnp.int32, (n, ncase), 0)
        == lax.broadcasted_iota(jnp.int32, (n, ncase), 1) + my_c * ncase,
        1.0,
        0.0,
    )
    chosen = exact(jnp.concatenate([both[:, 0:n], g01], axis=0), mine)
    first_step, g01_mine, inverse = chosen[0:n], chosen[n:2 * n], both[:, n:2 * n]
    for j in range(chunks):
        near_at = finish_second(j, near_at)
    forward(4)
    collect(3)
    g11, g12 = gram_in(1)
    over = exact(inverse, g11)
    side = exact(g11, jnp.concatenate([over, first_step], axis=1))
    beta = gauss_solve(g12 - sym(side[:, 0:n]), side[:, n:] - g01_mine)
    alpha = first_step + exact(over, beta)
    coefs = jnp.concatenate([alpha, -beta], axis=0).T
    ctop, clow = split(coefs)
    stack = jnp.concatenate([ctop, clow], axis=0)

    def mix(f):
        band = slice(f * allcase, (f + 2) * allcase)
        lead = mm(stack, rows_top[band, :])
        return lead[0:ncase] + lead[ncase:] + mm(ctop, rows_low[band, :])

    answer_rows = mix(0)
    for d in range(pd):
        sol_ref[d] = answer_rows[:, d * nport:(d + 1) * nport]
    collect(4)
    far_rows = mix(3)
    forward(2)
    for d in range(pd):
        nat_far[d] = far_rows[:, d * nport:(d + 1) * nport]
    answer = jnp.concatenate([sol_ref[:, k, :] for k in range(ncase)], axis=0)
    near = wide(pick(answer, near_in), pd)
    ends = jnp.concatenate(
        [near, jnp.concatenate([nat_far[:, k, :] for k in range(ncase)], axis=1)], axis=0
    )
    scaled = inv_keep[...] / stiff
    back = scaled - apply_tables(red_tab, ends, masks)
    for k in range(ncase):
        bub_ref[:, k, :] = back[:, k * ncomp:(k + 1) * ncomp]
    collect(2)
    drop_rows = mix(1)
    for d in range(pd):
        res_ref[d] = lines(gath.at[0, my_c], d) - drop_rows[:, d * nport:(d + 1) * nport]

    wait_on(far_send.at[:, :, rest], send_sem.at[0])
    wait_on(gath.at[:, pl.ds(1, nq - 1)], send_sem.at[1])
    wait_on(gram_recv.at[:, others], send_sem.at[2])
    wait_on(ask_send.at[rest], send_sem.at[3])


def emit(*refs):
    count = len(refs) // 2
    sems = refs[-1]
    copies = [
        pltpu.make_async_copy(refs[i], refs[count + i], sems.at[i]) for i in range(count)
    ]
    for copy in copies:
        copy.start()
    for copy in copies:
        copy.wait()


def local(
    comp_type,
    stiffness,
    near_port,
    far_owner,
    far_port,
    bubble_load,
    port_load,
    bubble_inverse,
    coupling,
    port_block,
):
    npy = lax.axis_size("py")
    parts = lax.axis_size("px") * npy
    nq = lax.axis_size("case")
    ncomp = comp_type.shape[0]
    modes, ncase, _ = bubble_load.shape
    pd, _, nport = port_load.shape
    kinds = bubble_inverse.shape[0]
    cap = 3 * ncomp // (2 * parts)
    depth = -(-cap // 8) * 8
    allcase = nq * ncase
    width = 128 if (ncase * pd) % 128 == 0 else ncase * pd
    chunks = ncase * pd // width
    fold = max(1, 128 // allcase)
    vmem = pl.BlockSpec(memory_space=pltpu.VMEM)
    hbm = pl.BlockSpec(memory_space=pltpu.HBM)

    def body(*refs):
        kernel((parts, npy, nq, depth, width, chunks, fold), *refs)

    shapes = (
        jax.ShapeDtypeStruct(port_load.shape, F32),
        jax.ShapeDtypeStruct(port_load.shape, F32),
        jax.ShapeDtypeStruct(bubble_load.shape, F32),
    )
    results = pl.pallas_call(
        body,
        out_shape=shapes,
        in_specs=[hbm] * 10,
        out_specs=(vmem, vmem, vmem),
        scratch_shapes=[
            pltpu.VMEM((1, ncomp), jnp.int32),
            pltpu.VMEM((1, ncomp), jnp.int32),
            pltpu.VMEM((1, ncomp), jnp.int32),
            pltpu.VMEM((1, ncomp), jnp.int32),
            pltpu.VMEM((1, ncomp), F32),
            pltpu.VMEM(bubble_load.shape, F32),
            pltpu.VMEM(port_load.shape, F32),
            pltpu.VMEM(bubble_inverse.shape, F32),
            pltpu.VMEM((kinds, modes, 2 * pd), F32),
            pltpu.VMEM(port_block.shape, F32),
            pltpu.VMEM((parts, 1, 3 * ncomp), F32),
            pltpu.VMEM((parts, 1, 3 * ncomp), F32),
            pltpu.VMEM((5, chunks, parts, depth, width), F32),
            pltpu.VMEM((5, chunks, parts, depth, width), F32),
            pltpu.VMEM((5, nq, ncase * pd, nport), F32),
            pltpu.VMEM((ncase * pd, nport), F32),
            pltpu.VMEM((5 * allcase, pd * nport), BF16),
            pltpu.VMEM((5 * allcase, pd * nport), BF16),
            pltpu.VMEM((2, 2 * ncase // fold, fold * allcase), F32),
            pltpu.VMEM((2, nq * parts, 2 * ncase // fold, fold * allcase), F32),
            pltpu.VMEM((modes, ncase * ncomp), F32),
            pltpu.VMEM((pd, ncase, nport), F32),
            pltpu.SemaphoreType.DMA((10,)),
            pltpu.SemaphoreType.DMA((4,)),
            pltpu.SemaphoreType.DMA((1 + 5 * chunks,)),
            pltpu.SemaphoreType.DMA((5, chunks, nq)),
            pltpu.SemaphoreType.DMA((2,)),
        ],
        compiler_params=pltpu.CompilerParams(
            collective_id=0, has_side_effects=True, vmem_limit_bytes=32 * 1024 * 1024
        ),
        name="condensed_solve",
    )(
        *(
            pltpu.with_memory_space_constraint(x, pltpu.HBM)
            for x in (
                comp_type.reshape(1, ncomp),
                near_port.reshape(1, ncomp),
                far_owner.reshape(1, ncomp),
                far_port.reshape(1, ncomp),
                stiffness.reshape(1, ncomp),
                bubble_load,
                port_load,
                bubble_inverse,
                jnp.swapaxes(coupling, 1, 2),
                port_block,
            )
        )
    )
    return pl.pallas_call(
        emit,
        out_shape=shapes,
        in_specs=[vmem] * 3,
        out_specs=(hbm, hbm, hbm),
        scratch_shapes=[pltpu.SemaphoreType.DMA((3,))],
        compiler_params=pltpu.CompilerParams(vmem_limit_bytes=4 * 1024 * 1024),
        name="emit",
    )(*results)


def solution(mesh):
    placed = (
        P(("px", "py")),
        P(("px", "py")),
        P(("px", "py")),
        P(("px", "py"), None),
        P(("px", "py")),
        P(None, "case", ("px", "py")),
        P(None, "case", ("px", "py")),
        P(),
        P(),
        P(),
    )
    return jax.shard_map(
        local,
        mesh=mesh,
        in_specs=placed,
        out_specs=(
            P(None, "case", ("px", "py")),
            P(None, "case", ("px", "py")),
            P(None, "case", ("px", "py")),
        ),
        check_vma=False,
    )
```

```python
import jax
import jax.numpy as jnp
from jax import lax
from jax.experimental import pallas as pl
from jax.experimental.pallas import tpu as pltpu
from jax.sharding import PartitionSpec as P

HIGH = lax.Precision.HIGHEST
F32 = jnp.float32
BF16 = jnp.bfloat16
MESH = pl.DeviceIdType.MESH
NT = (((1,), (1,)), ((), ()))
TN = (((0,), (0,)), ((), ()))


def split(x):
    top = x.astype(BF16)
    return top, (x - top.astype(F32)).astype(BF16)


def mm(a, b):
    return jnp.dot(a, b, preferred_element_type=F32)


def exact(a, b, dims=(((1,), (0,)), ((), ()))):
    return lax.dot_general(a, b, dims, precision=HIGH, preferred_element_type=F32)


def gauss_solve(matrix, target):
    n = matrix.shape[0]
    aug = jnp.concatenate([matrix, target], axis=1)
    rows = lax.broadcasted_iota(jnp.int32, aug.shape, 0)
    for j in range(0, n, 2):
        row0, row1 = aug[j:j + 1, :], aug[j + 1:j + 2, :]
        col0 = jnp.broadcast_to(aug[:, j:j + 1], aug.shape)
        col1 = jnp.broadcast_to(aug[:, j + 1:j + 2], aug.shape)
        a, c = col0[j:j + 1, :], col0[j + 1:j + 2, :]
        b, d = col1[j:j + 1, :], col1[j + 1:j + 2, :]
        scale = 1.0 / (a * d - b * c)
        new0 = (d * row0 - b * row1) * scale
        new1 = (a * row1 - c * row0) * scale
        rest = aug - col0 * new0 - col1 * new1
        aug = jnp.where(rows == j, new0, jnp.where(rows == j + 1, new1, rest))
    return aug[:, n:]


def kernel(
    sizes,
    kind_hbm,
    near_hbm,
    owner_hbm,
    far_hbm,
    stiff_hbm,
    bload_hbm,
    pload_hbm,
    binv_hbm,
    coup_hbm,
    pblock_hbm,
    sol_ref,
    res_ref,
    bub_ref,
    kind_ref,
    near_ref,
    owner_ref,
    far_ref,
    stiff_ref,
    bload_ref,
    pload_ref,
    binv_ref,
    coup_ref,
    pblock_ref,
    ask_send,
    ask_recv,
    far_send,
    far_recv,
    gath,
    bent_rows,
    rows_top,
    rows_low,
    gram_send,
    gram_recv,
    inv_keep,
    nat_far,
    in_sem,
    send_sem,
    part_rsem,
    case_rsem,
    gram_rsem,
):
    parts, npy, nq, depth, width, chunks, fold = sizes
    my_x, my_y, my_c = lax.axis_index("px"), lax.axis_index("py"), lax.axis_index("case")
    me = my_x * npy + my_y

    def part_id(step):
        other = lax.rem(me + step + parts, parts)
        return (other // npy, lax.rem(other, npy), my_c)

    def case_to(step):
        if nq == 4:
            other = my_c + (step % 2) * (1 - 2 * lax.rem(my_c, 2))
            return other + (step // 2) * (2 - 4 * (my_c // 2))
        return lax.rem(my_c + step, nq)

    def case_from(step):
        return case_to(step) if nq == 4 else lax.rem(my_c + nq - step, nq)

    def case_id(step):
        return (my_x, my_y, case_to(step))

    direct = (1, 2) if nq == 4 else tuple(range(1, nq))

    barrier = pltpu.get_barrier_semaphore()

    order = sorted(range(1, parts), key=lambda i: -min(i % npy, npy - i % npy))

    def each_other(act):
        def per_part(i, _):
            for q in reversed(range(nq)):
                act(i, q)
            return 0

        if parts <= 8:
            for i in order:
                per_part(i, 0)
        else:
            lax.fori_loop(1, parts, per_part, 0)
        for q in reversed(range(1, nq)):
            act(0, q)

    def device(i, q):
        x, y, _ = part_id(i)
        return (x, y, case_to(q))

    def greet_part(i, _):
        pl.semaphore_signal(barrier, inc=1, device_id=part_id(i), device_id_type=MESH)
        return 0

    lax.fori_loop(1, parts, greet_part, 0)
    for i in range(1, nq):
        pl.semaphore_signal(barrier, inc=1, device_id=case_id(i), device_id_type=MESH)

    inputs = (
        (near_hbm, near_ref),
        (owner_hbm, owner_ref),
        (far_hbm, far_ref),
        (kind_hbm, kind_ref),
        (stiff_hbm, stiff_ref),
        (binv_hbm, binv_ref),
        (bload_hbm, bload_ref),
        (coup_hbm, coup_ref),
        (pload_hbm, pload_ref),
        (pblock_hbm, pblock_ref),
    )
    fetches = [
        pltpu.make_async_copy(src, dst, in_sem.at[i]) for i, (src, dst) in enumerate(inputs)
    ]
    for fetch in fetches:
        fetch.start()

    kinds = binv_ref.shape[0]
    modes, ncase, ncomp = bload_ref.shape
    pd = pload_ref.shape[0]
    nport = pload_ref.shape[2]
    slots = parts * depth
    allcase = nq * ncase

    for fetch in fetches[0:5]:
        fetch.wait()
    kind_row = kind_ref[...]
    near_row = near_ref[...]
    owner_row = owner_ref[...]
    far_row = far_ref[...]

    def as_column(row):
        return jnp.broadcast_to(row.astype(F32), (ncomp, ncomp)).T

    sub = lax.broadcasted_iota(jnp.int32, (ncomp, ncomp), 0)
    lane = lax.broadcasted_iota(jnp.int32, (ncomp, ncomp), 1)
    same = (as_column(owner_row) == owner_row.astype(F32)) & (sub < lane)
    rank = jnp.sum(jnp.where(same, 1.0, 0.0), axis=0, keepdims=True).astype(jnp.int32)
    step_row = lax.rem(owner_row - me + parts, parts)
    slot_row = step_row * depth + rank
    slot_sub = lax.broadcasted_iota(jnp.int32, (slots, ncomp), 0)
    slot_pick = jnp.where(slot_sub == slot_row, 1.0, 0.0).astype(BF16)
    step_sub = lax.broadcasted_iota(jnp.int32, (parts, ncomp), 0)
    def send_parts(src, dst, e, sign):
        def body(i, _):
            pltpu.make_async_remote_copy(
                src_ref=src(i),
                dst_ref=dst(i),
                send_sem=send_sem.at[0 if e else 3],
                recv_sem=part_rsem.at[e],
                device_id=part_id(i if sign > 0 else -i),
                device_id_type=MESH,
            ).start()
            return 0

        if parts <= 8:
            for i in order:
                body(i, 0)
        else:
            lax.fori_loop(1, parts, body, 0)

    def wait_on(ref, sem):
        pltpu.make_async_copy(ref, ref, sem).wait()

    rest = pl.ds(1, parts - 1)

    def tile_cases(row):
        return jnp.concatenate([row] * ncase, axis=1)

    def kind_masks(row):
        row = tile_cases(row)
        return [jnp.where(row == t, 1.0, 0.0).astype(BF16) for t in range(kinds)]

    masks = kind_masks(kind_row)

    def table(parts_of):
        top, low = split(parts_of)
        return top, jnp.concatenate([top, low], axis=0)

    def apply_tables(tab, x, masks):
        top, low = split(x)
        lanes = x.shape[1]
        xt = jnp.concatenate([top * m[:, :lanes] for m in masks], axis=0)
        xl = jnp.concatenate([low * m[:, :lanes] for m in masks], axis=0)
        lead = mm(tab[1], xt)
        rows = tab[0].shape[0]
        return lead[:rows] + lead[rows:] + mm(tab[0], xl)

    def wide(field, rows):
        return jnp.concatenate(
            [field[k * rows:(k + 1) * rows] for k in range(field.shape[0] // rows)], axis=1
        )

    def tall(x, count):
        return jnp.concatenate(
            [x[:, k * count:(k + 1) * count] for k in range(x.shape[1] // count)], axis=0
        )

    def pick(x, onehot):
        top, low = split(x)
        return mm(jnp.concatenate([top, low], axis=1), jnp.concatenate([onehot, onehot], axis=0))

    def at_slots(onehot, x):
        top, low = split(x)
        return lax.dot_general(
            jnp.concatenate([onehot, onehot], axis=1),
            jnp.concatenate([top, low], axis=1),
            NT,
            preferred_element_type=F32,
        )

    def place(x, onehot):
        top, low = split(x)
        return mm(top, onehot) + mm(low, onehot)

    def take(e, j):
        wait_on(far_recv.at[e, j, rest], part_rsem.at[1 + e * chunks + j])
        return far_recv[e, j].reshape(slots, width).T

    def post(e, j, out, sign):
        far_send[e, j] = out
        far_recv[e, j, 0] = out[0]
        send_parts(
            lambda i: far_send.at[e, j, i], lambda i: far_recv.at[e, j, i], 1 + e * chunks + j, sign
        )

    cuts = [0] + [((j + 1) * width) // pd for j in range(chunks)]

    def span(f, j):
        if f in (1, 2):
            return pl.ds(cuts[j] * pd, (cuts[j + 1] - cuts[j]) * pd)
        return pl.ds(j * width, width)

    def send_case(f, block, sem, step):
        pltpu.make_async_remote_copy(
            src_ref=block,
            dst_ref=block,
            send_sem=send_sem.at[1],
            recv_sem=case_rsem.at[f, sem - 1],
            device_id=case_id(step),
            device_id_type=MESH,
        ).start()

    def publish(f, j, rows):
        gath[f, my_c, span(f, j)] = rows
        for i in reversed(direct):
            send_case(f, gath.at[f, my_c, span(f, j)], i, i)

    def forward(f):
        if nq == 4:
            block = gath.at[f, case_from(2)]
            wait_on(block, case_rsem.at[f, 1])
            send_case(f, block, 3, 1)

    def lines(ref, d):
        return ref[pl.ds(d, ncase, stride=pd), :]

    def collect(f):
        for i in range(1, nq):
            if nq != 4 or i != 2:
                wait_on(gath.at[f, case_from(i)], case_rsem.at[f, i - 1])

        def body(d, _):
            cols = pl.ds(pl.multiple_of(d * nport, nport), nport)
            block = jnp.concatenate([lines(gath.at[f, q], d) for q in range(nq)], axis=0)
            top, low = split(block)
            rows_top[f * allcase:(f + 1) * allcase, cols] = top
            rows_low[f * allcase:(f + 1) * allcase, cols] = low
            return 0

        lax.fori_loop(0, pd, body, 0, unroll=16)

    def against(x, f):
        top, low = split(x)
        band = slice(f * allcase, (f + 1) * allcase)
        lead = lax.dot_general(
            jnp.concatenate([top, low], axis=0),
            rows_top[band, :],
            NT,
            preferred_element_type=F32,
        )
        low_lead = lax.dot_general(
            jnp.concatenate([top, low], axis=0),
            rows_low[band, :],
            NT,
            preferred_element_type=F32,
        )
        total = lead + low_lead
        return total[:x.shape[0]] + total[x.shape[0]:]

    def own_rows(f):
        return jnp.concatenate([lines(gath.at[f, my_c], d) for d in range(pd)], axis=1)

    def gram_out(s, block):
        high = block.shape[0] // fold
        folded = jnp.concatenate([block[r * high:(r + 1) * high] for r in range(fold)], axis=1)
        gram_send[s] = folded
        gram_recv[s, my_c * parts] = folded

        def send(i, q):
            pltpu.make_async_remote_copy(
                src_ref=gram_send.at[s],
                dst_ref=gram_recv.at[s, my_c * parts + i],
                send_sem=send_sem.at[2],
                recv_sem=gram_rsem.at[s],
                device_id=device(i, q),
                device_id_type=MESH,
            ).start()

        each_other(send)

    others = pl.ds(1, nq * parts - 1)

    def gram_in(s):
        wait_on(gram_recv.at[s, others], gram_rsem.at[s])
        blocks = []
        for q in range(nq):
            total = jnp.sum(gram_recv[s, q * parts:(q + 1) * parts], axis=0)
            blocks.append(
                jnp.concatenate(
                    [total[:, r * allcase:(r + 1) * allcase] for r in range(fold)], axis=0
                )
            )
        return (
            sym(jnp.concatenate([block[:ncase] for block in blocks], axis=0)),
            sym(jnp.concatenate([block[ncase:] for block in blocks], axis=0)),
        )

    def sym(g):
        return 0.5 * (g + g.T)

    def part(x, j):
        return x[j * width:(j + 1) * width]

    for fetch in fetches[5:8]:
        fetch.wait()
    inv_tab = table(jnp.concatenate([binv_ref[t] for t in range(kinds)], axis=1))
    coup_tab = table(jnp.concatenate([coup_ref[t].T for t in range(kinds)], axis=1))
    ready = [0] + [-(-((j + 1) * width) // pd) for j in range(chunks)]
    condensed_near, leaving = [], None
    for j in range(chunks):
        a, b = ready[j], ready[j + 1]
        loads = jnp.concatenate([bload_ref[:, k, :] for k in range(a, b)], axis=1)
        lifted = apply_tables(inv_tab, loads, masks)
        inv_keep[:, a * ncomp:b * ncomp] = lifted
        condensed = -apply_tables(coup_tab, lifted, masks)
        condensed_near.append(tall(condensed[:pd], ncomp))
        out = tall(condensed[pd:], ncomp)
        leaving = out if leaving is None else jnp.concatenate([leaving, out], axis=0)
        if j == 0:
            naming = jnp.concatenate(
                [
                    jnp.where(step_sub == step_row, row, 0.0)
                    for row in ((far_row + 1).astype(F32), kind_row.astype(F32), stiff_ref[...])
                ],
                axis=0,
            )
            ranked = jnp.where(sub == rank, 1.0, 0.0)
            wanted = exact(naming, ranked, NT)
            wanted = jnp.concatenate([wanted[r * parts:(r + 1) * parts] for r in range(3)], axis=1)
            wanted = wanted.reshape(parts, 1, 3 * ncomp)
            ask_send[...] = wanted
            ask_recv[0] = wanted[0]
            pl.semaphore_wait(barrier, parts + nq - 2)
            send_parts(lambda i: ask_send.at[i], lambda i: ask_recv.at[i], 0, 1)
        post(0, j, at_slots(slot_pick, part(leaving, j)).reshape(parts, depth, width), 1)
    for fetch in fetches[8:]:
        fetch.wait()
    near_in = jnp.where(sub == near_row, 1.0, 0.0).astype(BF16)
    near_out = jnp.where(lane.astype(F32) == as_column(near_row), 1.0, 0.0).astype(BF16)
    near_slots = lax.dot_general(slot_pick, near_in, NT, preferred_element_type=F32).astype(BF16)

    stiff = tile_cases(stiff_ref[...])
    red_t = [exact(binv_ref[t], coup_ref[t], TN) for t in range(kinds)]
    schur = [pblock_ref[t] - exact(red_t[t], coup_ref[t], TN) for t in range(kinds)]

    def corner(a, b):
        rows, cols = slice(a * pd, (a + 1) * pd), slice(b * pd, (b + 1) * pd)
        return table(jnp.concatenate([schur[t][rows, cols] for t in range(kinds)], axis=1))

    nn_tab, nf_tab, fn_tab, ff_tab = corner(0, 0), corner(0, 1), corner(1, 0), corner(1, 1)
    red_tab = table(jnp.concatenate(red_t, axis=1))
    own = jnp.concatenate([pload_ref[:, k, :] for k in range(ncase)], axis=0)
    own = own + pick(jnp.concatenate(condensed_near, axis=0), near_out)
    wait_on(ask_recv.at[rest], part_rsem.at[0])
    asked = ask_recv[...].reshape(parts, 3 * ncomp)
    ports = jnp.concatenate([asked[:, 0:ncomp]] * (ncomp // parts), axis=0).T
    port_lane = lax.broadcasted_iota(jnp.int32, (depth, nport), 1).astype(F32)
    asked_pick = jnp.concatenate(
        [jnp.where(ports[0:depth, i:i + 1] - 1.0 == port_lane, 1.0, 0.0) for i in range(parts)],
        axis=0,
    ).astype(BF16)

    def slot_line(r):
        return jnp.concatenate(
            [asked[i:i + 1, r * ncomp:r * ncomp + depth] for i in range(parts)], axis=1
        )

    slot_masks = kind_masks(slot_line(1))
    slot_stiff = tile_cases(slot_line(2))

    def scatter(e, j, piece):
        post(e, j, at_slots(asked_pick, piece).reshape(parts, depth, width), -1)

        def rest_of_it():
            post(e + 1, j, at_slots(near_slots, piece).reshape(parts, depth, width), 1)

        return rest_of_it

    def join(a, b):
        return b if a is None else jnp.concatenate([a, b], axis=0)

    def near_side(tab, x, a, b):
        return apply_tables(tab, wide(x, pd), masks) * stiff[:, a * ncomp:b * ncomp]

    def far_side(tab, x, a, b):
        return apply_tables(tab, wide(x, pd), slot_masks) * slot_stiff[:, a * slots:b * slots]

    def near_ports(y):
        return pick(tall(y, ncomp), near_out)

    def far_ports(y):
        return place(tall(y, slots), asked_pick)

    def diagonal(e, field):
        y_near = near_side(nn_tab, pick(field, near_in), 0, ncase)
        far_at = [far_send[e, j].reshape(slots, width).T for j in range(chunks)]
        return y_near, far_side(ff_tab, jnp.concatenate(far_at, axis=0), 0, ncase)

    def take_far_values(e, j):
        return place(take(e, j), slot_pick)

    base = None
    for j in range(chunks):
        piece = part(own, j) + place(take(0, j), asked_pick)
        scatter(1, j, piece)()
        publish(0, j, piece)
        base = join(base, piece)

    y_near, y_far = diagonal(1, base)
    far_base, near_at, first, sent, later = None, None, None, 0, []
    for j in range(chunks):
        a, b = cuts[j], cuts[j + 1]
        if j == chunks - 1:
            forward(0)
        piece = take_far_values(1, j)
        publish(3, j, piece)
        far_base = join(far_base, piece)
        near_at = join(near_at, take(2, j))
        rows = slice(a * pd, b * pd)
        y = y_near[:, a * ncomp:b * ncomp] + near_side(nf_tab, far_base[rows], a, b)
        done = near_ports(y)
        y = y_far[:, a * slots:b * slots] + far_side(fn_tab, near_at[rows], a, b)
        done = done + far_ports(y)
        first = join(first, done)
        while (sent + 1) * width <= b * pd:
            later.append(scatter(3, sent, part(first, sent)))
            sent += 1
        publish(1, j, done)

    y_near, y_far = diagonal(3, first)
    straight = near_ports(y_near) + far_ports(y_far)
    collect(0)
    gram_out(0, against(jnp.concatenate([own_rows(0), own_rows(1)], axis=0), 0))
    far_first, crossed = None, None
    for j in range(chunks):
        a, b = cuts[j], cuts[j + 1]
        if j == chunks - 1:
            forward(1)
            forward(3)
            collect(1)
            square = against(own_rows(1), 1)
        piece = take_far_values(3, j)
        far_first = join(far_first, piece)
        crossed = join(crossed, near_ports(near_side(nf_tab, far_first[a * pd:b * pd], a, b)))
        if j < chunks - 1:
            later[j]()
            publish(4, j, piece)
    bent_rows[...] = straight + 2.0 * crossed
    bent = jnp.concatenate([lines(bent_rows, d) for d in range(pd)], axis=1)
    gram_out(1, jnp.concatenate([square, against(bent, 1)], axis=0))
    later[chunks - 1]()
    publish(4, chunks - 1, piece)

    n = allcase
    eye = jnp.where(
        lax.broadcasted_iota(jnp.int32, (n, n), 0) == lax.broadcasted_iota(jnp.int32, (n, n), 1),
        1.0,
        0.0,
    )
    near_at = None

    def finish_second(j, near_at):
        a, b = cuts[j], cuts[j + 1]
        rows = slice(a * pd, b * pd)
        near_at = join(near_at, take(4, j))
        y = far_side(fn_tab, near_at[rows], a, b)
        publish(2, j, straight[rows] + crossed[rows] + far_ports(y))
        return near_at

    g00, g01 = gram_in(0)
    both = gauss_solve(g01, jnp.concatenate([g00, eye], axis=1))
    mine = jnp.where(
        lax.broadcasted_iota(jnp.int32, (n, ncase), 0)
        == lax.broadcasted_iota(jnp.int32, (n, ncase), 1) + my_c * ncase,
        1.0,
        0.0,
    )
    chosen = exact(jnp.concatenate([both[:, 0:n], g01], axis=0), mine)
    first_step, g01_mine, inverse = chosen[0:n], chosen[n:2 * n], both[:, n:2 * n]
    for j in range(chunks):
        if j == chunks - 1:
            collect(3)
        near_at = finish_second(j, near_at)
    forward(4)
    g11, g12 = gram_in(1)
    over = exact(inverse, g11)
    side = exact(g11, jnp.concatenate([over, first_step], axis=1))
    beta = gauss_solve(g12 - sym(side[:, 0:n]), side[:, n:] - g01_mine)
    alpha = first_step + exact(over, beta)
    coefs = jnp.concatenate([alpha, -beta], axis=0).T
    ctop, clow = split(coefs)
    stack = jnp.concatenate([ctop, clow], axis=0)

    def mix(f):
        band = slice(f * allcase, (f + 2) * allcase)
        lead = mm(stack, rows_top[band, :])
        return lead[0:ncase] + lead[ncase:] + mm(ctop, rows_low[band, :])

    answer_rows = mix(0)
    for d in range(pd):
        sol_ref[d] = answer_rows[:, d * nport:(d + 1) * nport]
    collect(4)
    far_rows = mix(3)
    for d in range(pd):
        nat_far[d] = far_rows[:, d * nport:(d + 1) * nport]
    answer = jnp.concatenate([sol_ref[:, k, :] for k in range(ncase)], axis=0)
    near = wide(pick(answer, near_in), pd)
    ends = jnp.concatenate(
        [near, jnp.concatenate([nat_far[:, k, :] for k in range(ncase)], axis=1)], axis=0
    )
    scaled = inv_keep[...] / stiff
    forward(2)
    back = scaled - apply_tables(red_tab, ends, masks)
    for k in range(ncase):
        bub_ref[:, k, :] = back[:, k * ncomp:(k + 1) * ncomp]
    collect(2)
    drop_rows = mix(1)
    for d in range(pd):
        res_ref[d] = lines(gath.at[0, my_c], d) - drop_rows[:, d * nport:(d + 1) * nport]

    wait_on(far_send.at[:, :, rest], send_sem.at[0])
    wait_on(gath.at[:, pl.ds(1, nq - 1)], send_sem.at[1])
    wait_on(gram_recv.at[:, others], send_sem.at[2])
    wait_on(ask_send.at[rest], send_sem.at[3])


def emit(*refs):
    count = len(refs) // 2
    sems = refs[-1]
    copies = [
        pltpu.make_async_copy(refs[i], refs[count + i], sems.at[i]) for i in range(count)
    ]
    for copy in copies:
        copy.start()
    for copy in copies:
        copy.wait()


def local(
    comp_type,
    stiffness,
    near_port,
    far_owner,
    far_port,
    bubble_load,
    port_load,
    bubble_inverse,
    coupling,
    port_block,
):
    npy = lax.axis_size("py")
    parts = lax.axis_size("px") * npy
    nq = lax.axis_size("case")
    ncomp = comp_type.shape[0]
    modes, ncase, _ = bubble_load.shape
    pd, _, nport = port_load.shape
    kinds = bubble_inverse.shape[0]
    cap = 3 * ncomp // (2 * parts)
    depth = -(-cap // 8) * 8
    allcase = nq * ncase
    width = 128 if (ncase * pd) % 128 == 0 else ncase * pd
    chunks = ncase * pd // width
    fold = max(1, 128 // allcase)
    vmem = pl.BlockSpec(memory_space=pltpu.VMEM)
    hbm = pl.BlockSpec(memory_space=pltpu.HBM)

    def body(*refs):
        kernel((parts, npy, nq, depth, width, chunks, fold), *refs)

    shapes = (
        jax.ShapeDtypeStruct(port_load.shape, F32),
        jax.ShapeDtypeStruct(port_load.shape, F32),
        jax.ShapeDtypeStruct(bubble_load.shape, F32),
    )
    results = pl.pallas_call(
        body,
        out_shape=shapes,
        in_specs=[hbm] * 10,
        out_specs=(vmem, vmem, vmem),
        scratch_shapes=[
            pltpu.VMEM((1, ncomp), jnp.int32),
            pltpu.VMEM((1, ncomp), jnp.int32),
            pltpu.VMEM((1, ncomp), jnp.int32),
            pltpu.VMEM((1, ncomp), jnp.int32),
            pltpu.VMEM((1, ncomp), F32),
            pltpu.VMEM(bubble_load.shape, F32),
            pltpu.VMEM(port_load.shape, F32),
            pltpu.VMEM(bubble_inverse.shape, F32),
            pltpu.VMEM((kinds, modes, 2 * pd), F32),
            pltpu.VMEM(port_block.shape, F32),
            pltpu.VMEM((parts, 1, 3 * ncomp), F32),
            pltpu.VMEM((parts, 1, 3 * ncomp), F32),
            pltpu.VMEM((5, chunks, parts, depth, width), F32),
            pltpu.VMEM((5, chunks, parts, depth, width), F32),
            pltpu.VMEM((5, nq, ncase * pd, nport), F32),
            pltpu.VMEM((ncase * pd, nport), F32),
            pltpu.VMEM((5 * allcase, pd * nport), BF16),
            pltpu.VMEM((5 * allcase, pd * nport), BF16),
            pltpu.VMEM((2, 2 * ncase // fold, fold * allcase), F32),
            pltpu.VMEM((2, nq * parts, 2 * ncase // fold, fold * allcase), F32),
            pltpu.VMEM((modes, ncase * ncomp), F32),
            pltpu.VMEM((pd, ncase, nport), F32),
            pltpu.SemaphoreType.DMA((10,)),
            pltpu.SemaphoreType.DMA((4,)),
            pltpu.SemaphoreType.DMA((1 + 5 * chunks,)),
            pltpu.SemaphoreType.DMA((5, nq - 1)),
            pltpu.SemaphoreType.DMA((2,)),
        ],
        compiler_params=pltpu.CompilerParams(
            collective_id=0, has_side_effects=True, vmem_limit_bytes=32 * 1024 * 1024
        ),
        name="condensed_solve",
    )(
        *(
            pltpu.with_memory_space_constraint(x, pltpu.HBM)
            for x in (
                comp_type.reshape(1, ncomp),
                near_port.reshape(1, ncomp),
                far_owner.reshape(1, ncomp),
                far_port.reshape(1, ncomp),
                stiffness.reshape(1, ncomp),
                bubble_load,
                port_load,
                bubble_inverse,
                jnp.swapaxes(coupling, 1, 2),
                port_block,
            )
        )
    )
    return pl.pallas_call(
        emit,
        out_shape=shapes,
        in_specs=[vmem] * 3,
        out_specs=(hbm, hbm, hbm),
        scratch_shapes=[pltpu.SemaphoreType.DMA((3,))],
        compiler_params=pltpu.CompilerParams(vmem_limit_bytes=4 * 1024 * 1024),
        name="emit",
    )(*results)


def solution(mesh):
    placed = (
        P(("px", "py")),
        P(("px", "py")),
        P(("px", "py")),
        P(("px", "py"), None),
        P(("px", "py")),
        P(None, "case", ("px", "py")),
        P(None, "case", ("px", "py")),
        P(),
        P(),
        P(),
    )
    return jax.shard_map(
        local,
        mesh=mesh,
        in_specs=placed,
        out_specs=(
            P(None, "case", ("px", "py")),
            P(None, "case", ("px", "py")),
            P(None, "case", ("px", "py")),
        ),
        check_vma=False,
    )
```

```python
import jax
import jax.numpy as jnp
from jax import lax
from jax.experimental import pallas as pl
from jax.experimental.pallas import tpu as pltpu
from jax.sharding import PartitionSpec as P

HIGH = lax.Precision.HIGHEST
F32 = jnp.float32
BF16 = jnp.bfloat16
MESH = pl.DeviceIdType.MESH
NT = (((1,), (1,)), ((), ()))
TN = (((0,), (0,)), ((), ()))


def split(x):
    top = x.astype(BF16)
    return top, (x - top.astype(F32)).astype(BF16)


def mm(a, b):
    return jnp.dot(a, b, preferred_element_type=F32)


def exact(a, b, dims=(((1,), (0,)), ((), ()))):
    return lax.dot_general(a, b, dims, precision=HIGH, preferred_element_type=F32)


def invert(a, b, c, d):
    scale = 1.0 / (a * d - b * c)
    return d * scale, -b * scale, -c * scale, a * scale


def times(m, x):
    return m[0] * x[0] + m[1] * x[1], m[2] * x[0] + m[3] * x[1]


def gauss_solve(matrix, target, gain):
    n = matrix.shape[0]
    gain_row, gain_col = gain
    aug = jnp.concatenate([matrix * gain_row, target], axis=1) * gain_col
    rows = lax.broadcasted_iota(jnp.int32, aug.shape, 0)
    for j in range(0, n, 4):
        cols = [jnp.broadcast_to(aug[:, j + k:j + k + 1], aug.shape) for k in range(4)]
        line = [aug[j + k:j + k + 1, :] for k in range(4)]
        p = [[cols[k][j + i:j + i + 1, :] for k in range(4)] for i in range(4)]
        lead = invert(p[0][0], p[0][1], p[1][0], p[1][1])
        left, right = times(lead, (p[0][2], p[1][2])), times(lead, (p[0][3], p[1][3]))
        low = (p[2][0], p[2][1], p[3][0], p[3][1])
        under_left, under_right = times(low, left), times(low, right)
        tail = invert(
            p[2][2] - under_left[0],
            p[2][3] - under_right[0],
            p[3][2] - under_left[1],
            p[3][3] - under_right[1],
        )
        top = times(lead, (line[0], line[1]))
        carried = times(low, top)
        new2, new3 = times(tail, (line[2] - carried[0], line[3] - carried[1]))
        new0 = top[0] - left[0] * new2 - right[0] * new3
        new1 = top[1] - left[1] * new2 - right[1] * new3
        aug = (aug - cols[0] * new0 - cols[1] * new1) - (cols[2] * new2 + cols[3] * new3)
        for k, new in enumerate((new0, new1, new2, new3)):
            aug = jnp.where(rows == j + k, new, aug)
    return aug[:, n:] * gain_col


def kernel(
    sizes,
    kind_hbm,
    near_hbm,
    owner_hbm,
    far_hbm,
    stiff_hbm,
    bload_hbm,
    pload_hbm,
    binv_hbm,
    coup_hbm,
    pblock_hbm,
    sol_ref,
    res_ref,
    bub_ref,
    kind_ref,
    near_ref,
    owner_ref,
    far_ref,
    stiff_ref,
    bload_ref,
    pload_ref,
    binv_ref,
    coup_ref,
    pblock_ref,
    ask_send,
    ask_recv,
    far_send,
    far_recv,
    gath,
    bent_rows,
    rows_top,
    rows_low,
    gram_send,
    gram_recv,
    inv_keep,
    nat_far,
    in_sem,
    send_sem,
    part_rsem,
    case_rsem,
    gram_rsem,
):
    parts, npy, nq, depth, width, chunks, fold = sizes
    my_x, my_y, my_c = lax.axis_index("px"), lax.axis_index("py"), lax.axis_index("case")
    me = my_x * npy + my_y

    def part_id(step):
        other = lax.rem(me + step + parts, parts)
        return (other // npy, lax.rem(other, npy), my_c)

    def case_to(step):
        if nq == 4:
            other = my_c + (step % 2) * (1 - 2 * lax.rem(my_c, 2))
            return other + (step // 2) * (2 - 4 * (my_c // 2))
        return lax.rem(my_c + step, nq)

    def case_from(step):
        return case_to(step) if nq == 4 else lax.rem(my_c + nq - step, nq)

    def case_id(step):
        return (my_x, my_y, case_to(step))

    direct = (1, 2) if nq == 4 else tuple(range(1, nq))

    barrier = pltpu.get_barrier_semaphore()

    order = sorted(range(1, parts), key=lambda i: -min(i % npy, npy - i % npy))
    if npy == 4 and parts == 2 * npy:
        half = my_y // 2
        rows = (3 - 3 * half, 2 - half, my_y + 1 - 2 * lax.rem(my_y, 2), my_y)
        order = [
            lax.rem(x * npy + y - me + parts, parts)
            for y in rows
            for x in ((1 - my_x, my_x) if y is not my_y else (1 - my_x,))
        ]

    def each_other(act):
        def per_part(i, _):
            for q in reversed(range(nq)):
                act(i, q)
            return 0

        if parts <= 8:
            for i in order:
                per_part(i, 0)
        else:
            lax.fori_loop(1, parts, per_part, 0)
        for q in reversed(range(1, nq)):
            act(0, q)

    def device(i, q):
        x, y, _ = part_id(i)
        return (x, y, case_to(q))

    def greet_part(i, _):
        pl.semaphore_signal(barrier, inc=1, device_id=part_id(i), device_id_type=MESH)
        return 0

    lax.fori_loop(1, parts, greet_part, 0)
    for i in range(1, nq):
        pl.semaphore_signal(barrier, inc=1, device_id=case_id(i), device_id_type=MESH)

    inputs = (
        (near_hbm, near_ref),
        (owner_hbm, owner_ref),
        (far_hbm, far_ref),
        (kind_hbm, kind_ref),
        (stiff_hbm, stiff_ref),
        (binv_hbm, binv_ref),
        (bload_hbm, bload_ref),
        (coup_hbm, coup_ref),
        (pload_hbm, pload_ref),
        (pblock_hbm, pblock_ref),
    )
    fetches = [
        pltpu.make_async_copy(src, dst, in_sem.at[i]) for i, (src, dst) in enumerate(inputs)
    ]
    for fetch in fetches:
        fetch.start()

    kinds = binv_ref.shape[0]
    modes, ncase, ncomp = bload_ref.shape
    pd = pload_ref.shape[0]
    nport = pload_ref.shape[2]
    slots = parts * depth
    allcase = nq * ncase

    for fetch in fetches[0:5]:
        fetch.wait()
    kind_row = kind_ref[...]
    near_row = near_ref[...]
    owner_row = owner_ref[...]
    far_row = far_ref[...]

    def as_column(row):
        return jnp.broadcast_to(row.astype(F32), (ncomp, ncomp)).T

    sub = lax.broadcasted_iota(jnp.int32, (ncomp, ncomp), 0)
    lane = lax.broadcasted_iota(jnp.int32, (ncomp, ncomp), 1)
    same = (as_column(owner_row) == owner_row.astype(F32)) & (sub < lane)
    rank = jnp.sum(jnp.where(same, 1.0, 0.0), axis=0, keepdims=True).astype(jnp.int32)
    step_row = lax.rem(owner_row - me + parts, parts)
    slot_row = step_row * depth + rank
    slot_sub = lax.broadcasted_iota(jnp.int32, (slots, ncomp), 0)
    slot_pick = jnp.where(slot_sub == slot_row, 1.0, 0.0).astype(BF16)
    step_sub = lax.broadcasted_iota(jnp.int32, (parts, ncomp), 0)
    def send_parts(src, dst, e, sign):
        def body(i, _):
            pltpu.make_async_remote_copy(
                src_ref=src(i),
                dst_ref=dst(i),
                send_sem=send_sem.at[0 if e else 3],
                recv_sem=part_rsem.at[e],
                device_id=part_id(i if sign > 0 else -i),
                device_id_type=MESH,
            ).start()
            return 0

        if parts <= 8:
            for i in order:
                body(i if sign > 0 else parts - i, 0)
        else:
            lax.fori_loop(1, parts, body, 0)

    def wait_on(ref, sem):
        pltpu.make_async_copy(ref, ref, sem).wait()

    rest = pl.ds(1, parts - 1)

    def tile_cases(row):
        return jnp.concatenate([row] * ncase, axis=1)

    def kind_masks(row):
        row = tile_cases(row)
        return [jnp.where(row == t, 1.0, 0.0).astype(BF16) for t in range(kinds)]

    masks = kind_masks(kind_row)

    def table(parts_of):
        top, low = split(parts_of)
        return top, jnp.concatenate([top, low], axis=0)

    def apply_tables(tab, x, masks):
        top, low = split(x)
        lanes = x.shape[1]
        xt = jnp.concatenate([top * m[:, :lanes] for m in masks], axis=0)
        xl = jnp.concatenate([low * m[:, :lanes] for m in masks], axis=0)
        lead = mm(tab[1], xt)
        rows = tab[0].shape[0]
        return lead[:rows] + lead[rows:] + mm(tab[0], xl)

    def wide(field, rows):
        return jnp.concatenate(
            [field[k * rows:(k + 1) * rows] for k in range(field.shape[0] // rows)], axis=1
        )

    def tall(x, count):
        return jnp.concatenate(
            [x[:, k * count:(k + 1) * count] for k in range(x.shape[1] // count)], axis=0
        )

    def pick(x, onehot):
        top, low = split(x)
        return mm(jnp.concatenate([top, low], axis=1), jnp.concatenate([onehot, onehot], axis=0))

    def at_slots(onehot, x):
        top, low = split(x)
        return lax.dot_general(
            jnp.concatenate([onehot, onehot], axis=1),
            jnp.concatenate([top, low], axis=1),
            NT,
            preferred_element_type=F32,
        )

    def place(x, onehot):
        top, low = split(x)
        return mm(top, onehot) + mm(low, onehot)

    def take(e, j):
        wait_on(far_recv.at[e, j, rest], part_rsem.at[1 + e * chunks + j])
        return far_recv[e, j].reshape(slots, width).T

    def post(e, j, out, sign):
        far_send[e, j] = out
        far_recv[e, j, 0] = out[0]
        send_parts(
            lambda i: far_send.at[e, j, i], lambda i: far_recv.at[e, j, i], 1 + e * chunks + j, sign
        )

    cuts = [0] + [((j + 1) * width) // pd for j in range(chunks)]

    def span(f, j):
        if f in (1, 2):
            return pl.ds(cuts[j] * pd, (cuts[j + 1] - cuts[j]) * pd)
        return pl.ds(j * width, width)

    lanes_of = {f: (f,) for f in range(5)}
    if chunks > 1:
        lanes_of[2] = (2, 5)

    def lane_span(lane):
        if lane == 5:
            return span(2, chunks - 1)
        return pl.ds(0, cuts[chunks - 1] * pd if lane == 2 and chunks > 1 else ncase * pd)

    def send_case(lane, block, sem, step):
        pltpu.make_async_remote_copy(
            src_ref=block,
            dst_ref=block,
            send_sem=send_sem.at[1],
            recv_sem=case_rsem.at[lane, sem - 1],
            device_id=case_id(step),
            device_id_type=MESH,
        ).start()

    def publish(f, j, rows):
        gath[f, my_c, span(f, j)] = rows
        lane = lanes_of[f][-1] if j == chunks - 1 else f
        for i in reversed(direct):
            send_case(lane, gath.at[f, my_c, span(f, j)], i, i)

    def forward(f, *lanes):
        if nq == 4:
            for lane in lanes or lanes_of[f]:
                block = gath.at[f, case_from(2), lane_span(lane)]
                wait_on(block, case_rsem.at[lane, 1])
                send_case(lane, block, 3, 1)

    def lines(ref, d):
        return ref[pl.ds(d, ncase, stride=pd), :]

    def collect(f):
        for i in range(1, nq):
            if nq != 4 or i != 2:
                for lane in lanes_of[f]:
                    wait_on(gath.at[f, case_from(i), lane_span(lane)], case_rsem.at[lane, i - 1])

        def body(d, _):
            cols = pl.ds(pl.multiple_of(d * nport, nport), nport)
            block = jnp.concatenate([lines(gath.at[f, q], d) for q in range(nq)], axis=0)
            top, low = split(block)
            rows_top[f * allcase:(f + 1) * allcase, cols] = top
            rows_low[f * allcase:(f + 1) * allcase, cols] = low
            return 0

        lax.fori_loop(0, pd, body, 0, unroll=16)

    def against(x, f):
        top, low = split(x)
        band = slice(f * allcase, (f + 1) * allcase)
        lead = lax.dot_general(
            jnp.concatenate([top, low], axis=0),
            rows_top[band, :],
            NT,
            preferred_element_type=F32,
        )
        low_lead = lax.dot_general(
            jnp.concatenate([top, low], axis=0),
            rows_low[band, :],
            NT,
            preferred_element_type=F32,
        )
        total = lead + low_lead
        return total[:x.shape[0]] + total[x.shape[0]:]

    def own_rows(f):
        return jnp.concatenate([lines(gath.at[f, my_c], d) for d in range(pd)], axis=1)

    def gram_out(s, block):
        high = ncase // fold
        folded = jnp.concatenate([block[r * high:(r + 1) * high] for r in range(fold)], axis=1)
        gram_send[s] = folded
        gram_recv[s, my_c * parts] = folded

        def send(i, q):
            pltpu.make_async_remote_copy(
                src_ref=gram_send.at[s],
                dst_ref=gram_recv.at[s, my_c * parts + i],
                send_sem=send_sem.at[2],
                recv_sem=gram_rsem.at[s],
                device_id=device(i, q),
                device_id_type=MESH,
            ).start()

        each_other(send)

    others = pl.ds(1, nq * parts - 1)

    def gram_in(s):
        wait_on(gram_recv.at[s, others], gram_rsem.at[s])
        rows = []
        for q in range(nq):
            total = jnp.sum(gram_recv[s, q * parts:(q + 1) * parts], axis=0)
            for r in range(fold):
                rows.append(total[:, r * allcase:(r + 1) * allcase])
        return sym(jnp.concatenate(rows, axis=0))

    def sym(g):
        return 0.5 * (g + g.T)

    def part(x, j):
        return x[j * width:(j + 1) * width]

    for fetch in fetches[5:8]:
        fetch.wait()
    inv_tab = table(jnp.concatenate([binv_ref[t] for t in range(kinds)], axis=1))
    coup_tab = table(jnp.concatenate([coup_ref[t].T for t in range(kinds)], axis=1))
    ready = [0] + [-(-((j + 1) * width) // pd) for j in range(chunks)]
    condensed_near, leaving = [], None
    for j in range(chunks):
        a, b = ready[j], ready[j + 1]
        loads = jnp.concatenate([bload_ref[:, k, :] for k in range(a, b)], axis=1)
        lifted = apply_tables(inv_tab, loads, masks)
        inv_keep[:, a * ncomp:b * ncomp] = lifted
        condensed = -apply_tables(coup_tab, lifted, masks)
        condensed_near.append(tall(condensed[:pd], ncomp))
        out = tall(condensed[pd:], ncomp)
        leaving = out if leaving is None else jnp.concatenate([leaving, out], axis=0)
        if j == 0:
            naming = jnp.concatenate(
                [
                    jnp.where(step_sub == step_row, row, 0.0)
                    for row in ((far_row + 1).astype(F32), kind_row.astype(F32), stiff_ref[...])
                ],
                axis=0,
            )
            ranked = jnp.where(sub == rank, 1.0, 0.0)
            wanted = exact(naming, ranked, NT)
            wanted = jnp.concatenate([wanted[r * parts:(r + 1) * parts] for r in range(3)], axis=1)
            wanted = wanted.reshape(parts, 1, 3 * ncomp)
            ask_send[...] = wanted
            ask_recv[0] = wanted[0]
            pl.semaphore_wait(barrier, parts + nq - 2)
            send_parts(lambda i: ask_send.at[i], lambda i: ask_recv.at[i], 0, 1)
        post(0, j, at_slots(slot_pick, part(leaving, j)).reshape(parts, depth, width), 1)
    for fetch in fetches[8:]:
        fetch.wait()
    near_in = jnp.where(sub == near_row, 1.0, 0.0).astype(BF16)
    near_out = jnp.where(lane.astype(F32) == as_column(near_row), 1.0, 0.0).astype(BF16)
    near_slots = lax.dot_general(slot_pick, near_in, NT, preferred_element_type=F32).astype(BF16)

    stiff = tile_cases(stiff_ref[...])
    red_t = [exact(binv_ref[t], coup_ref[t], TN) for t in range(kinds)]
    schur = [pblock_ref[t] - exact(red_t[t], coup_ref[t], TN) for t in range(kinds)]

    def corner(a, b):
        rows, cols = slice(a * pd, (a + 1) * pd), slice(b * pd, (b + 1) * pd)
        return table(jnp.concatenate([schur[t][rows, cols] for t in range(kinds)], axis=1))

    nn_tab, nf_tab, fn_tab, ff_tab = corner(0, 0), corner(0, 1), corner(1, 0), corner(1, 1)
    red_tab = table(jnp.concatenate(red_t, axis=1))
    own = jnp.concatenate([pload_ref[:, k, :] for k in range(ncase)], axis=0)
    own = own + pick(jnp.concatenate(condensed_near, axis=0), near_out)
    wait_on(ask_recv.at[rest], part_rsem.at[0])
    asked = ask_recv[...].reshape(parts, 3 * ncomp)
    ports = jnp.concatenate([asked[:, 0:ncomp]] * (ncomp // parts), axis=0).T
    port_lane = lax.broadcasted_iota(jnp.int32, (depth, nport), 1).astype(F32)
    asked_pick = jnp.concatenate(
        [jnp.where(ports[0:depth, i:i + 1] - 1.0 == port_lane, 1.0, 0.0) for i in range(parts)],
        axis=0,
    ).astype(BF16)

    def slot_line(r):
        return jnp.concatenate(
            [asked[i:i + 1, r * ncomp:r * ncomp + depth] for i in range(parts)], axis=1
        )

    slot_masks = kind_masks(slot_line(1))
    slot_stiff = tile_cases(slot_line(2))

    def scatter(e, j, piece):
        post(e, j, at_slots(asked_pick, piece).reshape(parts, depth, width), -1)

        def rest_of_it():
            post(e + 1, j, at_slots(near_slots, piece).reshape(parts, depth, width), 1)

        return rest_of_it

    def join(a, b):
        return b if a is None else jnp.concatenate([a, b], axis=0)

    def near_side(tab, x, a, b):
        return apply_tables(tab, wide(x, pd), masks) * stiff[:, a * ncomp:b * ncomp]

    def far_side(tab, x, a, b):
        return apply_tables(tab, wide(x, pd), slot_masks) * slot_stiff[:, a * slots:b * slots]

    def near_ports(y):
        return pick(tall(y, ncomp), near_out)

    def far_ports(y):
        return place(tall(y, slots), asked_pick)

    def diagonal(e, field):
        y_near = near_side(nn_tab, pick(field, near_in), 0, ncase)
        far_at = [far_send[e, j].reshape(slots, width).T for j in range(chunks)]
        return y_near, far_side(ff_tab, jnp.concatenate(far_at, axis=0), 0, ncase)

    def take_far_values(e, j):
        return place(take(e, j), slot_pick)

    base = None
    for j in range(chunks):
        piece = part(own, j) + place(take(0, j), asked_pick)
        scatter(1, j, piece)()
        publish(0, j, piece)
        base = join(base, piece)

    y_near, y_far = diagonal(1, base)
    far_base, near_at, first, sent, later = None, None, None, 0, []
    for j in range(chunks):
        a, b = cuts[j], cuts[j + 1]
        if j == chunks - 1:
            forward(0)
        piece = take_far_values(1, j)
        publish(3, j, piece)
        far_base = join(far_base, piece)
        near_at = join(near_at, take(2, j))
        rows = slice(a * pd, b * pd)
        y = y_near[:, a * ncomp:b * ncomp] + near_side(nf_tab, far_base[rows], a, b)
        done = near_ports(y)
        y = y_far[:, a * slots:b * slots] + far_side(fn_tab, near_at[rows], a, b)
        done = done + far_ports(y)
        first = join(first, done)
        while (sent + 1) * width <= b * pd:
            later.append(scatter(3, sent, part(first, sent)))
            sent += 1
        publish(1, j, done)

    y_near, y_far = diagonal(3, first)
    straight = near_ports(y_near) + far_ports(y_far)
    collect(0)
    early = against(jnp.concatenate([own_rows(0), own_rows(1)], axis=0), 0)
    gram_out(1, early[ncase:])
    gram_out(0, early[:ncase])
    far_first, crossed = None, None
    for j in range(chunks):
        a, b = cuts[j], cuts[j + 1]
        if j == chunks - 1:
            forward(1)
            forward(3)
            collect(1)
            gram_out(2, against(own_rows(1), 1))
        piece = take_far_values(3, j)
        publish(4, j, piece)
        far_first = join(far_first, piece)
        crossed = join(crossed, near_ports(near_side(nf_tab, far_first[a * pd:b * pd], a, b)))
        if j < chunks - 1:
            later[j]()
    bent_rows[...] = straight + 2.0 * crossed
    bent = jnp.concatenate([lines(bent_rows, d) for d in range(pd)], axis=1)
    gram_out(3, against(bent, 1))
    later[chunks - 1]()

    n = allcase
    eye = jnp.where(
        lax.broadcasted_iota(jnp.int32, (n, n), 0) == lax.broadcasted_iota(jnp.int32, (n, n), 1),
        1.0,
        0.0,
    )
    near_at = None

    def finish_second(j, near_at):
        a, b = cuts[j], cuts[j + 1]
        rows = slice(a * pd, b * pd)
        near_at = join(near_at, take(4, j))
        y = far_side(fn_tab, near_at[rows], a, b)
        publish(2, j, straight[rows] + crossed[rows] + far_ports(y))
        return near_at

    g01, g00 = gram_in(1), gram_in(0)

    def gains(g):
        diagonal = g * eye
        return tuple(lax.rsqrt(jnp.sum(diagonal, axis=k, keepdims=True)) for k in (0, 1))

    both = gauss_solve(g01, jnp.concatenate([g00, eye], axis=1), gains(g01))
    mine = jnp.where(
        lax.broadcasted_iota(jnp.int32, (n, ncase), 0)
        == lax.broadcasted_iota(jnp.int32, (n, ncase), 1) + my_c * ncase,
        1.0,
        0.0,
    )
    chosen = exact(jnp.concatenate([both[:, 0:n], g01], axis=0), mine)
    first_step, g01_mine, inverse = chosen[0:n], chosen[n:2 * n], both[:, n:2 * n]
    for j in range(chunks):
        if j == chunks - 1:
            collect(3)
            g11 = gram_in(2)
            over = exact(inverse, g11)
            side = exact(g11, jnp.concatenate([over, first_step], axis=1))
        near_at = finish_second(j, near_at)
    forward(4)
    g12 = gram_in(3)
    beta = gauss_solve(g12 - sym(side[:, 0:n]), side[:, n:] - g01_mine, gains(g12))
    alpha = first_step + exact(over, beta)
    coefs = jnp.concatenate([alpha, -beta], axis=0).T
    ctop, clow = split(coefs)
    stack = jnp.concatenate([ctop, clow], axis=0)

    def mix(f):
        band = slice(f * allcase, (f + 2) * allcase)
        lead = mm(stack, rows_top[band, :])
        return lead[0:ncase] + lead[ncase:] + mm(ctop, rows_low[band, :])

    answer_rows = mix(0)
    for d in range(pd):
        sol_ref[d] = answer_rows[:, d * nport:(d + 1) * nport]
    collect(4)
    if chunks > 1:
        forward(2, 2)
    far_rows = mix(3)
    for d in range(pd):
        nat_far[d] = far_rows[:, d * nport:(d + 1) * nport]
    answer = jnp.concatenate([sol_ref[:, k, :] for k in range(ncase)], axis=0)
    near = wide(pick(answer, near_in), pd)
    ends = jnp.concatenate(
        [near, jnp.concatenate([nat_far[:, k, :] for k in range(ncase)], axis=1)], axis=0
    )
    scaled = inv_keep[...] / stiff
    forward(2, lanes_of[2][-1])
    back = scaled - apply_tables(red_tab, ends, masks)
    for k in range(ncase):
        bub_ref[:, k, :] = back[:, k * ncomp:(k + 1) * ncomp]
    collect(2)
    drop_rows = mix(1)
    for d in range(pd):
        res_ref[d] = lines(gath.at[0, my_c], d) - drop_rows[:, d * nport:(d + 1) * nport]

    wait_on(far_send.at[:, :, rest], send_sem.at[0])
    wait_on(gath.at[:, pl.ds(1, nq - 1)], send_sem.at[1])
    wait_on(gram_recv.at[:, others], send_sem.at[2])
    wait_on(ask_send.at[rest], send_sem.at[3])


def emit(*refs):
    count = len(refs) // 2
    sems = refs[-1]
    copies = [
        pltpu.make_async_copy(refs[i], refs[count + i], sems.at[i]) for i in range(count)
    ]
    for copy in copies:
        copy.start()
    for copy in copies:
        copy.wait()


def local(
    comp_type,
    stiffness,
    near_port,
    far_owner,
    far_port,
    bubble_load,
    port_load,
    bubble_inverse,
    coupling,
    port_block,
):
    npy = lax.axis_size("py")
    parts = lax.axis_size("px") * npy
    nq = lax.axis_size("case")
    ncomp = comp_type.shape[0]
    modes, ncase, _ = bubble_load.shape
    pd, _, nport = port_load.shape
    kinds = bubble_inverse.shape[0]
    cap = 3 * ncomp // (2 * parts)
    depth = -(-cap // 8) * 8
    allcase = nq * ncase
    width = 128 if (ncase * pd) % 128 == 0 else ncase * pd
    chunks = ncase * pd // width
    fold = max(1, 128 // allcase)
    vmem = pl.BlockSpec(memory_space=pltpu.VMEM)
    hbm = pl.BlockSpec(memory_space=pltpu.HBM)

    def body(*refs):
        kernel((parts, npy, nq, depth, width, chunks, fold), *refs)

    shapes = (
        jax.ShapeDtypeStruct(port_load.shape, F32),
        jax.ShapeDtypeStruct(port_load.shape, F32),
        jax.ShapeDtypeStruct(bubble_load.shape, F32),
    )
    results = pl.pallas_call(
        body,
        out_shape=shapes,
        in_specs=[hbm] * 10,
        out_specs=(vmem, vmem, vmem),
        scratch_shapes=[
            pltpu.VMEM((1, ncomp), jnp.int32),
            pltpu.VMEM((1, ncomp), jnp.int32),
            pltpu.VMEM((1, ncomp), jnp.int32),
            pltpu.VMEM((1, ncomp), jnp.int32),
            pltpu.VMEM((1, ncomp), F32),
            pltpu.VMEM(bubble_load.shape, F32),
            pltpu.VMEM(port_load.shape, F32),
            pltpu.VMEM(bubble_inverse.shape, F32),
            pltpu.VMEM((kinds, modes, 2 * pd), F32),
            pltpu.VMEM(port_block.shape, F32),
            pltpu.VMEM((parts, 1, 3 * ncomp), F32),
            pltpu.VMEM((parts, 1, 3 * ncomp), F32),
            pltpu.VMEM((5, chunks, parts, depth, width), F32),
            pltpu.VMEM((5, chunks, parts, depth, width), F32),
            pltpu.VMEM((5, nq, ncase * pd, nport), F32),
            pltpu.VMEM((ncase * pd, nport), F32),
            pltpu.VMEM((5 * allcase, pd * nport), BF16),
            pltpu.VMEM((5 * allcase, pd * nport), BF16),
            pltpu.VMEM((4, ncase // fold, fold * allcase), F32),
            pltpu.VMEM((4, nq * parts, ncase // fold, fold * allcase), F32),
            pltpu.VMEM((modes, ncase * ncomp), F32),
            pltpu.VMEM((pd, ncase, nport), F32),
            pltpu.SemaphoreType.DMA((10,)),
            pltpu.SemaphoreType.DMA((4,)),
            pltpu.SemaphoreType.DMA((1 + 5 * chunks,)),
            pltpu.SemaphoreType.DMA((6, nq - 1)),
            pltpu.SemaphoreType.DMA((4,)),
        ],
        compiler_params=pltpu.CompilerParams(
            collective_id=0, has_side_effects=True, vmem_limit_bytes=32 * 1024 * 1024
        ),
        name="condensed_solve",
    )(
        *(
            pltpu.with_memory_space_constraint(x, pltpu.HBM)
            for x in (
                comp_type.reshape(1, ncomp),
                near_port.reshape(1, ncomp),
                far_owner.reshape(1, ncomp),
                far_port.reshape(1, ncomp),
                stiffness.reshape(1, ncomp),
                bubble_load,
                port_load,
                bubble_inverse,
                jnp.swapaxes(coupling, 1, 2),
                port_block,
            )
        )
    )
    return pl.pallas_call(
        emit,
        out_shape=shapes,
        in_specs=[vmem] * 3,
        out_specs=(hbm, hbm, hbm),
        scratch_shapes=[pltpu.SemaphoreType.DMA((3,))],
        compiler_params=pltpu.CompilerParams(vmem_limit_bytes=4 * 1024 * 1024),
        name="emit",
    )(*results)


def solution(mesh):
    placed = (
        P(("px", "py")),
        P(("px", "py")),
        P(("px", "py")),
        P(("px", "py"), None),
        P(("px", "py")),
        P(None, "case", ("px", "py")),
        P(None, "case", ("px", "py")),
        P(),
        P(),
        P(),
    )
    return jax.shard_map(
        local,
        mesh=mesh,
        in_specs=placed,
        out_specs=(
            P(None, "case", ("px", "py")),
            P(None, "case", ("px", "py")),
            P(None, "case", ("px", "py")),
        ),
        check_vma=False,
    )
```

```python
import jax
import jax.numpy as jnp
from jax import lax
from jax.experimental import pallas as pl
from jax.experimental.pallas import tpu as pltpu
from jax.sharding import PartitionSpec as P

HIGH = lax.Precision.HIGHEST
F32 = jnp.float32
BF16 = jnp.bfloat16
MESH = pl.DeviceIdType.MESH
NT = (((1,), (1,)), ((), ()))
TN = (((0,), (0,)), ((), ()))


def split(x):
    top = x.astype(BF16)
    return top, (x - top.astype(F32)).astype(BF16)


def mm(a, b):
    return jnp.dot(a, b, preferred_element_type=F32)


def exact(a, b, dims=(((1,), (0,)), ((), ()))):
    return lax.dot_general(a, b, dims, precision=HIGH, preferred_element_type=F32)


def invert(a, b, c, d):
    scale = 1.0 / (a * d - b * c)
    return d * scale, -b * scale, -c * scale, a * scale


def times(m, x):
    return m[0] * x[0] + m[1] * x[1], m[2] * x[0] + m[3] * x[1]


def gauss_solve(matrix, target, gain):
    n = matrix.shape[0]
    gain_row, gain_col = gain
    aug = jnp.concatenate([matrix * gain_row, target], axis=1) * gain_col
    rows = lax.broadcasted_iota(jnp.int32, aug.shape, 0)
    for j in range(0, n, 4):
        cols = [jnp.broadcast_to(aug[:, j + k:j + k + 1], aug.shape) for k in range(4)]
        line = [aug[j + k:j + k + 1, :] for k in range(4)]
        p = [[cols[k][j + i:j + i + 1, :] for k in range(4)] for i in range(4)]
        lead = invert(p[0][0], p[0][1], p[1][0], p[1][1])
        left, right = times(lead, (p[0][2], p[1][2])), times(lead, (p[0][3], p[1][3]))
        low = (p[2][0], p[2][1], p[3][0], p[3][1])
        under_left, under_right = times(low, left), times(low, right)
        tail = invert(
            p[2][2] - under_left[0],
            p[2][3] - under_right[0],
            p[3][2] - under_left[1],
            p[3][3] - under_right[1],
        )
        top = times(lead, (line[0], line[1]))
        carried = times(low, top)
        new2, new3 = times(tail, (line[2] - carried[0], line[3] - carried[1]))
        new0 = top[0] - left[0] * new2 - right[0] * new3
        new1 = top[1] - left[1] * new2 - right[1] * new3
        aug = (aug - cols[0] * new0 - cols[1] * new1) - (cols[2] * new2 + cols[3] * new3)
        for k, new in enumerate((new0, new1, new2, new3)):
            aug = jnp.where(rows == j + k, new, aug)
    return aug[:, n:] * gain_col


def kernel(
    sizes,
    kind_hbm,
    near_hbm,
    owner_hbm,
    far_hbm,
    stiff_hbm,
    bload_hbm,
    pload_hbm,
    binv_hbm,
    coup_hbm,
    pblock_hbm,
    sol_ref,
    res_ref,
    bub_ref,
    kind_ref,
    near_ref,
    owner_ref,
    far_ref,
    stiff_ref,
    bload_ref,
    pload_ref,
    binv_ref,
    coup_ref,
    pblock_ref,
    ask_send,
    ask_recv,
    far_send,
    far_recv,
    gath,
    bent_rows,
    rows_top,
    rows_low,
    gram_send,
    gram_recv,
    inv_keep,
    nat_far,
    in_sem,
    send_sem,
    part_rsem,
    case_rsem,
    gram_rsem,
):
    parts, npy, nq, depth, width, chunks, fold = sizes
    my_x, my_y, my_c = lax.axis_index("px"), lax.axis_index("py"), lax.axis_index("case")
    me = my_x * npy + my_y

    def part_id(step):
        other = lax.rem(me + step + parts, parts)
        return (other // npy, lax.rem(other, npy), my_c)

    def case_to(step):
        if nq == 4:
            other = my_c + (step % 2) * (1 - 2 * lax.rem(my_c, 2))
            return other + (step // 2) * (2 - 4 * (my_c // 2))
        return lax.rem(my_c + step, nq)

    def case_from(step):
        return case_to(step) if nq == 4 else lax.rem(my_c + nq - step, nq)

    def case_id(step):
        return (my_x, my_y, case_to(step))

    direct = (1, 2) if nq == 4 else tuple(range(1, nq))

    barrier = pltpu.get_barrier_semaphore()

    order = sorted(range(1, parts), key=lambda i: -min(i % npy, npy - i % npy))
    if npy == 4 and parts == 2 * npy:
        half = my_y // 2
        rows = (3 - 3 * half, 2 - half, my_y + 1 - 2 * lax.rem(my_y, 2), my_y)
        order = [
            lax.rem(x * npy + y - me + parts, parts)
            for y in rows
            for x in ((1 - my_x, my_x) if y is not my_y else (1 - my_x,))
        ]

    def each_other(act):
        def per_part(i, _):
            for q in reversed(range(nq)):
                act(i, q)
            return 0

        if parts <= 8:
            for i in order:
                per_part(i, 0)
        else:
            lax.fori_loop(1, parts, per_part, 0)
        for q in reversed(range(1, nq)):
            act(0, q)

    def device(i, q):
        x, y, _ = part_id(i)
        return (x, y, case_to(q))

    def greet_part(i, _):
        pl.semaphore_signal(barrier, inc=1, device_id=part_id(i), device_id_type=MESH)
        return 0

    lax.fori_loop(1, parts, greet_part, 0)
    for i in range(1, nq):
        pl.semaphore_signal(barrier, inc=1, device_id=case_id(i), device_id_type=MESH)

    inputs = (
        (near_hbm, near_ref),
        (owner_hbm, owner_ref),
        (far_hbm, far_ref),
        (kind_hbm, kind_ref),
        (stiff_hbm, stiff_ref),
        (binv_hbm, binv_ref),
        (bload_hbm, bload_ref),
        (coup_hbm, coup_ref),
        (pload_hbm, pload_ref),
        (pblock_hbm, pblock_ref),
    )
    fetches = [
        pltpu.make_async_copy(src, dst, in_sem.at[i]) for i, (src, dst) in enumerate(inputs)
    ]
    for fetch in fetches:
        fetch.start()

    kinds = binv_ref.shape[0]
    modes, ncase, ncomp = bload_ref.shape
    pd = pload_ref.shape[0]
    nport = pload_ref.shape[2]
    slots = parts * depth
    allcase = nq * ncase

    for fetch in fetches[0:5]:
        fetch.wait()
    kind_row = kind_ref[...]
    near_row = near_ref[...]
    owner_row = owner_ref[...]
    far_row = far_ref[...]

    def as_column(row):
        return jnp.broadcast_to(row.astype(F32), (ncomp, ncomp)).T

    sub = lax.broadcasted_iota(jnp.int32, (ncomp, ncomp), 0)
    lane = lax.broadcasted_iota(jnp.int32, (ncomp, ncomp), 1)
    same = (as_column(owner_row) == owner_row.astype(F32)) & (sub < lane)
    rank = jnp.sum(jnp.where(same, 1.0, 0.0), axis=0, keepdims=True).astype(jnp.int32)
    step_row = lax.rem(owner_row - me + parts, parts)
    slot_row = step_row * depth + rank
    slot_sub = lax.broadcasted_iota(jnp.int32, (slots, ncomp), 0)
    slot_pick = jnp.where(slot_sub == slot_row, 1.0, 0.0).astype(BF16)
    step_sub = lax.broadcasted_iota(jnp.int32, (parts, ncomp), 0)
    def send_parts(src, dst, e, sign):
        def body(i, _):
            pltpu.make_async_remote_copy(
                src_ref=src(i),
                dst_ref=dst(i),
                send_sem=send_sem.at[0 if e else 3],
                recv_sem=part_rsem.at[e],
                device_id=part_id(i if sign > 0 else -i),
                device_id_type=MESH,
            ).start()
            return 0

        if parts <= 8:
            for i in order:
                body(i if sign > 0 else parts - i, 0)
        else:
            lax.fori_loop(1, parts, body, 0)

    def wait_on(ref, sem):
        pltpu.make_async_copy(ref, ref, sem).wait()

    rest = pl.ds(1, parts - 1)

    def tile_cases(row):
        return jnp.concatenate([row] * ncase, axis=1)

    def kind_masks(row):
        row = tile_cases(row)
        return [jnp.where(row == t, 1.0, 0.0).astype(BF16) for t in range(kinds)]

    masks = kind_masks(kind_row)

    def table(parts_of):
        top, low = split(parts_of)
        return top, jnp.concatenate([top, low], axis=0)

    def apply_tables(tab, x, masks):
        top, low = split(x)
        lanes = x.shape[1]
        xt = jnp.concatenate([top * m[:, :lanes] for m in masks], axis=0)
        xl = jnp.concatenate([low * m[:, :lanes] for m in masks], axis=0)
        lead = mm(tab[1], xt)
        rows = tab[0].shape[0]
        return lead[:rows] + lead[rows:] + mm(tab[0], xl)

    def wide(field, rows):
        return jnp.concatenate(
            [field[k * rows:(k + 1) * rows] for k in range(field.shape[0] // rows)], axis=1
        )

    def tall(x, count):
        return jnp.concatenate(
            [x[:, k * count:(k + 1) * count] for k in range(x.shape[1] // count)], axis=0
        )

    def pick(x, onehot):
        top, low = split(x)
        return mm(jnp.concatenate([top, low], axis=1), jnp.concatenate([onehot, onehot], axis=0))

    def at_slots(onehot, x):
        top, low = split(x)
        return lax.dot_general(
            jnp.concatenate([onehot, onehot], axis=1),
            jnp.concatenate([top, low], axis=1),
            NT,
            preferred_element_type=F32,
        )

    def place(x, onehot):
        top, low = split(x)
        return mm(top, onehot) + mm(low, onehot)

    def take(e, j):
        wait_on(far_recv.at[e, j, rest], part_rsem.at[1 + e * chunks + j])
        return far_recv[e, j].reshape(slots, width).T

    def post(e, j, out, sign):
        far_send[e, j] = out
        far_recv[e, j, 0] = out[0]
        send_parts(
            lambda i: far_send.at[e, j, i], lambda i: far_recv.at[e, j, i], 1 + e * chunks + j, sign
        )

    cuts = [0] + [((j + 1) * width) // pd for j in range(chunks)]

    def span(f, j):
        if f in (1, 2):
            return pl.ds(cuts[j] * pd, (cuts[j + 1] - cuts[j]) * pd)
        return pl.ds(j * width, width)

    lanes_of = {f: (f,) for f in range(5)}
    if chunks > 1:
        lanes_of[2] = (2, 5)

    def lane_span(lane):
        if lane == 5:
            return span(2, chunks - 1)
        return pl.ds(0, cuts[chunks - 1] * pd if lane == 2 and chunks > 1 else ncase * pd)

    def send_case(lane, block, sem, step):
        pltpu.make_async_remote_copy(
            src_ref=block,
            dst_ref=block,
            send_sem=send_sem.at[1],
            recv_sem=case_rsem.at[lane, sem - 1],
            device_id=case_id(step),
            device_id_type=MESH,
        ).start()

    def publish(f, j, rows):
        gath[f, my_c, span(f, j)] = rows
        lane = lanes_of[f][-1] if j == chunks - 1 else f
        for i in reversed(direct):
            send_case(lane, gath.at[f, my_c, span(f, j)], i, i)

    def forward(f, *lanes):
        if nq == 4:
            for lane in lanes or lanes_of[f]:
                block = gath.at[f, case_from(2), lane_span(lane)]
                wait_on(block, case_rsem.at[lane, 1])
                send_case(lane, block, 3, 1)

    def lines(ref, d):
        return ref[pl.ds(d, ncase, stride=pd), :]

    def collect(f):
        for i in range(1, nq):
            if nq != 4 or i != 2:
                for lane in lanes_of[f]:
                    wait_on(gath.at[f, case_from(i), lane_span(lane)], case_rsem.at[lane, i - 1])

        def body(d, _):
            cols = pl.ds(pl.multiple_of(d * nport, nport), nport)
            block = jnp.concatenate([lines(gath.at[f, q], d) for q in range(nq)], axis=0)
            top, low = split(block)
            rows_top[f * allcase:(f + 1) * allcase, cols] = top
            rows_low[f * allcase:(f + 1) * allcase, cols] = low
            return 0

        lax.fori_loop(0, pd, body, 0, unroll=16)

    def against(x, f):
        top, low = split(x)
        band = slice(f * allcase, (f + 1) * allcase)
        lead = lax.dot_general(
            jnp.concatenate([top, low], axis=0),
            rows_top[band, :],
            NT,
            preferred_element_type=F32,
        )
        low_lead = lax.dot_general(
            jnp.concatenate([top, low], axis=0),
            rows_low[band, :],
            NT,
            preferred_element_type=F32,
        )
        total = lead + low_lead
        return total[:x.shape[0]] + total[x.shape[0]:]

    def own_rows(f):
        return jnp.concatenate([lines(gath.at[f, my_c], d) for d in range(pd)], axis=1)

    def gram_out(s, block):
        high = ncase // fold
        folded = jnp.concatenate([block[r * high:(r + 1) * high] for r in range(fold)], axis=1)
        gram_send[s] = folded
        gram_recv[s, my_c * parts] = folded

        def send(i, q):
            pltpu.make_async_remote_copy(
                src_ref=gram_send.at[s],
                dst_ref=gram_recv.at[s, my_c * parts + i],
                send_sem=send_sem.at[2],
                recv_sem=gram_rsem.at[s],
                device_id=device(i, q),
                device_id_type=MESH,
            ).start()

        each_other(send)

    others = pl.ds(1, nq * parts - 1)

    def gram_in(s):
        wait_on(gram_recv.at[s, others], gram_rsem.at[s])
        rows = []
        for q in range(nq):
            total = jnp.sum(gram_recv[s, q * parts:(q + 1) * parts], axis=0)
            for r in range(fold):
                rows.append(total[:, r * allcase:(r + 1) * allcase])
        return sym(jnp.concatenate(rows, axis=0))

    def sym(g):
        return 0.5 * (g + g.T)

    def part(x, j):
        return x[j * width:(j + 1) * width]

    for fetch in fetches[5:8]:
        fetch.wait()
    inv_tab = table(jnp.concatenate([binv_ref[t] for t in range(kinds)], axis=1))
    coup_tab = table(jnp.concatenate([coup_ref[t].T for t in range(kinds)], axis=1))
    ready = [0] + [-(-((j + 1) * width) // pd) for j in range(chunks)]
    condensed_near, leaving = [], None
    for j in range(chunks):
        a, b = ready[j], ready[j + 1]
        loads = jnp.concatenate([bload_ref[:, k, :] for k in range(a, b)], axis=1)
        lifted = apply_tables(inv_tab, loads, masks)
        inv_keep[:, a * ncomp:b * ncomp] = lifted
        condensed = -apply_tables(coup_tab, lifted, masks)
        condensed_near.append(tall(condensed[:pd], ncomp))
        out = tall(condensed[pd:], ncomp)
        leaving = out if leaving is None else jnp.concatenate([leaving, out], axis=0)
        if j == 0:
            naming = jnp.concatenate(
                [
                    jnp.where(step_sub == step_row, row, 0.0)
                    for row in ((far_row + 1).astype(F32), kind_row.astype(F32), stiff_ref[...])
                ],
                axis=0,
            )
            ranked = jnp.where(sub == rank, 1.0, 0.0)
            wanted = exact(naming, ranked, NT)
            wanted = jnp.concatenate([wanted[r * parts:(r + 1) * parts] for r in range(3)], axis=1)
            wanted = wanted.reshape(parts, 1, 3 * ncomp)
            ask_send[...] = wanted
            ask_recv[0] = wanted[0]
            pl.semaphore_wait(barrier, parts + nq - 2)
            send_parts(lambda i: ask_send.at[i], lambda i: ask_recv.at[i], 0, 1)
        post(0, j, at_slots(slot_pick, part(leaving, j)).reshape(parts, depth, width), 1)
    for fetch in fetches[8:]:
        fetch.wait()
    near_in = jnp.where(sub == near_row, 1.0, 0.0).astype(BF16)
    near_out = jnp.where(lane.astype(F32) == as_column(near_row), 1.0, 0.0).astype(BF16)
    near_slots = lax.dot_general(slot_pick, near_in, NT, preferred_element_type=F32).astype(BF16)

    stiff = tile_cases(stiff_ref[...])
    red_t = [exact(binv_ref[t], coup_ref[t], TN) for t in range(kinds)]
    schur = [pblock_ref[t] - exact(red_t[t], coup_ref[t], TN) for t in range(kinds)]

    def corner(a, b):
        rows, cols = slice(a * pd, (a + 1) * pd), slice(b * pd, (b + 1) * pd)
        return table(jnp.concatenate([schur[t][rows, cols] for t in range(kinds)], axis=1))

    nn_tab, nf_tab, fn_tab, ff_tab = corner(0, 0), corner(0, 1), corner(1, 0), corner(1, 1)
    red_tab = table(jnp.concatenate(red_t, axis=1))
    own = jnp.concatenate([pload_ref[:, k, :] for k in range(ncase)], axis=0)
    own = own + pick(jnp.concatenate(condensed_near, axis=0), near_out)
    wait_on(ask_recv.at[rest], part_rsem.at[0])
    asked = ask_recv[...].reshape(parts, 3 * ncomp)
    ports = jnp.concatenate([asked[:, 0:ncomp]] * (ncomp // parts), axis=0).T
    port_lane = lax.broadcasted_iota(jnp.int32, (depth, nport), 1).astype(F32)
    asked_pick = jnp.concatenate(
        [jnp.where(ports[0:depth, i:i + 1] - 1.0 == port_lane, 1.0, 0.0) for i in range(parts)],
        axis=0,
    ).astype(BF16)

    def slot_line(r):
        return jnp.concatenate(
            [asked[i:i + 1, r * ncomp:r * ncomp + depth] for i in range(parts)], axis=1
        )

    slot_masks = kind_masks(slot_line(1))
    slot_stiff = tile_cases(slot_line(2))

    def scatter(e, j, piece):
        post(e, j, at_slots(asked_pick, piece).reshape(parts, depth, width), -1)

        def rest_of_it():
            post(e + 1, j, at_slots(near_slots, piece).reshape(parts, depth, width), 1)

        return rest_of_it

    def join(a, b):
        return b if a is None else jnp.concatenate([a, b], axis=0)

    def near_side(tab, x, a, b):
        return apply_tables(tab, wide(x, pd), masks) * stiff[:, a * ncomp:b * ncomp]

    def far_side(tab, x, a, b):
        return apply_tables(tab, wide(x, pd), slot_masks) * slot_stiff[:, a * slots:b * slots]

    def near_ports(y):
        return pick(tall(y, ncomp), near_out)

    def far_ports(y):
        return place(tall(y, slots), asked_pick)

    def diagonal(e, field):
        y_near = near_side(nn_tab, pick(field, near_in), 0, ncase)
        far_at = [far_send[e, j].reshape(slots, width).T for j in range(chunks)]
        return y_near, far_side(ff_tab, jnp.concatenate(far_at, axis=0), 0, ncase)

    def take_far_values(e, j):
        return place(take(e, j), slot_pick)

    base = None
    for j in range(chunks):
        piece = part(own, j) + place(take(0, j), asked_pick)
        scatter(1, j, piece)()
        publish(0, j, piece)
        base = join(base, piece)

    y_near, y_far = diagonal(1, base)
    far_base, near_at, first, sent, later = None, None, None, 0, []
    for j in range(chunks):
        a, b = cuts[j], cuts[j + 1]
        if j == chunks - 1:
            forward(0)
        piece = take_far_values(1, j)
        publish(3, j, piece)
        far_base = join(far_base, piece)
        near_at = join(near_at, take(2, j))
        rows = slice(a * pd, b * pd)
        y = y_near[:, a * ncomp:b * ncomp] + near_side(nf_tab, far_base[rows], a, b)
        done = near_ports(y)
        y = y_far[:, a * slots:b * slots] + far_side(fn_tab, near_at[rows], a, b)
        done = done + far_ports(y)
        first = join(first, done)
        while (sent + 1) * width <= b * pd:
            later.append(scatter(3, sent, part(first, sent)))
            sent += 1
        publish(1, j, done)

    y_near, y_far = diagonal(3, first)
    straight = near_ports(y_near) + far_ports(y_far)
    collect(0)
    early = against(jnp.concatenate([own_rows(0), own_rows(1)], axis=0), 0)
    gram_out(1, early[ncase:])
    gram_out(0, early[:ncase])
    far_first, crossed = None, None
    for j in range(chunks):
        a, b = cuts[j], cuts[j + 1]
        if j == chunks - 1:
            forward(1)
            forward(3)
            collect(1)
            gram_out(2, against(own_rows(1), 1))
        piece = take_far_values(3, j)
        publish(4, j, piece)
        far_first = join(far_first, piece)
        crossed = join(crossed, near_ports(near_side(nf_tab, far_first[a * pd:b * pd], a, b)))
        if j < chunks - 1:
            later[j]()
    bent_rows[...] = straight + 2.0 * crossed
    bent = jnp.concatenate([lines(bent_rows, d) for d in range(pd)], axis=1)
    gram_out(3, against(bent, 1))
    later[chunks - 1]()

    n = allcase
    eye = jnp.where(
        lax.broadcasted_iota(jnp.int32, (n, n), 0) == lax.broadcasted_iota(jnp.int32, (n, n), 1),
        1.0,
        0.0,
    )
    near_at = None

    def finish_second(j, near_at):
        a, b = cuts[j], cuts[j + 1]
        rows = slice(a * pd, b * pd)
        near_at = join(near_at, take(4, j))
        y = far_side(fn_tab, near_at[rows], a, b)
        publish(2, j, straight[rows] + crossed[rows] + far_ports(y))
        return near_at

    g01, g00 = gram_in(1), gram_in(0)

    def gains(g):
        diagonal = g * eye
        return tuple(lax.rsqrt(jnp.sum(diagonal, axis=k, keepdims=True)) for k in (0, 1))

    both = gauss_solve(g01, jnp.concatenate([g00, eye], axis=1), gains(g01))
    mine = jnp.where(
        lax.broadcasted_iota(jnp.int32, (n, ncase), 0)
        == lax.broadcasted_iota(jnp.int32, (n, ncase), 1) + my_c * ncase,
        1.0,
        0.0,
    )
    chosen = exact(jnp.concatenate([both[:, 0:n], g01], axis=0), mine)
    first_step, g01_mine, inverse = chosen[0:n], chosen[n:2 * n], both[:, n:2 * n]
    for j in range(chunks):
        if j == chunks - 1:
            collect(3)
            g11 = gram_in(2)
            over = exact(inverse, g11)
            side = exact(g11, jnp.concatenate([over, first_step], axis=1))
        near_at = finish_second(j, near_at)
    forward(4)
    g12 = gram_in(3)
    beta = gauss_solve(g12 - sym(side[:, 0:n]), side[:, n:] - g01_mine, gains(g12))
    alpha = first_step + exact(over, beta)
    coefs = jnp.concatenate([alpha, -beta], axis=0).T
    ctop, clow = split(coefs)
    stack = jnp.concatenate([ctop, clow], axis=0)

    def mix(f, low=0, high=2):
        band = slice((f + low) * allcase, (f + high) * allcase)
        cols = slice(low * allcase, high * allcase)
        lead = mm(stack[:, cols], rows_top[band, :])
        return lead[0:ncase] + lead[ncase:] + mm(ctop[:, cols], rows_low[band, :])

    answer_rows = mix(0)
    for d in range(pd):
        sol_ref[d] = answer_rows[:, d * nport:(d + 1) * nport]
    collect(4)
    if chunks > 1:
        forward(2, 2)
    far_rows = mix(3)
    for d in range(pd):
        nat_far[d] = far_rows[:, d * nport:(d + 1) * nport]
    answer = jnp.concatenate([sol_ref[:, k, :] for k in range(ncase)], axis=0)
    near = wide(pick(answer, near_in), pd)
    ends = jnp.concatenate(
        [near, jnp.concatenate([nat_far[:, k, :] for k in range(ncase)], axis=1)], axis=0
    )
    scaled = inv_keep[...] / stiff
    forward(2, lanes_of[2][-1])
    settled = mix(1, 0, 1)
    for d in range(pd):
        res_ref[d] = lines(gath.at[0, my_c], d) - settled[:, d * nport:(d + 1) * nport]
    back = scaled - apply_tables(red_tab, ends, masks)
    for k in range(ncase):
        bub_ref[:, k, :] = back[:, k * ncomp:(k + 1) * ncomp]
    collect(2)
    drop_rows = mix(1, 1, 2)
    for d in range(pd):
        res_ref[d] = res_ref[d] - drop_rows[:, d * nport:(d + 1) * nport]

    wait_on(far_send.at[:, :, rest], send_sem.at[0])
    wait_on(gath.at[:, pl.ds(1, nq - 1)], send_sem.at[1])
    wait_on(gram_recv.at[:, others], send_sem.at[2])
    wait_on(ask_send.at[rest], send_sem.at[3])


def emit(*refs):
    count = len(refs) // 2
    sems = refs[-1]
    copies = [
        pltpu.make_async_copy(refs[i], refs[count + i], sems.at[i]) for i in range(count)
    ]
    for copy in copies:
        copy.start()
    for copy in copies:
        copy.wait()


def local(
    comp_type,
    stiffness,
    near_port,
    far_owner,
    far_port,
    bubble_load,
    port_load,
    bubble_inverse,
    coupling,
    port_block,
):
    npy = lax.axis_size("py")
    parts = lax.axis_size("px") * npy
    nq = lax.axis_size("case")
    ncomp = comp_type.shape[0]
    modes, ncase, _ = bubble_load.shape
    pd, _, nport = port_load.shape
    kinds = bubble_inverse.shape[0]
    cap = 3 * ncomp // (2 * parts)
    depth = -(-cap // 8) * 8
    allcase = nq * ncase
    width = 128 if (ncase * pd) % 128 == 0 else ncase * pd
    chunks = ncase * pd // width
    fold = max(1, 128 // allcase)
    vmem = pl.BlockSpec(memory_space=pltpu.VMEM)
    hbm = pl.BlockSpec(memory_space=pltpu.HBM)

    def body(*refs):
        kernel((parts, npy, nq, depth, width, chunks, fold), *refs)

    shapes = (
        jax.ShapeDtypeStruct(port_load.shape, F32),
        jax.ShapeDtypeStruct(port_load.shape, F32),
        jax.ShapeDtypeStruct(bubble_load.shape, F32),
    )
    results = pl.pallas_call(
        body,
        out_shape=shapes,
        in_specs=[hbm] * 10,
        out_specs=(vmem, vmem, vmem),
        scratch_shapes=[
            pltpu.VMEM((1, ncomp), jnp.int32),
            pltpu.VMEM((1, ncomp), jnp.int32),
            pltpu.VMEM((1, ncomp), jnp.int32),
            pltpu.VMEM((1, ncomp), jnp.int32),
            pltpu.VMEM((1, ncomp), F32),
            pltpu.VMEM(bubble_load.shape, F32),
            pltpu.VMEM(port_load.shape, F32),
            pltpu.VMEM(bubble_inverse.shape, F32),
            pltpu.VMEM((kinds, modes, 2 * pd), F32),
            pltpu.VMEM(port_block.shape, F32),
            pltpu.VMEM((parts, 1, 3 * ncomp), F32),
            pltpu.VMEM((parts, 1, 3 * ncomp), F32),
            pltpu.VMEM((5, chunks, parts, depth, width), F32),
            pltpu.VMEM((5, chunks, parts, depth, width), F32),
            pltpu.VMEM((5, nq, ncase * pd, nport), F32),
            pltpu.VMEM((ncase * pd, nport), F32),
            pltpu.VMEM((5 * allcase, pd * nport), BF16),
            pltpu.VMEM((5 * allcase, pd * nport), BF16),
            pltpu.VMEM((4, ncase // fold, fold * allcase), F32),
            pltpu.VMEM((4, nq * parts, ncase // fold, fold * allcase), F32),
            pltpu.VMEM((modes, ncase * ncomp), F32),
            pltpu.VMEM((pd, ncase, nport), F32),
            pltpu.SemaphoreType.DMA((10,)),
            pltpu.SemaphoreType.DMA((4,)),
            pltpu.SemaphoreType.DMA((1 + 5 * chunks,)),
            pltpu.SemaphoreType.DMA((6, nq - 1)),
            pltpu.SemaphoreType.DMA((4,)),
        ],
        compiler_params=pltpu.CompilerParams(
            collective_id=0, has_side_effects=True, vmem_limit_bytes=32 * 1024 * 1024
        ),
        name="condensed_solve",
    )(
        *(
            pltpu.with_memory_space_constraint(x, pltpu.HBM)
            for x in (
                comp_type.reshape(1, ncomp),
                near_port.reshape(1, ncomp),
                far_owner.reshape(1, ncomp),
                far_port.reshape(1, ncomp),
                stiffness.reshape(1, ncomp),
                bubble_load,
                port_load,
                bubble_inverse,
                jnp.swapaxes(coupling, 1, 2),
                port_block,
            )
        )
    )
    return pl.pallas_call(
        emit,
        out_shape=shapes,
        in_specs=[vmem] * 3,
        out_specs=(hbm, hbm, hbm),
        scratch_shapes=[pltpu.SemaphoreType.DMA((3,))],
        compiler_params=pltpu.CompilerParams(vmem_limit_bytes=4 * 1024 * 1024),
        name="emit",
    )(*results)


def solution(mesh):
    placed = (
        P(("px", "py")),
        P(("px", "py")),
        P(("px", "py")),
        P(("px", "py"), None),
        P(("px", "py")),
        P(None, "case", ("px", "py")),
        P(None, "case", ("px", "py")),
        P(),
        P(),
        P(),
    )
    return jax.shard_map(
        local,
        mesh=mesh,
        in_specs=placed,
        out_specs=(
            P(None, "case", ("px", "py")),
            P(None, "case", ("px", "py")),
            P(None, "case", ("px", "py")),
        ),
        check_vma=False,
    )
```

```python
import jax
import jax.numpy as jnp
from jax import lax
from jax.experimental import pallas as pl
from jax.experimental.pallas import tpu as pltpu
from jax.sharding import PartitionSpec as P

HIGH = lax.Precision.HIGHEST
F32 = jnp.float32
BF16 = jnp.bfloat16
MESH = pl.DeviceIdType.MESH
NT = (((1,), (1,)), ((), ()))
TN = (((0,), (0,)), ((), ()))


def split(x):
    top = x.astype(BF16)
    return top, (x - top.astype(F32)).astype(BF16)


def mm(a, b):
    return jnp.dot(a, b, preferred_element_type=F32)


def exact(a, b, dims=(((1,), (0,)), ((), ()))):
    return lax.dot_general(a, b, dims, precision=HIGH, preferred_element_type=F32)


def invert(a, b, c, d):
    scale = 1.0 / (a * d - b * c)
    return d * scale, -b * scale, -c * scale, a * scale


def times(m, x):
    return m[0] * x[0] + m[1] * x[1], m[2] * x[0] + m[3] * x[1]


def gauss_solve(matrix, target, gain):
    n = matrix.shape[0]
    gain_row, gain_col = gain
    aug = jnp.concatenate([matrix * gain_row, target], axis=1) * gain_col
    rows = lax.broadcasted_iota(jnp.int32, aug.shape, 0)
    for j in range(0, n, 4):
        cols = [jnp.broadcast_to(aug[:, j + k:j + k + 1], aug.shape) for k in range(4)]
        line = [aug[j + k:j + k + 1, :] for k in range(4)]
        p = [[cols[k][j + i:j + i + 1, :] for k in range(4)] for i in range(4)]
        lead = invert(p[0][0], p[0][1], p[1][0], p[1][1])
        left, right = times(lead, (p[0][2], p[1][2])), times(lead, (p[0][3], p[1][3]))
        low = (p[2][0], p[2][1], p[3][0], p[3][1])
        under_left, under_right = times(low, left), times(low, right)
        tail = invert(
            p[2][2] - under_left[0],
            p[2][3] - under_right[0],
            p[3][2] - under_left[1],
            p[3][3] - under_right[1],
        )
        top = times(lead, (line[0], line[1]))
        carried = times(low, top)
        new2, new3 = times(tail, (line[2] - carried[0], line[3] - carried[1]))
        new0 = top[0] - left[0] * new2 - right[0] * new3
        new1 = top[1] - left[1] * new2 - right[1] * new3
        aug = (aug - cols[0] * new0 - cols[1] * new1) - (cols[2] * new2 + cols[3] * new3)
        for k, new in enumerate((new0, new1, new2, new3)):
            aug = jnp.where(rows == j + k, new, aug)
    return aug[:, n:] * gain_col


def kernel(
    sizes,
    kind_hbm,
    near_hbm,
    owner_hbm,
    far_hbm,
    stiff_hbm,
    bload_hbm,
    pload_hbm,
    binv_hbm,
    coup_hbm,
    pblock_hbm,
    sol_ref,
    res_ref,
    bub_ref,
    kind_ref,
    near_ref,
    owner_ref,
    far_ref,
    stiff_ref,
    bload_ref,
    pload_ref,
    binv_ref,
    coup_ref,
    pblock_ref,
    ask_send,
    ask_recv,
    far_send,
    far_recv,
    gath,
    bent_rows,
    rows_top,
    rows_low,
    gram_send,
    gram_recv,
    inv_keep,
    nat_far,
    in_sem,
    send_sem,
    part_rsem,
    case_rsem,
    gram_rsem,
):
    parts, npy, nq, depth, width, chunks, fold = sizes
    my_x, my_y, my_c = lax.axis_index("px"), lax.axis_index("py"), lax.axis_index("case")
    me = my_x * npy + my_y

    def part_id(step):
        other = lax.rem(me + step + parts, parts)
        return (other // npy, lax.rem(other, npy), my_c)

    def case_to(step):
        if nq == 4:
            other = my_c + (step % 2) * (1 - 2 * lax.rem(my_c, 2))
            return other + (step // 2) * (2 - 4 * (my_c // 2))
        return lax.rem(my_c + step, nq)

    def case_from(step):
        return case_to(step) if nq == 4 else lax.rem(my_c + nq - step, nq)

    def case_id(step):
        return (my_x, my_y, case_to(step))

    direct = (1, 2) if nq == 4 else tuple(range(1, nq))

    barrier = pltpu.get_barrier_semaphore()

    order = sorted(range(1, parts), key=lambda i: -min(i % npy, npy - i % npy))
    if npy == 4 and parts == 2 * npy:
        half = my_y // 2
        rows = (3 - 3 * half, 2 - half, my_y + 1 - 2 * lax.rem(my_y, 2), my_y)
        order = [
            lax.rem(x * npy + y - me + parts, parts)
            for y in rows
            for x in ((1 - my_x, my_x) if y is not my_y else (1 - my_x,))
        ]

    def each_other(act):
        def per_part(i, _):
            for q in reversed(range(nq)):
                act(i, q)
            return 0

        if parts <= 8:
            for i in order:
                per_part(i, 0)
        else:
            lax.fori_loop(1, parts, per_part, 0)
        for q in reversed(range(1, nq)):
            act(0, q)

    def device(i, q):
        x, y, _ = part_id(i)
        return (x, y, case_to(q))

    def greet_part(i, _):
        pl.semaphore_signal(barrier, inc=1, device_id=part_id(i), device_id_type=MESH)
        return 0

    lax.fori_loop(1, parts, greet_part, 0)
    for i in range(1, nq):
        pl.semaphore_signal(barrier, inc=1, device_id=case_id(i), device_id_type=MESH)

    inputs = (
        (near_hbm, near_ref),
        (owner_hbm, owner_ref),
        (far_hbm, far_ref),
        (kind_hbm, kind_ref),
        (stiff_hbm, stiff_ref),
        (binv_hbm, binv_ref),
        (bload_hbm, bload_ref),
        (coup_hbm, coup_ref),
        (pload_hbm, pload_ref),
        (pblock_hbm, pblock_ref),
    )
    fetches = [
        pltpu.make_async_copy(src, dst, in_sem.at[i]) for i, (src, dst) in enumerate(inputs)
    ]
    for fetch in fetches:
        fetch.start()

    kinds = binv_ref.shape[0]
    modes, ncase, ncomp = bload_ref.shape
    pd = pload_ref.shape[0]
    nport = pload_ref.shape[2]
    slots = parts * depth
    allcase = nq * ncase

    for fetch in fetches[0:5]:
        fetch.wait()
    kind_row = kind_ref[...]
    near_row = near_ref[...]
    owner_row = owner_ref[...]
    far_row = far_ref[...]

    def as_column(row):
        return jnp.broadcast_to(row.astype(F32), (ncomp, ncomp)).T

    sub = lax.broadcasted_iota(jnp.int32, (ncomp, ncomp), 0)
    lane = lax.broadcasted_iota(jnp.int32, (ncomp, ncomp), 1)
    same = (as_column(owner_row) == owner_row.astype(F32)) & (sub < lane)
    rank = jnp.sum(jnp.where(same, 1.0, 0.0), axis=0, keepdims=True).astype(jnp.int32)
    step_row = lax.rem(owner_row - me + parts, parts)
    slot_row = step_row * depth + rank
    slot_sub = lax.broadcasted_iota(jnp.int32, (slots, ncomp), 0)
    slot_pick = jnp.where(slot_sub == slot_row, 1.0, 0.0).astype(BF16)
    step_sub = lax.broadcasted_iota(jnp.int32, (parts, ncomp), 0)
    def send_parts(src, dst, e, sign):
        def body(i, _):
            pltpu.make_async_remote_copy(
                src_ref=src(i),
                dst_ref=dst(i),
                send_sem=send_sem.at[0 if e else 3],
                recv_sem=part_rsem.at[e],
                device_id=part_id(i if sign > 0 else -i),
                device_id_type=MESH,
            ).start()
            return 0

        if parts <= 8:
            for i in order:
                body(i if sign > 0 else parts - i, 0)
        else:
            lax.fori_loop(1, parts, body, 0)

    def wait_on(ref, sem):
        pltpu.make_async_copy(ref, ref, sem).wait()

    rest = pl.ds(1, parts - 1)

    def tile_cases(row):
        return jnp.concatenate([row] * ncase, axis=1)

    def kind_masks(row):
        row = tile_cases(row)
        return [jnp.where(row == t, 1.0, 0.0).astype(BF16) for t in range(kinds)]

    masks = kind_masks(kind_row)

    def table(parts_of):
        top, low = split(parts_of)
        return top, jnp.concatenate([top, low], axis=0)

    def apply_tables(tab, x, masks):
        top, low = split(x)
        lanes = x.shape[1]
        xt = jnp.concatenate([top * m[:, :lanes] for m in masks], axis=0)
        xl = jnp.concatenate([low * m[:, :lanes] for m in masks], axis=0)
        lead = mm(tab[1], xt)
        rows = tab[0].shape[0]
        return lead[:rows] + lead[rows:] + mm(tab[0], xl)

    def wide(field, rows):
        return jnp.concatenate(
            [field[k * rows:(k + 1) * rows] for k in range(field.shape[0] // rows)], axis=1
        )

    def tall(x, count):
        return jnp.concatenate(
            [x[:, k * count:(k + 1) * count] for k in range(x.shape[1] // count)], axis=0
        )

    def pick(x, onehot):
        top, low = split(x)
        return mm(jnp.concatenate([top, low], axis=1), jnp.concatenate([onehot, onehot], axis=0))

    def at_slots(onehot, x):
        top, low = split(x)
        return lax.dot_general(
            jnp.concatenate([onehot, onehot], axis=1),
            jnp.concatenate([top, low], axis=1),
            NT,
            preferred_element_type=F32,
        )

    def place(x, onehot):
        top, low = split(x)
        return mm(top, onehot) + mm(low, onehot)

    def take(e, j):
        wait_on(far_recv.at[e, j, rest], part_rsem.at[1 + e * chunks + j])
        return far_recv[e, j].reshape(slots, width).T

    def post(e, j, out, sign):
        far_send[e, j] = out
        far_recv[e, j, 0] = out[0]
        send_parts(
            lambda i: far_send.at[e, j, i], lambda i: far_recv.at[e, j, i], 1 + e * chunks + j, sign
        )

    cuts = [0] + [((j + 1) * width) // pd for j in range(chunks)]

    def span(f, j):
        if f in (1, 2):
            return pl.ds(cuts[j] * pd, (cuts[j + 1] - cuts[j]) * pd)
        return pl.ds(j * width, width)

    lanes_of = {f: (f,) for f in range(5)}
    if chunks > 1:
        lanes_of[2] = (2, 5)

    def lane_span(lane):
        if lane == 5:
            return span(2, chunks - 1)
        return pl.ds(0, cuts[chunks - 1] * pd if lane == 2 and chunks > 1 else ncase * pd)

    def send_case(lane, block, sem, step):
        pltpu.make_async_remote_copy(
            src_ref=block,
            dst_ref=block,
            send_sem=send_sem.at[1],
            recv_sem=case_rsem.at[lane, sem - 1],
            device_id=case_id(step),
            device_id_type=MESH,
        ).start()

    def publish(f, j, rows):
        gath[f, my_c, span(f, j)] = rows
        lane = lanes_of[f][-1] if j == chunks - 1 else f
        for i in reversed(direct):
            send_case(lane, gath.at[f, my_c, span(f, j)], i, i)

    def forward(f, *lanes):
        if nq == 4:
            for lane in lanes or lanes_of[f]:
                block = gath.at[f, case_from(2), lane_span(lane)]
                wait_on(block, case_rsem.at[lane, 1])
                send_case(lane, block, 3, 1)

    def lines(ref, d):
        return ref[pl.ds(d, ncase, stride=pd), :]

    def collect(f):
        for i in range(1, nq):
            if nq != 4 or i != 2:
                for lane in lanes_of[f]:
                    wait_on(gath.at[f, case_from(i), lane_span(lane)], case_rsem.at[lane, i - 1])

        def body(d, _):
            cols = pl.ds(pl.multiple_of(d * nport, nport), nport)
            block = jnp.concatenate([lines(gath.at[f, q], d) for q in range(nq)], axis=0)
            top, low = split(block)
            rows_top[f * allcase:(f + 1) * allcase, cols] = top
            rows_low[f * allcase:(f + 1) * allcase, cols] = low
            return 0

        lax.fori_loop(0, pd, body, 0, unroll=16)

    def against(x, f):
        top, low = split(x)
        band = slice(f * allcase, (f + 1) * allcase)
        lead = lax.dot_general(
            jnp.concatenate([top, low], axis=0),
            rows_top[band, :],
            NT,
            preferred_element_type=F32,
        )
        low_lead = lax.dot_general(
            jnp.concatenate([top, low], axis=0),
            rows_low[band, :],
            NT,
            preferred_element_type=F32,
        )
        total = lead + low_lead
        return total[:x.shape[0]] + total[x.shape[0]:]

    def own_rows(f):
        return jnp.concatenate([lines(gath.at[f, my_c], d) for d in range(pd)], axis=1)

    def gram_out(s, block):
        high = ncase // fold
        folded = jnp.concatenate([block[r * high:(r + 1) * high] for r in range(fold)], axis=1)
        gram_send[s] = folded
        gram_recv[s, my_c * parts] = folded

        def send(i, q):
            pltpu.make_async_remote_copy(
                src_ref=gram_send.at[s],
                dst_ref=gram_recv.at[s, my_c * parts + i],
                send_sem=send_sem.at[2],
                recv_sem=gram_rsem.at[s],
                device_id=device(i, q),
                device_id_type=MESH,
            ).start()

        each_other(send)

    others = pl.ds(1, nq * parts - 1)

    def gram_in(s):
        wait_on(gram_recv.at[s, others], gram_rsem.at[s])
        rows = []
        for q in range(nq):
            total = jnp.sum(gram_recv[s, q * parts:(q + 1) * parts], axis=0)
            for r in range(fold):
                rows.append(total[:, r * allcase:(r + 1) * allcase])
        return sym(jnp.concatenate(rows, axis=0))

    def sym(g):
        return 0.5 * (g + g.T)

    def part(x, j):
        return x[j * width:(j + 1) * width]

    for fetch in fetches[5:8]:
        fetch.wait()
    inv_tab = table(jnp.concatenate([binv_ref[t] for t in range(kinds)], axis=1))
    coup_tab = table(jnp.concatenate([coup_ref[t].T for t in range(kinds)], axis=1))
    ready = [0] + [-(-((j + 1) * width) // pd) for j in range(chunks)]
    condensed_near, leaving = [], None
    for j in range(chunks):
        a, b = ready[j], ready[j + 1]
        loads = jnp.concatenate([bload_ref[:, k, :] for k in range(a, b)], axis=1)
        lifted = apply_tables(inv_tab, loads, masks)
        inv_keep[:, a * ncomp:b * ncomp] = lifted
        condensed = -apply_tables(coup_tab, lifted, masks)
        condensed_near.append(tall(condensed[:pd], ncomp))
        out = tall(condensed[pd:], ncomp)
        leaving = out if leaving is None else jnp.concatenate([leaving, out], axis=0)
        if j == 0:
            naming = jnp.concatenate(
                [
                    jnp.where(step_sub == step_row, row, 0.0)
                    for row in ((far_row + 1).astype(F32), kind_row.astype(F32), stiff_ref[...])
                ],
                axis=0,
            )
            ranked = jnp.where(sub == rank, 1.0, 0.0)
            wanted = exact(naming, ranked, NT)
            wanted = jnp.concatenate([wanted[r * parts:(r + 1) * parts] for r in range(3)], axis=1)
            wanted = wanted.reshape(parts, 1, 3 * ncomp)
            ask_send[...] = wanted
            ask_recv[0] = wanted[0]
            pl.semaphore_wait(barrier, parts + nq - 2)
            send_parts(lambda i: ask_send.at[i], lambda i: ask_recv.at[i], 0, 1)
        post(0, j, at_slots(slot_pick, part(leaving, j)).reshape(parts, depth, width), 1)
    for fetch in fetches[8:]:
        fetch.wait()
    near_in = jnp.where(sub == near_row, 1.0, 0.0).astype(BF16)
    near_out = jnp.where(lane.astype(F32) == as_column(near_row), 1.0, 0.0).astype(BF16)
    near_slots = lax.dot_general(slot_pick, near_in, NT, preferred_element_type=F32).astype(BF16)

    stiff = tile_cases(stiff_ref[...])
    red_t = [exact(binv_ref[t], coup_ref[t], TN) for t in range(kinds)]
    schur = [pblock_ref[t] - exact(red_t[t], coup_ref[t], TN) for t in range(kinds)]

    def corner(a, b):
        rows, cols = slice(a * pd, (a + 1) * pd), slice(b * pd, (b + 1) * pd)
        return table(jnp.concatenate([schur[t][rows, cols] for t in range(kinds)], axis=1))

    nn_tab, nf_tab, fn_tab, ff_tab = corner(0, 0), corner(0, 1), corner(1, 0), corner(1, 1)
    red_tab = table(jnp.concatenate(red_t, axis=1))
    own = jnp.concatenate([pload_ref[:, k, :] for k in range(ncase)], axis=0)
    own = own + pick(jnp.concatenate(condensed_near, axis=0), near_out)
    wait_on(ask_recv.at[rest], part_rsem.at[0])
    asked = ask_recv[...].reshape(parts, 3 * ncomp)
    ports = jnp.concatenate([asked[:, 0:ncomp]] * (ncomp // parts), axis=0).T
    port_lane = lax.broadcasted_iota(jnp.int32, (depth, nport), 1).astype(F32)
    asked_pick = jnp.concatenate(
        [jnp.where(ports[0:depth, i:i + 1] - 1.0 == port_lane, 1.0, 0.0) for i in range(parts)],
        axis=0,
    ).astype(BF16)

    def slot_line(r):
        return jnp.concatenate(
            [asked[i:i + 1, r * ncomp:r * ncomp + depth] for i in range(parts)], axis=1
        )

    slot_masks = kind_masks(slot_line(1))
    slot_stiff = tile_cases(slot_line(2))

    def scatter(e, j, piece):
        post(e, j, at_slots(asked_pick, piece).reshape(parts, depth, width), -1)

        def rest_of_it():
            post(e + 1, j, at_slots(near_slots, piece).reshape(parts, depth, width), 1)

        return rest_of_it

    def join(a, b):
        return b if a is None else jnp.concatenate([a, b], axis=0)

    def near_side(tab, x, a, b):
        return apply_tables(tab, wide(x, pd), masks) * stiff[:, a * ncomp:b * ncomp]

    def far_side(tab, x, a, b):
        return apply_tables(tab, wide(x, pd), slot_masks) * slot_stiff[:, a * slots:b * slots]

    def near_ports(y):
        return pick(tall(y, ncomp), near_out)

    def far_ports(y):
        return place(tall(y, slots), asked_pick)

    def diagonal(e, field):
        y_near = near_side(nn_tab, pick(field, near_in), 0, ncase)
        far_at = [far_send[e, j].reshape(slots, width).T for j in range(chunks)]
        return y_near, far_side(ff_tab, jnp.concatenate(far_at, axis=0), 0, ncase)

    def take_far_values(e, j):
        return place(take(e, j), slot_pick)

    base = None
    for j in range(chunks):
        piece = part(own, j) + place(take(0, j), asked_pick)
        scatter(1, j, piece)()
        publish(0, j, piece)
        base = join(base, piece)

    y_near, y_far = diagonal(1, base)
    far_base, near_at, first, sent, later = None, None, None, 0, []
    for j in range(chunks):
        a, b = cuts[j], cuts[j + 1]
        if j == chunks - 1:
            forward(0)
        piece = take_far_values(1, j)
        publish(3, j, piece)
        far_base = join(far_base, piece)
        near_at = join(near_at, take(2, j))
        rows = slice(a * pd, b * pd)
        y = y_near[:, a * ncomp:b * ncomp] + near_side(nf_tab, far_base[rows], a, b)
        done = near_ports(y)
        y = y_far[:, a * slots:b * slots] + far_side(fn_tab, near_at[rows], a, b)
        done = done + far_ports(y)
        first = join(first, done)
        while (sent + 1) * width <= b * pd:
            later.append(scatter(3, sent, part(first, sent)))
            sent += 1
        publish(1, j, done)

    y_near, y_far = diagonal(3, first)
    straight = near_ports(y_near) + far_ports(y_far)
    collect(0)
    early = against(jnp.concatenate([own_rows(0), own_rows(1)], axis=0), 0)
    gram_out(1, early[ncase:])
    gram_out(0, early[:ncase])
    far_first, crossed = None, None
    for j in range(chunks):
        a, b = cuts[j], cuts[j + 1]
        if j == chunks - 1:
            forward(1)
            forward(3)
            collect(1)
            gram_out(2, against(own_rows(1), 1))
        piece = take_far_values(3, j)
        publish(4, j, piece)
        far_first = join(far_first, piece)
        crossed = join(crossed, near_ports(near_side(nf_tab, far_first[a * pd:b * pd], a, b)))
        if j < chunks - 1:
            later[j]()
    bent_rows[...] = straight + 2.0 * crossed
    bent = jnp.concatenate([lines(bent_rows, d) for d in range(pd)], axis=1)
    gram_out(3, against(bent, 1))
    later[chunks - 1]()

    n = allcase
    eye = jnp.where(
        lax.broadcasted_iota(jnp.int32, (n, n), 0) == lax.broadcasted_iota(jnp.int32, (n, n), 1),
        1.0,
        0.0,
    )
    near_at = None

    def finish_second(j, near_at):
        a, b = cuts[j], cuts[j + 1]
        rows = slice(a * pd, b * pd)
        near_at = join(near_at, take(4, j))
        y = far_side(fn_tab, near_at[rows], a, b)
        publish(2, j, straight[rows] + crossed[rows] + far_ports(y))
        return near_at

    g01, g00 = gram_in(1), gram_in(0)

    def gains(g):
        diagonal = g * eye
        return tuple(lax.rsqrt(jnp.sum(diagonal, axis=k, keepdims=True)) for k in (0, 1))

    both = gauss_solve(g01, jnp.concatenate([g00, eye], axis=1), gains(g01))
    mine = jnp.where(
        lax.broadcasted_iota(jnp.int32, (n, ncase), 0)
        == lax.broadcasted_iota(jnp.int32, (n, ncase), 1) + my_c * ncase,
        1.0,
        0.0,
    )
    chosen = exact(jnp.concatenate([both[:, 0:n], g01], axis=0), mine)
    first_step, g01_mine, inverse = chosen[0:n], chosen[n:2 * n], both[:, n:2 * n]
    for j in range(chunks):
        if j == chunks - 1:
            collect(3)
            g11 = gram_in(2)
            over = exact(inverse, g11)
            side = exact(g11, jnp.concatenate([over, first_step], axis=1))
        near_at = finish_second(j, near_at)
    forward(4)
    g12 = gram_in(3)
    beta = gauss_solve(g12 - sym(side[:, 0:n]), side[:, n:] - g01_mine, gains(g12))
    alpha = first_step + exact(over, beta)
    coefs = jnp.concatenate([alpha, -beta], axis=0).T
    ctop, clow = split(coefs)
    stack = jnp.concatenate([ctop, clow], axis=0)

    def mix(f, low=0, high=2):
        band = slice((f + low) * allcase, (f + high) * allcase)
        cols = slice(low * allcase, high * allcase)
        lead = mm(stack[:, cols], rows_top[band, :])
        return lead[0:ncase] + lead[ncase:] + mm(ctop[:, cols], rows_low[band, :])

    answer_rows = mix(0)
    for d in range(pd):
        sol_ref[d] = answer_rows[:, d * nport:(d + 1) * nport]
    if chunks > 1:
        forward(2, 2)
    collect(4)
    far_rows = mix(3)
    for d in range(pd):
        nat_far[d] = far_rows[:, d * nport:(d + 1) * nport]
    answer = jnp.concatenate([sol_ref[:, k, :] for k in range(ncase)], axis=0)
    near = wide(pick(answer, near_in), pd)
    ends = jnp.concatenate(
        [near, jnp.concatenate([nat_far[:, k, :] for k in range(ncase)], axis=1)], axis=0
    )
    scaled = inv_keep[...] / stiff
    forward(2, lanes_of[2][-1])
    settled = mix(1, 0, 1)
    for d in range(pd):
        res_ref[d] = lines(gath.at[0, my_c], d) - settled[:, d * nport:(d + 1) * nport]
    back = scaled - apply_tables(red_tab, ends, masks)
    for k in range(ncase):
        bub_ref[:, k, :] = back[:, k * ncomp:(k + 1) * ncomp]
    collect(2)
    drop_rows = mix(1, 1, 2)
    for d in range(pd):
        res_ref[d] = res_ref[d] - drop_rows[:, d * nport:(d + 1) * nport]

    wait_on(far_send.at[:, :, rest], send_sem.at[0])
    wait_on(gath.at[:, pl.ds(1, nq - 1)], send_sem.at[1])
    wait_on(gram_recv.at[:, others], send_sem.at[2])
    wait_on(ask_send.at[rest], send_sem.at[3])


def emit(*refs):
    count = len(refs) // 2
    sems = refs[-1]
    copies = [
        pltpu.make_async_copy(refs[i], refs[count + i], sems.at[i]) for i in range(count)
    ]
    for copy in copies:
        copy.start()
    for copy in copies:
        copy.wait()


def local(
    comp_type,
    stiffness,
    near_port,
    far_owner,
    far_port,
    bubble_load,
    port_load,
    bubble_inverse,
    coupling,
    port_block,
):
    npy = lax.axis_size("py")
    parts = lax.axis_size("px") * npy
    nq = lax.axis_size("case")
    ncomp = comp_type.shape[0]
    modes, ncase, _ = bubble_load.shape
    pd, _, nport = port_load.shape
    kinds = bubble_inverse.shape[0]
    cap = 3 * ncomp // (2 * parts)
    depth = -(-cap // 8) * 8
    allcase = nq * ncase
    width = 128 if (ncase * pd) % 128 == 0 else ncase * pd
    chunks = ncase * pd // width
    fold = max(1, 128 // allcase)
    vmem = pl.BlockSpec(memory_space=pltpu.VMEM)
    hbm = pl.BlockSpec(memory_space=pltpu.HBM)

    def body(*refs):
        kernel((parts, npy, nq, depth, width, chunks, fold), *refs)

    shapes = (
        jax.ShapeDtypeStruct(port_load.shape, F32),
        jax.ShapeDtypeStruct(port_load.shape, F32),
        jax.ShapeDtypeStruct(bubble_load.shape, F32),
    )
    results = pl.pallas_call(
        body,
        out_shape=shapes,
        in_specs=[hbm] * 10,
        out_specs=(vmem, vmem, vmem),
        scratch_shapes=[
            pltpu.VMEM((1, ncomp), jnp.int32),
            pltpu.VMEM((1, ncomp), jnp.int32),
            pltpu.VMEM((1, ncomp), jnp.int32),
            pltpu.VMEM((1, ncomp), jnp.int32),
            pltpu.VMEM((1, ncomp), F32),
            pltpu.VMEM(bubble_load.shape, F32),
            pltpu.VMEM(port_load.shape, F32),
            pltpu.VMEM(bubble_inverse.shape, F32),
            pltpu.VMEM((kinds, modes, 2 * pd), F32),
            pltpu.VMEM(port_block.shape, F32),
            pltpu.VMEM((parts, 1, 3 * ncomp), F32),
            pltpu.VMEM((parts, 1, 3 * ncomp), F32),
            pltpu.VMEM((5, chunks, parts, depth, width), F32),
            pltpu.VMEM((5, chunks, parts, depth, width), F32),
            pltpu.VMEM((5, nq, ncase * pd, nport), F32),
            pltpu.VMEM((ncase * pd, nport), F32),
            pltpu.VMEM((5 * allcase, pd * nport), BF16),
            pltpu.VMEM((5 * allcase, pd * nport), BF16),
            pltpu.VMEM((4, ncase // fold, fold * allcase), F32),
            pltpu.VMEM((4, nq * parts, ncase // fold, fold * allcase), F32),
            pltpu.VMEM((modes, ncase * ncomp), F32),
            pltpu.VMEM((pd, ncase, nport), F32),
            pltpu.SemaphoreType.DMA((10,)),
            pltpu.SemaphoreType.DMA((4,)),
            pltpu.SemaphoreType.DMA((1 + 5 * chunks,)),
            pltpu.SemaphoreType.DMA((6, nq - 1)),
            pltpu.SemaphoreType.DMA((4,)),
        ],
        compiler_params=pltpu.CompilerParams(
            collective_id=0, has_side_effects=True, vmem_limit_bytes=32 * 1024 * 1024
        ),
        name="condensed_solve",
    )(
        *(
            pltpu.with_memory_space_constraint(x, pltpu.HBM)
            for x in (
                comp_type.reshape(1, ncomp),
                near_port.reshape(1, ncomp),
                far_owner.reshape(1, ncomp),
                far_port.reshape(1, ncomp),
                stiffness.reshape(1, ncomp),
                bubble_load,
                port_load,
                bubble_inverse,
                jnp.swapaxes(coupling, 1, 2),
                port_block,
            )
        )
    )
    return pl.pallas_call(
        emit,
        out_shape=shapes,
        in_specs=[vmem] * 3,
        out_specs=(hbm, hbm, hbm),
        scratch_shapes=[pltpu.SemaphoreType.DMA((3,))],
        compiler_params=pltpu.CompilerParams(vmem_limit_bytes=4 * 1024 * 1024),
        name="emit",
    )(*results)


def solution(mesh):
    placed = (
        P(("px", "py")),
        P(("px", "py")),
        P(("px", "py")),
        P(("px", "py"), None),
        P(("px", "py")),
        P(None, "case", ("px", "py")),
        P(None, "case", ("px", "py")),
        P(),
        P(),
        P(),
    )
    return jax.shard_map(
        local,
        mesh=mesh,
        in_specs=placed,
        out_specs=(
            P(None, "case", ("px", "py")),
            P(None, "case", ("px", "py")),
            P(None, "case", ("px", "py")),
        ),
        check_vma=False,
    )
```
